32 devices in a mesh: dp: 8 (over z, core), ctx: 4 (over y, x).
Axes of the slice: x: 2, y: 2, z: 4, core: 2. Of those that a mesh axis runs over, the one named last changes fastest.
Arguments:
- tokens: bfloat16 [8, 1024, 1024], P('dp', 'ctx'), may hold values from -6 to 6
- segments: int32 [8, 1024], P('dp'), may hold values from 0 to 3, never falling along the last dimension, each value on 1 to 512 neighbouring positions
- qkv_weight: bfloat16 [1024, 3072], P(('dp', 'ctx')), may hold values from -0.1875 to 0.1875
- qkv_bias: bfloat16 [3072], P(('dp', 'ctx')), may hold values from -3 to 3
- out_weight: bfloat16 [1024, 1024], P(('dp', 'ctx')), may hold values from -0.75 to 0.75
- out_bias: bfloat16 [1024], P(('dp', 'ctx')), may hold values from -3 to 3
- fc1_weight: bfloat16 [1024, 4096], P(('dp', 'ctx')), may hold values from -0.1875 to 0.1875
- fc1_bias: bfloat16 [4096], P(('dp', 'ctx')), may hold values from -3 to 3
- fc2_weight: bfloat16 [4096, 1024], P(('dp', 'ctx')), may hold values from -0.09375 to 0.09375
- fc2_bias: bfloat16 [1024], P(('dp', 'ctx')), may hold values from -3 to 3
- norm_gain: bfloat16 [1024], P(('dp', 'ctx')), may hold values from 0.5 to 1.5
- norm_shift: bfloat16 [1024], P(('dp', 'ctx')), may hold values from -2 to 2
- cotangent: bfloat16 [8, 1024, 1024], P('dp', 'ctx'), may hold values from -6 to 6
Outputs:
- result: bfloat16 [8, 1024, 1024], P('dp', 'ctx')
- grad_tokens: bfloat16 [8, 1024, 1024], P('dp', 'ctx')
- grad_qkv_weight: float32 [1024, 3072], P(('dp', 'ctx'))
- grad_qkv_bias: float32 [3072], P(('dp', 'ctx'))
- grad_out_weight: float32 [1024, 1024], P(('dp', 'ctx'))
- grad_out_bias: float32 [1024], P(('dp', 'ctx'))
- grad_fc1_weight: float32 [1024, 4096], P(('dp', 'ctx'))
- grad_fc1_bias: float32 [4096], P(('dp', 'ctx'))
- grad_fc2_weight: float32 [4096, 1024], P(('dp', 'ctx'))
- grad_fc2_bias: float32 [1024], P(('dp', 'ctx'))
- grad_norm_gain: float32 [1024], P(('dp', 'ctx'))
- grad_norm_shift: float32 [1024], P(('dp', 'ctx'))
The draws below stay inside these ranges and needn't reach their ends.
Inputs may be any that keep to these rules, and one draw needn't show every extreme that they name: `segments`: segment numbers never fall along a sequence; each document has 1 to 512 tokens, and one of each sequence has exactly 512.
All inputs are finite; a program needn't handle non-finite values.
Results may differ from the reference program's by a relative error of at most 0.0093.
Values may be sent and summed in bfloat16 or wider, within the bound.
A program may use at most 192 MiB of HBM per device.

```python
import math
from functools import partial
import jax
import jax.numpy as jnp
import numpy as np
from jax import lax

D = 1024
HEADS = 16
ROT = 32
FF = 4096
LEN = 1024
SEQS = 8


def with_spikes(entries, key, source, target, parts, factor):
    def block_of(dim):
        return (jnp.arange(entries.shape[dim]) // (entries.shape[dim] // parts)).reshape((-1,) + (1,) * (entries.ndim - 1 - dim))

    near = jax.random.permutation(key, parts)[block_of(target)]
    second = (block_of(target) + parts // 2) % parts
    return jnp.where((block_of(source) == near) | (block_of(source) == second), factor * entries, entries)


def steps_of(own_key, dims, shards, least, top_value):
    gain = 1.0
    for axis_at, parts in shards:
        heights = jax.random.uniform(jax.random.fold_in(jax.random.fold_in(own_key, 6), axis_at), (parts,), jnp.float32, least / len(shards), top_value / len(shards))
        gain = gain * jnp.repeat(jnp.exp(heights), dims[axis_at] // parts).reshape((-1,) + (1,) * (len(dims) - 1 - axis_at))
    return gain


def split_up(number_of, total, most, skew):
    weights = [(1 << 20) // math.isqrt(rank ** skew) + 1 for rank in range(2, number_of + 1)]
    spare, given = total - most - (number_of - 1), [1] * (number_of - 1)
    while spare > 0:
        candidates = [i for i in range(number_of - 1) if given[i] < most]
        mass, remaining = sum([weights[i] for i in candidates]), spare
        for i in candidates:
            extra = min(most - given[i], max(1, remaining * weights[i] // mass), spare)
            given[i] = given[i] + extra
            spare = spare - extra
    return np.array([most] + given)


def uneven_parts(stream_key, count, total, limit, skew):
    if count == 2:
        one = jax.random.randint(stream_key, (), max(1, total - limit), min(limit, total - 1) + 1)
        return jnp.stack([one, total - one])
    tallies = jnp.asarray(split_up(count, total, limit, skew), jnp.int32)
    pairs = (count - 1) // 2
    giver, sink = tallies[1:1 + 2 * pairs:2], tallies[2:2 + 2 * pairs:2]
    room = jnp.minimum(giver - 1, limit - sink)
    shifted = jax.random.randint(jax.random.fold_in(stream_key, 1), (pairs,), 0, 1 << 20) % (room + 1)
    tallies = tallies.at[1:1 + 2 * pairs:2].set(giver - shifted).at[2:2 + 2 * pairs:2].set(sink + shifted)
    return tallies[jax.random.permutation(jax.random.fold_in(stream_key, 2), count)]


def gaussian(rng, shape, spread, limit, pieces=(), kind=jnp.bfloat16):
    values = jax.random.normal(rng, shape, jnp.float32) * spread
    if len(pieces) > 0:
        values = steps_of(rng, shape, pieces, -0.22, 0.18) * values
    return jnp.clip(values, min=-limit, max=limit).astype(kind)


def gaussian_with(own_key, dims, deviation, reach, cuts, heavy, kind=jnp.bfloat16):
    values = deviation * jax.random.normal(own_key, dims, jnp.float32)
    if cuts:
        values = values * steps_of(own_key, dims, cuts, -0.22, 0.18)
    return jnp.clip(with_spikes(values, jax.random.fold_in(own_key, 3), *heavy), -reach, reach).astype(kind)


def setup_inputs(seed: int = 0) -> dict:
    splits = jax.random.split(jax.random.key(seed), 14)
    tokens = gaussian(splits[0], (SEQS, LEN, D), 1.0, 6.0, ((0, 8), (1, 4)))
    segments = jax.vmap(lambda own: jnp.searchsorted(jnp.cumsum(uneven_parts(own, 4, LEN, LEN // 2, 0)), jnp.arange(LEN), side="right"))(jax.random.split(splits[1], SEQS)).reshape((SEQS, LEN)).astype(jnp.int32)
    qkv_weight = gaussian(splits[2], (D, 3 * D), D ** -0.5, 0.1875, ((0, 32),))
    qkv_bias = gaussian(splits[3], (3 * D,), 0.5, 3.0, ((0, 32),))
    out_weight = gaussian(splits[4], (D, D), (D // 16) ** -0.5, 0.75, ((0, 32),))
    out_bias = gaussian(splits[5], (D,), 0.5, 3.0, ((0, 32),))
    fc1_weight = gaussian(splits[6], (D, FF), D ** -0.5, 0.1875, ((0, 32),))
    fc1_bias = gaussian(splits[7], (FF,), 0.5, 3.0, ((0, 32),))
    fc2_weight = gaussian(splits[8], (FF, D), FF ** -0.5, 0.09375, ((0, 32),))
    fc2_bias = gaussian(splits[9], (D,), 0.5, 3.0, ((0, 32),))
    norm_gain = jnp.clip(1.0 + 0.1 * jax.random.normal(splits[10], (D,), jnp.float32), 0.5, 1.5).astype(jnp.bfloat16)
    norm_shift = gaussian(splits[11], (D,), 0.3, 2.0, ((0, 32),))
    cotangent = gaussian_with(splits[12], (SEQS, LEN, D), 1.0, 6.0, ((0, 8), (1, 4)), (0, 2, 8, 2.0))
    return dict(tokens=tokens, segments=segments, qkv_weight=qkv_weight, qkv_bias=qkv_bias, out_weight=out_weight, out_bias=out_bias, fc1_weight=fc1_weight, fc1_bias=fc1_bias, fc2_weight=fc2_weight, fc2_bias=fc2_bias, norm_gain=norm_gain, norm_shift=norm_shift, cotangent=cotangent)


epsilon = 1e-05

@jax.custom_vjp
def low(v):
    return lax.optimization_barrier(v.astype(jnp.bfloat16)).astype(jnp.float32)

@jax.custom_vjp
def low_back(v):
    return v

def low_keep(v):
    return (low(v), None)

def low_pass(kept, grad):
    return (grad,)

def back_keep(v):
    return (v, None)

def back_low(kept, grad):
    return (low(grad),)
low.defvjp(low_keep, low_pass)
low_back.defvjp(back_keep, back_low)

def matmul(left, right):
    return jnp.dot(left, right, precision=lax.Precision.HIGHEST, preferred_element_type=jnp.float32)

def angles(positions, rotary):
    freq_table = 1.0 / 10000.0 ** (jnp.arange(0, rotary, 2, dtype=jnp.float32) / rotary)
    theta = positions.astype(jnp.float32)[:, None] * freq_table[None, :]
    return (jnp.cos(theta)[:, None, :], jnp.sin(theta)[:, None, :])

def rotate(tensor, cosine, sine_table, rotary):
    half_len = rotary // 2
    first_half = tensor[..., :half_len]
    second_half = tensor[..., half_len:rotary]
    return jnp.concatenate([first_half * cosine - second_half * sine_table, second_half * cosine + first_half * sine_table, tensor[..., rotary:]], axis=-1)

def forward(tokens, qkv_weight, qkv_bias, out_weight, out_bias, fc1_weight, fc1_bias, fc2_weight, fc2_bias, norm_gain, norm_shift, segments):
    seq_count, length, model_width = tokens.shape
    head_dim = model_width // HEADS
    inputs = tokens.reshape(-1, model_width)
    center = inputs - lax.optimization_barrier(jnp.mean(inputs, axis=-1, keepdims=True))
    scaled = center * lax.rsqrt(lax.optimization_barrier(jnp.mean(center * center, axis=-1, keepdims=True)) + epsilon)
    normed = low(scaled * norm_gain + norm_shift)
    mixed = low_back(matmul(normed, qkv_weight) + qkv_bias)
    split_shape = (seq_count, length, HEADS, head_dim)
    positions = jnp.arange(length, dtype=jnp.int32)
    cosine, sine_table = angles(positions, ROT)
    queries = low(rotate(mixed[:, :model_width].reshape(split_shape), cosine, sine_table, ROT))
    keys_all = low(rotate(mixed[:, model_width:2 * model_width].reshape(split_shape), cosine, sine_table, ROT))
    values_all = low(mixed[:, 2 * model_width:].reshape(split_shape))
    score_scale = float(head_dim) ** (-0.5)

    def one_sequence(packed):
        seq_queries, seq_keys, seq_values, seg_ids = packed
        scores = low_back(jnp.einsum('qhd,khd->hqk', seq_queries, seq_keys, precision=lax.Precision.HIGHEST) * score_scale)
        allowed = (seg_ids[:, None] == seg_ids[None, :]) & (positions[None, :] <= positions[:, None])
        scores = jnp.where(allowed[None], scores, -1e+30)
        row_max = lax.optimization_barrier(jnp.max(scores, axis=-1, keepdims=True))
        log_total = row_max + jnp.log(lax.optimization_barrier(jnp.sum(jnp.exp(scores - row_max), axis=-1, keepdims=True)))
        weights = low(jnp.exp(scores - log_total))
        return jnp.einsum('hqk,khd->qhd', weights, seq_values, precision=lax.Precision.HIGHEST)
    attended = lax.map(jax.checkpoint(one_sequence), (queries, keys_all, values_all, segments))
    attended = low(low_back(attended.reshape(-1, model_width)))
    attn_part = matmul(attended, out_weight) + out_bias
    hidden = low_back(matmul(normed, fc1_weight) + fc1_bias)
    act = low(jax.nn.gelu(hidden, approximate=True))
    mlp_part = matmul(act, fc2_weight) + fc2_bias
    return (inputs + attn_part + mlp_part).reshape(tokens.shape)

def reference(tokens, segments, qkv_weight, qkv_bias, out_weight, out_bias, fc1_weight, fc1_bias, fc2_weight, fc2_bias, norm_gain, norm_shift, cotangent):
    floats = [tokens.astype(jnp.float32), qkv_weight.astype(jnp.float32), qkv_bias.astype(jnp.float32), out_weight.astype(jnp.float32), out_bias.astype(jnp.float32), fc1_weight.astype(jnp.float32), fc1_bias.astype(jnp.float32), fc2_weight.astype(jnp.float32), fc2_bias.astype(jnp.float32), norm_gain.astype(jnp.float32), norm_shift.astype(jnp.float32)]
    result, pullback = jax.vjp(partial(forward, segments=segments), *floats)
    gradients = pullback(cotangent.astype(jnp.float32))
    return (result.astype(jnp.bfloat16), gradients[0].astype(jnp.bfloat16), gradients[1], gradients[2], gradients[3], gradients[4], gradients[5], gradients[6], gradients[7], gradients[8], gradients[9], gradients[10])
```

```python
import jax
import jax.numpy as jnp
from jax import lax
from jax.sharding import PartitionSpec as P

HEADS = 16
ROT = 32
epsilon = 1e-05
BOTH = ("dp", "ctx")


def angles(positions, rotary):
    freq_table = 1.0 / 10000.0 ** (jnp.arange(0, rotary, 2, dtype=jnp.float32) / rotary)
    theta = positions.astype(jnp.float32)[:, None] * freq_table[None, :]
    return (jnp.cos(theta)[:, None, :], jnp.sin(theta)[:, None, :])


def rotate(tensor, cosine, sine_table, rotary):
    half_len = rotary // 2
    first_half = tensor[..., :half_len]
    second_half = tensor[..., half_len:rotary]
    return jnp.concatenate(
        [
            first_half * cosine - second_half * sine_table,
            second_half * cosine + first_half * sine_table,
            tensor[..., rotary:],
        ],
        axis=-1,
    )


def contract_rows(left, right):
    return lax.dot_general(
        left, right, (((0,), (0,)), ((), ())), preferred_element_type=jnp.float32
    )


def times_transposed(left, right):
    return lax.dot_general(
        left, right, (((1,), (1,)), ((), ())), preferred_element_type=jnp.float32
    )


def times(left, right):
    return jnp.dot(left, right, preferred_element_type=jnp.float32)


def gelu_tanh(hidden_in):
    return jax.nn.gelu(hidden_in, approximate=True)


def normalise(inputs):
    center = inputs - jnp.mean(inputs, axis=-1, keepdims=True)
    inverse = lax.rsqrt(jnp.mean(center * center, axis=-1, keepdims=True) + epsilon)
    return center * inverse, inverse


def attention(q, k, v, segments, back, cosine, sine):
    length, head_dim = q.shape[1], q.shape[3]
    scale = float(head_dim) ** (-0.5)
    index = jnp.arange(length, dtype=jnp.int32)
    allowed = (segments[:, :, None] == segments[:, None, :]) & (index[None, :] <= index[:, None])[
        None
    ]
    scores = jnp.einsum("sqhd,skhd->shqk", q, k, preferred_element_type=jnp.float32) * scale
    scores = jnp.where(allowed[:, None], scores, -1e30)
    row_max = jnp.max(scores, axis=-1, keepdims=True)
    log_total = row_max + jnp.log(jnp.sum(jnp.exp(scores - row_max), axis=-1, keepdims=True))
    probs = jnp.exp(scores - log_total)
    probs_low = probs.astype(jnp.bfloat16)
    attended = jnp.einsum("shqk,skhd->sqhd", probs_low, v, preferred_element_type=jnp.float32)

    def backward(grad_attended):
        grad_weights = jnp.einsum(
            "sqhd,skhd->shqk", grad_attended, v, preferred_element_type=jnp.float32
        )
        row_dot = jnp.sum(grad_weights * probs, axis=-1, keepdims=True)
        grad_scores = (probs * (grad_weights - row_dot)).astype(jnp.bfloat16)
        grad_q = (
            jnp.einsum("shqk,skhd->sqhd", grad_scores, k, preferred_element_type=jnp.float32)
            * scale
        )
        grad_k = (
            jnp.einsum("shqk,sqhd->skhd", grad_scores, q, preferred_element_type=jnp.float32)
            * scale
        )
        grad_v = jnp.einsum(
            "shqk,sqhd->skhd", probs_low, grad_attended, preferred_element_type=jnp.float32
        )
        return grad_q, grad_k, grad_v

    return attended, backward


def local(
    dp,
    ctx,
    tokens,
    segments,
    qkv_weight,
    qkv_bias,
    out_weight,
    out_bias,
    fc1_weight,
    fc1_bias,
    fc2_weight,
    fc2_bias,
    norm_gain,
    norm_shift,
    cotangent,
):
    f32, b16 = jnp.float32, jnp.bfloat16
    seqs, part, width = tokens.shape
    length = part * ctx
    rows = seqs * length
    ff = fc1_weight.shape[1]
    fl, dl = ff // ctx, width // ctx
    heads = HEADS // ctx
    head_dim = width // HEADS
    wr, fr = qkv_weight.shape[0], fc2_weight.shape[0]
    mine = lax.axis_index("ctx")
    devices = dp * ctx

    pieces = [qkv_bias, fc1_bias, out_bias, fc2_bias, norm_gain, norm_shift]
    marks = [0]
    for piece in pieces:
        marks.append(marks[-1] + piece.shape[0])
    small = lax.all_gather(jnp.concatenate(pieces), BOTH, axis=0)
    parts = [small[:, a:b] for a, b in zip(marks, marks[1:])]
    b_qkv = lax.dynamic_index_in_dim(
        parts[0].reshape(3, ctx, dl), mine, 1, keepdims=False
    ).reshape(3 * dl)
    b_fc1 = lax.dynamic_index_in_dim(
        parts[1].reshape(dp, ctx, fr), mine, 1, keepdims=False
    ).reshape(fl)
    b_out, b_fc2, gain, shift = [p.reshape(width).astype(f32) for p in parts[2:]]

    send_qkv = jnp.moveaxis(qkv_weight.reshape(wr, 3, ctx, dl), 2, 0).reshape(ctx, wr, 3 * dl)
    send_fc1 = jnp.moveaxis(fc1_weight.reshape(wr, dp, ctx, fr), 2, 0).reshape(ctx, wr, fl)
    sent = lax.all_to_all(
        jnp.concatenate([send_qkv, send_fc1], axis=2), "ctx", split_axis=0, concat_axis=0
    )
    out_perm = [(b, (b % dp) * ctx + b // dp) for b in range(devices)]
    out_back = [(j, i) for i, j in out_perm]
    out_piece = lax.ppermute(out_weight, BOTH, out_perm)
    w_qkv = lax.all_gather(sent[:, :, : 3 * dl], "dp", axis=0).reshape(width, 3 * dl)
    w_fc1 = lax.all_gather(sent[:, :, 3 * dl :], "dp", axis=0).reshape(width, fl)
    w_fc2 = lax.all_gather(fc2_weight, "dp", axis=0).reshape(fl, width)
    w_out = lax.all_gather(out_piece, "dp", axis=0).reshape(dl, width)

    tokens_all = lax.all_gather(tokens, "ctx", axis=1, tiled=True)
    cot_all = lax.all_gather(cotangent, "ctx", axis=1, tiled=True)

    positions = jnp.arange(length, dtype=jnp.int32)
    cosine, sine = angles(positions, ROT)

    scaled_all, _ = normalise(tokens_all.astype(f32).reshape(rows, width))
    normed = (scaled_all * gain + shift).astype(b16)
    grad_out = cot_all.reshape(rows, width)

    mixed = times(normed, w_qkv) + b_qkv.astype(f32)
    shape4 = (seqs, length, heads, head_dim)
    q = rotate(mixed[:, :dl].reshape(shape4), cosine, sine, ROT).astype(b16)
    k = rotate(mixed[:, dl : 2 * dl].reshape(shape4), cosine, sine, ROT).astype(b16)
    v = mixed[:, 2 * dl :].astype(b16).reshape(shape4)
    attended, attention_back = attention(q, k, v, segments, None, cosine, sine)
    attended = attended.reshape(rows, dl).astype(b16)

    hidden = times(normed, w_fc1) + b_fc1.astype(f32)
    act, gelu_back = jax.vjp(gelu_tanh, hidden)
    act = act.astype(b16)
    partial = times(attended, w_out) + times(act, w_fc2)
    summed = lax.psum_scatter(
        partial.astype(b16).reshape(seqs, length, width), "ctx", scatter_dimension=1, tiled=True
    )
    result = (tokens.astype(f32) + summed.astype(f32) + (b_out + b_fc2)).astype(b16)

    grad_act = times_transposed(grad_out, w_fc2)
    grad_hidden = gelu_back(grad_act)[0].astype(b16)
    grad_fc2 = contract_rows(act, grad_out)
    grad_fc2 = lax.psum_scatter(grad_fc2.astype(b16), "dp", scatter_dimension=0, tiled=True)
    grad_fc1 = contract_rows(normed, grad_hidden)
    grad_fc1_b = jnp.sum(grad_hidden, axis=0, dtype=f32)
    grad_fc1 = lax.psum_scatter(grad_fc1.astype(b16), "dp", scatter_dimension=0, tiled=True)
    grad_out_w = contract_rows(attended, grad_out)
    grad_out_w = lax.psum_scatter(grad_out_w.astype(b16), "dp", scatter_dimension=0, tiled=True)
    grad_attended = times_transposed(grad_out, w_out).astype(b16).reshape(shape4)
    grad_q, grad_k, grad_v = attention_back(grad_attended)
    grad_mixed = jnp.concatenate(
        [
            rotate(grad_q, cosine, -sine, ROT).reshape(rows, dl),
            rotate(grad_k, cosine, -sine, ROT).reshape(rows, dl),
            grad_v.reshape(rows, dl),
        ],
        axis=1,
    ).astype(b16)
    grad_normed = times_transposed(grad_hidden, w_fc1) + times_transposed(grad_mixed, w_qkv)
    grad_normed = lax.psum_scatter(
        grad_normed.astype(b16).reshape(seqs, length, width), "ctx", scatter_dimension=1, tiled=True
    ).astype(f32)
    grad_qkv = contract_rows(normed, grad_mixed)
    grad_qkv_b = jnp.sum(grad_mixed, axis=0, dtype=f32)
    grad_qkv = lax.psum_scatter(grad_qkv.astype(b16), "dp", scatter_dimension=0, tiled=True)

    back = lax.all_to_all(
        jnp.concatenate([grad_qkv, grad_fc1], axis=1).reshape(ctx, wr, 3 * dl + fl),
        "ctx",
        split_axis=0,
        concat_axis=0,
    ).astype(f32)
    grad_qkv = jnp.moveaxis(back[:, :, : 3 * dl].reshape(ctx, wr, 3, dl), 0, 2).reshape(
        wr, 3 * width
    )
    grad_fc1 = jnp.moveaxis(back[:, :, 3 * dl :].reshape(ctx, wr, dp, fr), 0, 2).reshape(wr, ff)
    grad_out_w = lax.ppermute(grad_out_w, BOTH, out_back).astype(f32)
    grad_fc2 = grad_fc2.astype(f32)

    grad_normed = grad_normed.reshape(seqs, part, width)
    own = tokens.astype(f32)
    cot = cotangent.astype(f32)
    scaled, inverse = normalise(own)
    grad_gain = jnp.sum(grad_normed * scaled, axis=(0, 1))
    grad_shift = jnp.sum(grad_normed, axis=(0, 1))
    grad_scaled = grad_normed * gain
    grad_input = inverse * (
        grad_scaled
        - jnp.mean(grad_scaled, axis=-1, keepdims=True)
        - scaled * jnp.mean(grad_scaled * scaled, axis=-1, keepdims=True)
    )
    grad_tokens = (cot + grad_input).astype(b16)

    wide_qkv_b = lax.dynamic_update_index_in_dim(
        jnp.zeros((3, ctx, dl), f32), grad_qkv_b.reshape(3, dl), mine, 1
    )
    wide_fc1_b = lax.dynamic_update_index_in_dim(
        jnp.zeros((dp, ctx, fr), f32), grad_fc1_b.reshape(dp, fr), mine, 1
    )
    bias_out = jnp.sum(cot, axis=(0, 1))
    sums = jnp.concatenate(
        [
            x.reshape(devices, -1)
            for x in (wide_qkv_b, wide_fc1_b, bias_out, grad_gain, grad_shift)
        ],
        axis=1,
    )
    sums = lax.psum_scatter(sums, BOTH, scatter_dimension=0, tiled=True)[0]
    at = [0, marks[1], marks[2], marks[3], marks[3] + wr, marks[3] + 2 * wr]
    g_qkv_b, g_fc1_b, g_bias, g_gain, g_shift = [sums[a:b] for a, b in zip(at, at[1:])]
    return (
        result,
        grad_tokens,
        grad_qkv,
        g_qkv_b,
        grad_out_w,
        g_bias,
        grad_fc1,
        g_fc1_b,
        grad_fc2,
        g_bias,
        g_gain,
        g_shift,
    )


def solution(mesh):
    sizes = (mesh.shape["dp"], mesh.shape["ctx"])
    seq, mat, vec = P("dp", "ctx", None), P(BOTH, None), P(BOTH)
    placed = (seq, P("dp", None), mat, vec, mat, vec, mat, vec, mat, vec, vec, vec, seq)
    return jax.shard_map(
        lambda *args: local(*sizes, *args),
        mesh=mesh,
        in_specs=placed,
        out_specs=(seq, seq, mat, vec, mat, vec, mat, vec, mat, vec, vec, vec),
        check_vma=False,
    )
```

```python
import functools

import jax
import jax.numpy as jnp
from jax import lax
from jax.experimental import pallas as pl
from jax.experimental.pallas import tpu as pltpu
from jax.sharding import PartitionSpec as P

HEADS = 16
ROT = 32
epsilon = 1e-05
BOTH = ("dp", "ctx")
MESH = pl.DeviceIdType.MESH


def angles(positions, rotary):
    freq_table = 1.0 / 10000.0 ** (jnp.arange(0, rotary, 2, dtype=jnp.float32) / rotary)
    theta = positions.astype(jnp.float32)[:, None] * freq_table[None, :]
    return (jnp.cos(theta)[:, None, :], jnp.sin(theta)[:, None, :])


def rotate(tensor, cosine, sine_table, rotary):
    half_len = rotary // 2
    first_half = tensor[..., :half_len]
    second_half = tensor[..., half_len:rotary]
    return jnp.concatenate(
        [
            first_half * cosine - second_half * sine_table,
            second_half * cosine + first_half * sine_table,
            tensor[..., rotary:],
        ],
        axis=-1,
    )


def contract_rows(left, right):
    return lax.dot_general(
        left, right, (((0,), (0,)), ((), ())), preferred_element_type=jnp.float32
    )


def times_transposed(left, right):
    return lax.dot_general(
        left, right, (((1,), (1,)), ((), ())), preferred_element_type=jnp.float32
    )


def times(left, right):
    return jnp.dot(left, right, preferred_element_type=jnp.float32)


def gelu_tanh(hidden_in):
    return jax.nn.gelu(hidden_in, approximate=True)


def normalise(inputs):
    center = inputs - jnp.mean(inputs, axis=-1, keepdims=True)
    inverse = lax.rsqrt(jnp.mean(center * center, axis=-1, keepdims=True) + epsilon)
    return center * inverse, inverse


def attention(q, k, v, segments, back, cosine, sine):
    length, head_dim = q.shape[1], q.shape[3]
    scale = float(head_dim) ** (-0.5)
    index = jnp.arange(length, dtype=jnp.int32)
    allowed = (segments[:, :, None] == segments[:, None, :]) & (index[None, :] <= index[:, None])[
        None
    ]
    scores = jnp.einsum("sqhd,skhd->shqk", q, k, preferred_element_type=jnp.float32) * scale
    scores = jnp.where(allowed[:, None], scores, -1e30)
    row_max = jnp.max(scores, axis=-1, keepdims=True)
    log_total = row_max + jnp.log(jnp.sum(jnp.exp(scores - row_max), axis=-1, keepdims=True))
    probs = jnp.exp(scores - log_total)
    probs_low = probs.astype(jnp.bfloat16)
    attended = jnp.einsum("shqk,skhd->sqhd", probs_low, v, preferred_element_type=jnp.float32)

    def backward(grad_attended):
        grad_weights = jnp.einsum(
            "sqhd,skhd->shqk", grad_attended, v, preferred_element_type=jnp.float32
        )
        row_dot = jnp.sum(grad_weights * probs, axis=-1, keepdims=True)
        grad_scores = (probs * (grad_weights - row_dot)).astype(jnp.bfloat16)
        grad_q = (
            jnp.einsum("shqk,skhd->sqhd", grad_scores, k, preferred_element_type=jnp.float32)
            * scale
        )
        grad_k = (
            jnp.einsum("shqk,sqhd->skhd", grad_scores, q, preferred_element_type=jnp.float32)
            * scale
        )
        grad_v = jnp.einsum(
            "shqk,sqhd->skhd", probs_low, grad_attended, preferred_element_type=jnp.float32
        )
        return grad_q, grad_k, grad_v

    return attended, backward


def gather_kernel(
    nz, nc,
    tok_ref, cot_ref, qkv_ref, fc1_ref, fc2_ref, out_ref, small_ref,
    tok_all, cot_all, w_qkv, w_fc1, w_fc2, w_out, small_all,
    ctx_send, ctx_recv, z_send, z_recv, sib_send, sib_recv, loc,
):
    d, c = lax.axis_index("dp"), lax.axis_index("ctx")
    z, k = d // 2, lax.rem(d, 2)
    other = 2 * z + 1 - k
    wr, width = out_ref.shape
    dl = width // nc
    fr = fc2_ref.shape[0]
    nd = 2 * nz

    def ctx_to(j):
        return lax.rem(c + j, nc)

    def ctx_from(j):
        return lax.rem(c + nc - j, nc)

    def z_to(j):
        return 2 * lax.rem(z + j, nz) + k

    def z_from(j):
        return 2 * lax.rem(z + nz - j, nz) + k

    barrier = pltpu.get_barrier_semaphore()
    for j in range(1, nc):
        pl.semaphore_signal(barrier, inc=1, device_id=(d, ctx_to(j)), device_id_type=MESH)
    for j in range(1, nz):
        pl.semaphore_signal(barrier, inc=1, device_id=(z_to(j), c), device_id_type=MESH)
    pl.semaphore_signal(barrier, inc=1, device_id=(other, c), device_id_type=MESH)
    pl.semaphore_wait(barrier, nc + nz - 1)

    def remote(src, dst, send, recv, device):
        return pltpu.make_async_remote_copy(
            src_ref=src, dst_ref=dst, send_sem=send, recv_sem=recv,
            device_id=device, device_id_type=MESH,
        )

    def rows(at):
        return pl.ds(pl.multiple_of(at * wr, wr), wr)

    def lanes(at, size):
        return pl.ds(pl.multiple_of(at * size, size), size)

    SMALL, QKV, FC1, TOK, COT, OUT, FC2 = range(7)

    def qkv_pieces(to, owner, sub):
        return [
            (qkv_ref.at[:, lanes(t * nc + to, dl)], w_qkv.at[owner, rows(sub), pl.ds(t * dl, dl)])
            for t in range(3)
        ]

    def fc1_pieces(to, owner, sub):
        return [
            (fc1_ref.at[:, lanes(g * nc + to, fr)], w_fc1.at[owner, rows(sub), pl.ds(g * fr, fr)])
            for g in range(nd)
        ]

    def ctx_pieces(array, to):
        if array == SMALL:
            return [(small_ref, small_all.at[d, c])]
        if array == QKV:
            return qkv_pieces(to, d, c)
        if array == FC1:
            return fc1_pieces(to, d, c)
        if array == TOK:
            return [(tok_ref, tok_all.at[c])]
        return [(cot_ref, cot_all.at[c])]

    def ctx_whole(array, sub):
        return {
            SMALL: lambda: small_all.at[d, sub],
            QKV: lambda: w_qkv.at[d, rows(sub), :],
            FC1: lambda: w_fc1.at[d, rows(sub), :],
            TOK: lambda: tok_all.at[sub],
            COT: lambda: cot_all.at[sub],
        }[array]()

    def ctx_start(array):
        for j in range(1, nc):
            for src, dst in ctx_pieces(array, ctx_to(j)):
                remote(src, dst, ctx_send.at[array, j], ctx_recv.at[array, j], (d, ctx_to(j))).start()
        for src, dst in ctx_pieces(array, c):
            pltpu.make_async_copy(src, dst, loc.at[array]).start()

    def ctx_finish(array):
        for j in range(1, nc):
            got = ctx_whole(array, ctx_from(j))
            remote(got, got, ctx_send.at[array, j], ctx_recv.at[array, j], (d, ctx_to(j))).wait()
        mine = ctx_whole(array, c)
        pltpu.make_async_copy(mine, mine, loc.at[array]).wait()

    blocks = {SMALL: small_all, QKV: w_qkv, FC1: w_fc1, FC2: w_fc2}

    def z_copy(array, j, own):
        block = blocks[array].at[own]
        src = fc2_ref if array == FC2 else block
        return remote(src, block, z_send.at[array, j], z_recv.at[array, j], (z_to(j), c))

    def sib_copy(array, j, at):
        block = blocks[array].at[at]
        src = fc2_ref if array == FC2 and j == 0 else block
        return remote(src, block, sib_send.at[array, j], sib_recv.at[array, j], (other, c))

    def z_start(array):
        for j in range(1, nz):
            z_copy(array, j, d).start()
        sib_copy(array, 0, d).start()

    def z_pass_on(array):
        for j in range(1, nz):
            z_copy(array, j, z_from(j)).wait_recv()
            sib_copy(array, j, z_from(j)).start()

    def z_finish(array):
        for j in range(1, nz):
            z_copy(array, j, d).wait_send()
        for j in range(nz):
            sib_copy(array, j, d if j == 0 else z_from(j)).wait_send()
            sib_copy(array, j, lax.rem(z + nz - j, nz) * 2 + 1 - k).wait_recv()

    def out_copy(j, to, sub):
        return remote(out_ref, w_out.at[k, rows(sub), :], ctx_send.at[OUT, j], ctx_recv.at[OUT, j], (d, to))

    half = w_out.at[k]

    def out_z(j, to):
        return remote(half, half, z_send.at[OUT, j], z_recv.at[OUT, j], (to, c))

    ctx_start(SMALL)
    ctx_start(QKV)
    ctx_start(TOK)
    ctx_start(FC1)
    own_fc2 = pltpu.make_async_copy(fc2_ref, w_fc2.at[d], loc.at[FC2])
    own_fc2.start()
    own_out = pltpu.make_async_copy(out_ref, w_out.at[k, rows(c), :], loc.at[OUT])

    @pl.when(z == c)
    def _():
        own_out.start()

    for j in range(1, nc):
        @pl.when(ctx_to(j) == z)
        def _():
            out_copy(j, z, c).start()

    ctx_finish(SMALL)
    z_start(SMALL)
    ctx_finish(QKV)
    z_start(QKV)
    ctx_start(COT)
    ctx_finish(FC1)
    z_start(FC1)
    z_start(FC2)

    @pl.when(z == c)
    def _():
        for j in range(1, nc):
            out_copy(j, z, ctx_from(j)).wait_recv()
        own_out.wait()
        for j in range(1, nz):
            out_z(j, z_to(j)).start()

    for j in range(1, nc):
        @pl.when(ctx_to(j) == z)
        def _():
            out_copy(j, z, c).wait_send()

    z_pass_on(SMALL)
    z_finish(SMALL)
    z_pass_on(QKV)
    z_finish(QKV)
    ctx_finish(TOK)
    z_pass_on(FC1)
    z_finish(FC1)
    ctx_finish(COT)
    own_fc2.wait()
    z_pass_on(FC2)
    z_finish(FC2)

    for j in range(1, nz):
        @pl.when(lax.rem(z + nz - j, nz) == c)
        def _():
            out_z(j, z_to(j)).wait_recv()

    @pl.when(z == c)
    def _():
        for j in range(1, nz):
            out_z(j, z_to(j)).wait_send()

    give = remote(half, half, sib_send.at[OUT, 0], sib_recv.at[OUT, 0], (other, c))
    give.start()
    give.wait()


def gather_all(nz, nc, tokens, cotangent, qkv_weight, fc1_weight, fc2_weight, out_weight, small):
    part, width = tokens.shape
    wr, fr = qkv_weight.shape[0], fc2_weight.shape[0]
    nd, dl = 2 * nz, width // nc
    b16 = jnp.bfloat16
    shapes = [
        ((nc, part, width), b16),
        ((nc, part, width), b16),
        ((nd, nc * wr, 3 * dl), b16),
        ((nd, nc * wr, nd * fr), b16),
        ((nd, fr, width), b16),
        ((2, nc * wr, width), b16),
        ((nd, nc) + small.shape, jnp.float32),
    ]
    return pl.pallas_call(
        functools.partial(gather_kernel, nz, nc),
        out_shape=[jax.ShapeDtypeStruct(s, t) for s, t in shapes],
        in_specs=[pl.BlockSpec(memory_space=pl.ANY)] * 7,
        out_specs=[pl.BlockSpec(memory_space=pl.ANY)] * 7,
        scratch_shapes=[
            pltpu.SemaphoreType.DMA((7, nc)),
            pltpu.SemaphoreType.DMA((7, nc)),
            pltpu.SemaphoreType.DMA((7, nz)),
            pltpu.SemaphoreType.DMA((7, nz)),
            pltpu.SemaphoreType.DMA((7, nz)),
            pltpu.SemaphoreType.DMA((7, nz)),
            pltpu.SemaphoreType.DMA((7,)),
        ],
        compiler_params=pltpu.CompilerParams(collective_id=0, has_side_effects=True),
        name="gather",
    )(tokens, cotangent, qkv_weight, fc1_weight, fc2_weight, out_weight, small)


def local(
    dp,
    ctx,
    tokens,
    segments,
    qkv_weight,
    qkv_bias,
    out_weight,
    out_bias,
    fc1_weight,
    fc1_bias,
    fc2_weight,
    fc2_bias,
    norm_gain,
    norm_shift,
    cotangent,
):
    f32, b16 = jnp.float32, jnp.bfloat16
    seqs, part, width = tokens.shape
    length = part * ctx
    rows = seqs * length
    ff = fc1_weight.shape[1]
    fl, dl = ff // ctx, width // ctx
    heads = HEADS // ctx
    head_dim = width // HEADS
    wr, fr = qkv_weight.shape[0], fc2_weight.shape[0]
    mine = lax.axis_index("ctx")
    devices = dp * ctx

    pieces = [qkv_bias, fc1_bias, out_bias, fc2_bias, norm_gain, norm_shift]
    marks = [0]
    for piece in pieces:
        marks.append(marks[-1] + piece.shape[0])
    direct = wr % 16 == 0 and dp == 2 * ctx and seqs == 1
    if direct:
        vector = jnp.concatenate(pieces).astype(f32)
        vector = jnp.pad(vector, (0, -marks[-1] % 128))[None]
        tokens_all, cot_all, w_qkv, w_fc1, w_fc2, w_out, small = gather_all(
            dp // 2,
            ctx,
            tokens[0],
            cotangent[0],
            qkv_weight,
            fc1_weight,
            fc2_weight,
            out_weight,
            vector,
        )
        tokens_all = tokens_all.reshape(seqs, length, width)
        cot_all = cot_all.reshape(seqs, length, width)
        w_qkv, w_fc1 = w_qkv.reshape(width, 3 * dl), w_fc1.reshape(width, fl)
        w_fc2, w_out = w_fc2.reshape(fl, width), w_out.reshape(dl, width)
        small = small.reshape(devices, -1)
    else:
        small = lax.all_gather(jnp.concatenate(pieces), BOTH, axis=0)
    parts = [small[:, a:b] for a, b in zip(marks, marks[1:])]
    b_qkv = lax.dynamic_index_in_dim(
        parts[0].reshape(3, ctx, dl), mine, 1, keepdims=False
    ).reshape(3 * dl)
    b_fc1 = lax.dynamic_index_in_dim(
        parts[1].reshape(dp, ctx, fr), mine, 1, keepdims=False
    ).reshape(fl)
    b_out, b_fc2, gain, shift = [p.reshape(width).astype(f32) for p in parts[2:]]

    out_perm = [(b, (b % dp) * ctx + b // dp) for b in range(devices)]
    out_back = [(j, i) for i, j in out_perm]
    if not direct:
        send_qkv = jnp.moveaxis(qkv_weight.reshape(wr, 3, ctx, dl), 2, 0).reshape(ctx, wr, 3 * dl)
        send_fc1 = jnp.moveaxis(fc1_weight.reshape(wr, dp, ctx, fr), 2, 0).reshape(ctx, wr, fl)
        sent = lax.all_to_all(
            jnp.concatenate([send_qkv, send_fc1], axis=2), "ctx", split_axis=0, concat_axis=0
        )
        out_piece = lax.ppermute(out_weight, BOTH, out_perm)
        w_qkv = lax.all_gather(sent[:, :, : 3 * dl], "dp", axis=0).reshape(width, 3 * dl)
        w_fc1 = lax.all_gather(sent[:, :, 3 * dl :], "dp", axis=0).reshape(width, fl)
        w_fc2 = lax.all_gather(fc2_weight, "dp", axis=0).reshape(fl, width)
        w_out = lax.all_gather(out_piece, "dp", axis=0).reshape(dl, width)

        tokens_all = lax.all_gather(tokens, "ctx", axis=1, tiled=True)
        cot_all = lax.all_gather(cotangent, "ctx", axis=1, tiled=True)

    positions = jnp.arange(length, dtype=jnp.int32)
    cosine, sine = angles(positions, ROT)

    scaled_all, _ = normalise(tokens_all.astype(f32).reshape(rows, width))
    normed = (scaled_all * gain + shift).astype(b16)
    grad_out = cot_all.reshape(rows, width)

    mixed = times(normed, w_qkv) + b_qkv.astype(f32)
    shape4 = (seqs, length, heads, head_dim)
    q = rotate(mixed[:, :dl].reshape(shape4), cosine, sine, ROT).astype(b16)
    k = rotate(mixed[:, dl : 2 * dl].reshape(shape4), cosine, sine, ROT).astype(b16)
    v = mixed[:, 2 * dl :].astype(b16).reshape(shape4)
    attended, attention_back = attention(q, k, v, segments, None, cosine, sine)
    attended = attended.reshape(rows, dl).astype(b16)

    hidden = times(normed, w_fc1) + b_fc1.astype(f32)
    act, gelu_back = jax.vjp(gelu_tanh, hidden)
    act = act.astype(b16)
    partial = times(attended, w_out) + times(act, w_fc2)
    summed = lax.psum_scatter(
        partial.astype(b16).reshape(seqs, length, width), "ctx", scatter_dimension=1, tiled=True
    )
    result = (tokens.astype(f32) + summed.astype(f32) + (b_out + b_fc2)).astype(b16)

    grad_act = times_transposed(grad_out, w_fc2)
    grad_hidden = gelu_back(grad_act)[0].astype(b16)
    grad_fc2 = contract_rows(act, grad_out)
    grad_fc2 = lax.psum_scatter(grad_fc2.astype(b16), "dp", scatter_dimension=0, tiled=True)
    grad_fc1 = contract_rows(normed, grad_hidden)
    grad_fc1_b = jnp.sum(grad_hidden, axis=0, dtype=f32)
    grad_fc1 = lax.psum_scatter(grad_fc1.astype(b16), "dp", scatter_dimension=0, tiled=True)
    grad_out_w = contract_rows(attended, grad_out)
    grad_out_w = lax.psum_scatter(grad_out_w.astype(b16), "dp", scatter_dimension=0, tiled=True)
    grad_attended = times_transposed(grad_out, w_out).astype(b16).reshape(shape4)
    grad_q, grad_k, grad_v = attention_back(grad_attended)
    grad_mixed = jnp.concatenate(
        [
            rotate(grad_q, cosine, -sine, ROT).reshape(rows, dl),
            rotate(grad_k, cosine, -sine, ROT).reshape(rows, dl),
            grad_v.reshape(rows, dl),
        ],
        axis=1,
    ).astype(b16)
    grad_normed = times_transposed(grad_hidden, w_fc1) + times_transposed(grad_mixed, w_qkv)
    grad_normed = lax.psum_scatter(
        grad_normed.astype(b16).reshape(seqs, length, width), "ctx", scatter_dimension=1, tiled=True
    ).astype(f32)
    grad_qkv = contract_rows(normed, grad_mixed)
    grad_qkv_b = jnp.sum(grad_mixed, axis=0, dtype=f32)
    grad_qkv = lax.psum_scatter(grad_qkv.astype(b16), "dp", scatter_dimension=0, tiled=True)

    back = lax.all_to_all(
        jnp.concatenate([grad_qkv, grad_fc1], axis=1).reshape(ctx, wr, 3 * dl + fl),
        "ctx",
        split_axis=0,
        concat_axis=0,
    ).astype(f32)
    grad_qkv = jnp.moveaxis(back[:, :, : 3 * dl].reshape(ctx, wr, 3, dl), 0, 2).reshape(
        wr, 3 * width
    )
    grad_fc1 = jnp.moveaxis(back[:, :, 3 * dl :].reshape(ctx, wr, dp, fr), 0, 2).reshape(wr, ff)
    grad_out_w = lax.ppermute(grad_out_w, BOTH, out_back).astype(f32)
    grad_fc2 = grad_fc2.astype(f32)

    grad_normed = grad_normed.reshape(seqs, part, width)
    own = tokens.astype(f32)
    cot = cotangent.astype(f32)
    scaled, inverse = normalise(own)
    grad_gain = jnp.sum(grad_normed * scaled, axis=(0, 1))
    grad_shift = jnp.sum(grad_normed, axis=(0, 1))
    grad_scaled = grad_normed * gain
    grad_input = inverse * (
        grad_scaled
        - jnp.mean(grad_scaled, axis=-1, keepdims=True)
        - scaled * jnp.mean(grad_scaled * scaled, axis=-1, keepdims=True)
    )
    grad_tokens = (cot + grad_input).astype(b16)

    wide_qkv_b = lax.dynamic_update_index_in_dim(
        jnp.zeros((3, ctx, dl), f32), grad_qkv_b.reshape(3, dl), mine, 1
    )
    wide_fc1_b = lax.dynamic_update_index_in_dim(
        jnp.zeros((dp, ctx, fr), f32), grad_fc1_b.reshape(dp, fr), mine, 1
    )
    bias_out = jnp.sum(cot, axis=(0, 1))
    sums = jnp.concatenate(
        [
            x.reshape(devices, -1)
            for x in (wide_qkv_b, wide_fc1_b, bias_out, grad_gain, grad_shift)
        ],
        axis=1,
    )
    sums = lax.psum_scatter(sums, BOTH, scatter_dimension=0, tiled=True)[0]
    at = [0, marks[1], marks[2], marks[3], marks[3] + wr, marks[3] + 2 * wr]
    g_qkv_b, g_fc1_b, g_bias, g_gain, g_shift = [sums[a:b] for a, b in zip(at, at[1:])]
    return (
        result,
        grad_tokens,
        grad_qkv,
        g_qkv_b,
        grad_out_w,
        g_bias,
        grad_fc1,
        g_fc1_b,
        grad_fc2,
        g_bias,
        g_gain,
        g_shift,
    )


def solution(mesh):
    sizes = (mesh.shape["dp"], mesh.shape["ctx"])
    seq, mat, vec = P("dp", "ctx", None), P(BOTH, None), P(BOTH)
    placed = (seq, P("dp", None), mat, vec, mat, vec, mat, vec, mat, vec, vec, vec, seq)
    return jax.shard_map(
        lambda *args: local(*sizes, *args),
        mesh=mesh,
        in_specs=placed,
        out_specs=(seq, seq, mat, vec, mat, vec, mat, vec, mat, vec, vec, vec),
        check_vma=False,
    )
```

```python
import functools

import jax
import jax.numpy as jnp
import numpy as np
from jax import lax
from jax.experimental import pallas as pl
from jax.experimental.pallas import tpu as pltpu
from jax.sharding import PartitionSpec as P

HEADS = 16
ROT = 32
epsilon = 1e-05
BOTH = ("dp", "ctx")
MESH = pl.DeviceIdType.MESH


def angles(positions, rotary):
    freq_table = 1.0 / 10000.0 ** (jnp.arange(0, rotary, 2, dtype=jnp.float32) / rotary)
    theta = positions.astype(jnp.float32)[:, None] * freq_table[None, :]
    return (jnp.cos(theta)[:, None, :], jnp.sin(theta)[:, None, :])


def rotate(tensor, cosine, sine_table, rotary):
    half_len = rotary // 2
    first_half = tensor[..., :half_len]
    second_half = tensor[..., half_len:rotary]
    return jnp.concatenate(
        [
            first_half * cosine - second_half * sine_table,
            second_half * cosine + first_half * sine_table,
            tensor[..., rotary:],
        ],
        axis=-1,
    )


def contract_rows(left, right):
    return lax.dot_general(
        left, right, (((0,), (0,)), ((), ())), preferred_element_type=jnp.float32
    )


def times_transposed(left, right):
    return lax.dot_general(
        left, right, (((1,), (1,)), ((), ())), preferred_element_type=jnp.float32
    )


def times(left, right):
    return jnp.dot(left, right, preferred_element_type=jnp.float32)


def gelu_tanh(hidden_in):
    return jax.nn.gelu(hidden_in, approximate=True)


def normalise(inputs):
    center = inputs - jnp.mean(inputs, axis=-1, keepdims=True)
    inverse = lax.rsqrt(jnp.mean(center * center, axis=-1, keepdims=True) + epsilon)
    return center * inverse, inverse


def attention(q, k, v, segments, back, cosine, sine):
    length, head_dim = q.shape[1], q.shape[3]
    scale = float(head_dim) ** (-0.5)
    index = jnp.arange(length, dtype=jnp.int32)
    allowed = (segments[:, :, None] == segments[:, None, :]) & (index[None, :] <= index[:, None])[
        None
    ]
    scores = jnp.einsum("sqhd,skhd->shqk", q, k, preferred_element_type=jnp.float32) * scale
    scores = jnp.where(allowed[:, None], scores, -1e30)
    row_max = jnp.max(scores, axis=-1, keepdims=True)
    log_total = row_max + jnp.log(jnp.sum(jnp.exp(scores - row_max), axis=-1, keepdims=True))
    probs = jnp.exp(scores - log_total)
    probs_low = probs.astype(jnp.bfloat16)
    attended = jnp.einsum("shqk,skhd->sqhd", probs_low, v, preferred_element_type=jnp.float32)

    def backward(grad_attended):
        grad_weights = jnp.einsum(
            "sqhd,skhd->shqk", grad_attended, v, preferred_element_type=jnp.float32
        )
        row_dot = jnp.sum(grad_weights * probs, axis=-1, keepdims=True)
        grad_scores = (probs * (grad_weights - row_dot)).astype(jnp.bfloat16)
        grad_q = (
            jnp.einsum("shqk,skhd->sqhd", grad_scores, k, preferred_element_type=jnp.float32)
            * scale
        )
        grad_k = (
            jnp.einsum("shqk,sqhd->skhd", grad_scores, q, preferred_element_type=jnp.float32)
            * scale
        )
        grad_v = jnp.einsum(
            "shqk,sqhd->skhd", probs_low, grad_attended, preferred_element_type=jnp.float32
        )
        return grad_q, grad_k, grad_v

    return attended, backward


def dot(left, right, contract):
    return lax.dot_general(
        left, right, ((contract[:1], contract[1:]), ((), ())), preferred_element_type=jnp.float32
    )


NORMAL, RIGHT_T, LEFT_T = (1, 0), (1, 1), (0, 0)


def turn_tables(length, head_dim, lanes):
    half = ROT // 2
    freq = np.float32(1.0) / np.power(
        np.float32(10000.0), np.arange(0, ROT, 2, dtype=np.float32) / np.float32(ROT)
    )
    theta = np.arange(length, dtype=np.float32)[:, None] * freq[None, :]
    cosine, sine = np.cos(theta), np.sin(theta)
    keep = np.ones((length, head_dim), np.float32)
    keep[:, :half] = cosine
    keep[:, half:ROT] = cosine
    ahead = np.zeros((length, head_dim), np.float32)
    ahead[:, :half] = -sine
    behind = np.zeros((length, head_dim), np.float32)
    behind[:, half:ROT] = sine
    return [np.tile(t, (1, lanes // head_dim)) for t in (keep, ahead, behind)]


def turn(x, keep, ahead, behind):
    half, lanes = ROT // 2, x.shape[1]
    return (
        x * keep
        + pltpu.roll(x, lanes - half, axis=1) * ahead
        + pltpu.roll(x, half, axis=1) * behind
    )


def forward_kernel(
    nz, nc, marks,
    tok_ref, cot_ref, qkv_ref, fc1_ref, fc2_ref, out_ref, small_ref,
    seg_row_ref, seg_col_ref, keep_ref, ahead_ref, behind_ref,
    o_cot, o_qkv, o_fc1, o_fc2, o_out, o_small, o_normed, o_act, o_slope, o_attended, o_gmixed,
    tok_all, cot_all, w_qkv, w_fc1, w_fc2, w_out, small_all,
    small_rows, vec_d, b_qkv, b_fc1, normed, q_s, k_s, v_s, attended, g_att, act, slope, gmixed,
    acc_q, acc_k, acc_v, acc_a, bias_s,
    ctx_send, ctx_recv, z_send, z_recv, sib_send, sib_recv, loc, out_sem,
):
    f32, b16 = jnp.float32, jnp.bfloat16
    d, c = lax.axis_index("dp"), lax.axis_index("ctx")
    z, k = d // 2, lax.rem(d, 2)
    other = 2 * z + 1 - k
    wr, width = out_ref.shape
    dl = width // nc
    fr = fc2_ref.shape[0]
    nd = 2 * nz
    part = tok_ref.shape[0]
    length = part * nc
    head_dim = width // HEADS
    heads = HEADS // nc
    fl = nd * fr

    def ctx_to(j):
        return lax.rem(c + j, nc)

    def ctx_from(j):
        return lax.rem(c + nc - j, nc)

    def z_to(j):
        return 2 * lax.rem(z + j, nz) + k

    def z_from(j):
        return 2 * lax.rem(z + nz - j, nz) + k

    barrier = pltpu.get_barrier_semaphore()
    for j in range(1, nc):
        pl.semaphore_signal(barrier, inc=1, device_id=(d, ctx_to(j)), device_id_type=MESH)
    for j in range(1, nz):
        pl.semaphore_signal(barrier, inc=1, device_id=(z_to(j), c), device_id_type=MESH)
    pl.semaphore_signal(barrier, inc=1, device_id=(other, c), device_id_type=MESH)
    pl.semaphore_wait(barrier, nc + nz - 1)

    def remote(src, dst, send, recv, device):
        return pltpu.make_async_remote_copy(
            src_ref=src, dst_ref=dst, send_sem=send, recv_sem=recv,
            device_id=device, device_id_type=MESH,
        )

    def rows(at):
        return pl.ds(pl.multiple_of(at * wr, wr), wr)

    def lanes(at, size):
        return pl.ds(pl.multiple_of(at * size, size), size)

    SMALL, QKV, FC1, TOK, COT, OUT, FC2 = range(7)

    def ctx_pieces(array, to):
        if array == SMALL:
            return [(small_ref, small_all.at[d, c])]
        if array == QKV:
            return [
                (qkv_ref.at[:, lanes(t * nc + to, dl)], w_qkv.at[d, rows(c), pl.ds(t * dl, dl)])
                for t in range(3)
            ]
        if array == FC1:
            return [
                (fc1_ref.at[:, lanes(g * nc + to, fr)], w_fc1.at[d, rows(c), pl.ds(g * fr, fr)])
                for g in range(nd)
            ]
        if array == TOK:
            return [(tok_ref, tok_all.at[c])]
        return [(cot_ref, cot_all.at[c])]

    def ctx_whole(array, sub):
        return {
            SMALL: lambda: small_all.at[d, sub],
            QKV: lambda: w_qkv.at[d, rows(sub), :],
            FC1: lambda: w_fc1.at[d, rows(sub), :],
            TOK: lambda: tok_all.at[sub],
            COT: lambda: cot_all.at[sub],
        }[array]()

    def ctx_start(array):
        for j in range(1, nc):
            for src, dst in ctx_pieces(array, ctx_to(j)):
                remote(src, dst, ctx_send.at[array, j], ctx_recv.at[array, j], (d, ctx_to(j))).start()
        for src, dst in ctx_pieces(array, c):
            pltpu.make_async_copy(src, dst, loc.at[array]).start()

    def ctx_arrive(array, j):
        got = ctx_whole(array, ctx_from(j))
        if j == 0:
            pltpu.make_async_copy(got, got, loc.at[array]).wait()
        else:
            remote(got, got, ctx_send.at[array, j], ctx_recv.at[array, j], (d, ctx_to(j))).wait_recv()

    def ctx_sent(array):
        for j in range(1, nc):
            got = ctx_whole(array, ctx_from(j))
            remote(got, got, ctx_send.at[array, j], ctx_recv.at[array, j], (d, ctx_to(j))).wait_send()

    def ctx_finish(array):
        for j in range(nc):
            ctx_arrive(array, j)

    blocks = {SMALL: small_all, QKV: w_qkv, FC1: w_fc1, FC2: w_fc2}

    def z_copy(array, j, own):
        block = blocks[array].at[own]
        src = fc2_ref if array == FC2 else block
        return remote(src, block, z_send.at[array, j], z_recv.at[array, j], (z_to(j), c))

    def sib_copy(array, j, at):
        block = blocks[array].at[at]
        src = fc2_ref if array == FC2 and j == 0 else block
        return remote(src, block, sib_send.at[array, j], sib_recv.at[array, j], (other, c))

    def z_start(array):
        for j in range(1, nz):
            z_copy(array, j, d).start()
        sib_copy(array, 0, d).start()

    def z_pass_on(array):
        for j in range(1, nz):
            z_copy(array, j, z_from(j)).wait_recv()
            sib_copy(array, j, z_from(j)).start()

    def z_finish(array):
        for j in range(nz):
            sib_copy(array, j, lax.rem(z + nz - j, nz) * 2 + 1 - k).wait_recv()

    def z_sent(array):
        for j in range(1, nz):
            z_copy(array, j, d).wait_send()
        for j in range(nz):
            sib_copy(array, j, d if j == 0 else z_from(j)).wait_send()

    def out_copy(j, to, sub):
        return remote(out_ref, w_out.at[k, rows(sub), :], ctx_send.at[OUT, j], ctx_recv.at[OUT, j], (d, to))

    half = w_out.at[k]

    def out_z(j, to):
        return remote(half, half, z_send.at[OUT, j], z_recv.at[OUT, j], (to, c))

    def out_sib(which):
        piece = w_out.at[which]
        return remote(piece, piece, sib_send.at[OUT, 0], sib_recv.at[OUT, 0], (other, c))

    ctx_start(SMALL)
    ctx_start(QKV)
    own_out = pltpu.make_async_copy(out_ref, w_out.at[k, rows(c), :], loc.at[OUT])

    @pl.when(z == c)
    def _():
        own_out.start()

    for j in range(1, nc):
        @pl.when(ctx_to(j) == z)
        def _():
            out_copy(j, z, c).start()

    ctx_start(TOK)
    ctx_start(FC1)
    own_fc2 = pltpu.make_async_copy(fc2_ref, w_fc2.at[d], loc.at[FC2])
    own_fc2.start()

    ctx_finish(SMALL)
    z_start(SMALL)
    ctx_finish(QKV)
    z_start(QKV)

    @pl.when(z == c)
    def _():
        for j in range(1, nc):
            out_copy(j, z, ctx_from(j)).wait_recv()
        own_out.wait()
        for j in range(1, nz):
            out_z(j, z_to(j)).start()
        out_sib(k).start()

    ctx_start(COT)
    ctx_finish(FC1)
    z_pass_on(SMALL)
    z_finish(SMALL)

    def collect(p, carry):
        small_rows[pl.ds(p, 1), :] = small_all[p // nc, lax.rem(p, nc)]
        return carry

    lax.fori_loop(0, nd * nc, collect, 0)
    table = small_rows[...]
    pack = table.shape[1]

    def vector(mark, size, first, count):
        entry = lax.broadcasted_iota(jnp.int32, (1, count), 1).astype(f32) + first
        owner = jnp.floor((entry + 0.5) * (1.0 / size))
        lane = entry - owner * size + mark
        pick = lax.broadcasted_iota(jnp.int32, (pack, count), 0).astype(f32) == lane
        found = dot(table.astype(b16), jnp.where(pick, 1.0, 0.0).astype(b16), NORMAL)
        here = lax.broadcasted_iota(jnp.int32, (nd * nc, count), 0).astype(f32) == owner
        return jnp.sum(jnp.where(here, found, 0.0), axis=0, keepdims=True)

    for i in range(2):
        vec_d[pl.ds(i, 1), :] = vector(marks[2 + i], wr, 0.0, width)
    for t in range(3):
        b_qkv[:, pl.ds(t * dl, dl)] = vector(marks[1], 3 * wr, (t * width + c * dl).astype(f32), dl)
    for g in range(nd):
        b_fc1[:, pl.ds(g * fr, fr)] = small_all[g, c][:, :fr]

    z_pass_on(QKV)
    z_start(FC1)
    z_finish(QKV)

    chunk = 32

    def block_rows(b):
        return pl.ds(pl.multiple_of(b * part, part), part)

    def normalise_block(b):
        def step(i, carry):
            at = pl.multiple_of(i * chunk, chunk)
            x = tok_all[b, pl.ds(at, chunk), :].astype(f32)
            x = x - jnp.mean(x, axis=-1, keepdims=True)
            x = x * lax.rsqrt(jnp.mean(x * x, axis=-1, keepdims=True) + epsilon)
            normed[pl.ds(pl.multiple_of(b * part, part) + at, chunk), :] = (
                x * vec_d[0:1, :] + vec_d[1:2, :]
            ).astype(b16)
            return carry

        lax.fori_loop(0, part // chunk, step, 0)

    def qkv_block(b):
        at = block_rows(b)
        x = normed[at, :]
        keep = jnp.tile(keep_ref[at, :], (1, dl // keep_ref.shape[1]))
        ahead = jnp.tile(ahead_ref[at, :], (1, dl // keep_ref.shape[1]))
        behind = jnp.tile(behind_ref[at, :], (1, dl // keep_ref.shape[1]))
        for t, to in enumerate((q_s, k_s, v_s)):
            w = w_qkv[:, :, pl.ds(t * dl, dl)].reshape(width, dl)
            y = dot(x, w, NORMAL) + b_qkv[:, pl.ds(t * dl, dl)]
            if t < 2:
                y = turn(y, keep, ahead, behind)
            to[at, :] = y.astype(b16)

    for j in range(nc):
        ctx_arrive(TOK, j)
        normalise_block(ctx_from(j))
        qkv_block(ctx_from(j))

    z_pass_on(FC1)
    z_start(FC2)
    z_finish(FC1)

    def hidden_block(b, carry):
        at = block_rows(b)
        x = normed[at, :]
        for g in range(0, fl, 256):
            w = w_fc1[:, :, pl.ds(g, 256)].reshape(width, 256)
            h = dot(x, w, NORMAL) + b_fc1[:, pl.ds(g, 256)]
            s = h * h
            t = jnp.tanh(h * (0.7978845608028654 + (0.7978845608028654 * 0.044715) * s))
            half_t = 0.5 + 0.5 * t
            act[at, pl.ds(g, 256)] = (h * half_t).astype(b16)
            slope[at, pl.ds(g, 256)] = half_t + 0.5 * h * (1.0 - t * t) * (
                0.7978845608028654 + (3 * 0.7978845608028654 * 0.044715) * s
            )
        return carry

    lax.fori_loop(0, nc, hidden_block, 0)

    ctx_finish(COT)
    for j in range(1, nz):
        @pl.when(lax.rem(z + nz - j, nz) == c)
        def _():
            out_z(j, z_to(j)).wait_recv()
            out_sib(k).start()
    out_sib(1 - k).wait_recv()

    w_o = w_out[...].reshape(dl, width)

    def g_att_block(b, carry):
        g_att[block_rows(b), :] = dot(cot_all[b], w_o, RIGHT_T).astype(b16)
        return carry

    lax.fori_loop(0, nc, g_att_block, 0)

    tile = 256
    reach = 512 // tile
    scale = float(head_dim) ** (-0.5)
    acc_k[...] = jnp.zeros_like(acc_k)
    acc_v[...] = jnp.zeros_like(acc_v)
    for i in range(length // tile):
        first = max(0, i - reach) * tile
        count = (i + 1) * tile - first
        at = pl.ds(i * tile, tile)
        to = pl.ds(first, count)
        same = seg_col_ref[at, :1] == seg_row_ref[:1, to]
        row = lax.broadcasted_iota(jnp.int32, (tile, count), 0) + (i * tile - first)
        col = lax.broadcasted_iota(jnp.int32, (tile, count), 1)
        bias_s[:, :count] = jnp.where(same & (col <= row), 0.0, -1e30)
        acc_q[...] = jnp.zeros_like(acc_q)
        acc_a[...] = jnp.zeros_like(acc_a)

        def head_step(h, carry):
            lane = lax.broadcasted_iota(jnp.int32, (1, dl), 1)
            mine = (lane >= h * head_dim) & (lane < (h + 1) * head_dim)
            only = jnp.where(mine, 1.0, 0.0)
            only_low = only.astype(b16)
            qh = q_s[at, :] * only_low
            gh = g_att[at, :] * only_low
            keys, values = k_s[to, :], v_s[to, :]
            s = dot(qh, keys, RIGHT_T) * scale + bias_s[:, :count]
            e = jnp.exp(s - jnp.max(s, axis=-1, keepdims=True))
            p = e * (1.0 / jnp.sum(e, axis=-1, keepdims=True))
            p_low = p.astype(b16)
            acc_a[...] += dot(p_low, values, NORMAL) * only
            gw = dot(gh, values, RIGHT_T)
            gs = (p * (gw - jnp.sum(gw * p, axis=-1, keepdims=True))).astype(b16)
            acc_q[...] += dot(gs, keys, NORMAL) * only
            acc_k[to, :] += dot(gs, qh, LEFT_T)
            acc_v[to, :] += dot(p_low, gh, LEFT_T)
            return carry

        lax.fori_loop(0, heads, head_step, 0)
        attended[at, :] = acc_a[...].astype(b16)
        wide = (1, dl // keep_ref.shape[1])
        gmixed[at, pl.ds(0, dl)] = turn(
            acc_q[...] * scale,
            jnp.tile(keep_ref[at, :], wide),
            -jnp.tile(ahead_ref[at, :], wide),
            -jnp.tile(behind_ref[at, :], wide),
        ).astype(b16)

    def finish_block(b, carry):
        at = block_rows(b)
        wide = (1, dl // keep_ref.shape[1])
        gmixed[at, pl.ds(dl, dl)] = turn(
            acc_k[at, :] * scale,
            jnp.tile(keep_ref[at, :], wide),
            -jnp.tile(ahead_ref[at, :], wide),
            -jnp.tile(behind_ref[at, :], wide),
        ).astype(b16)
        gmixed[at, pl.ds(2 * dl, dl)] = acc_v[at, :].astype(b16)
        return carry

    lax.fori_loop(0, nc, finish_block, 0)

    own_fc2.wait()
    z_pass_on(FC2)
    z_finish(FC2)

    for array in (SMALL, QKV, FC1, FC2):
        z_sent(array)
    for array in (SMALL, QKV, FC1, TOK, COT):
        ctx_sent(array)
    for j in range(1, nc):
        @pl.when(ctx_to(j) == z)
        def _():
            out_copy(j, z, c).wait_send()

    @pl.when(z == c)
    def _():
        for j in range(1, nz):
            out_z(j, z_to(j)).wait_send()

    out_sib(k).wait_send()

    saves = [
        (cot_all, o_cot), (w_qkv, o_qkv), (w_fc1, o_fc1), (w_fc2, o_fc2), (w_out, o_out),
        (small_all, o_small), (normed, o_normed), (act, o_act), (slope, o_slope),
        (attended, o_attended), (gmixed, o_gmixed),
    ]
    for n, (src, dst) in enumerate(saves):
        pltpu.make_async_copy(src, dst, out_sem.at[n]).start()
    for n, (src, dst) in enumerate(saves):
        pltpu.make_async_copy(src, dst, out_sem.at[n]).wait()


def forward_all(nz, nc, marks, tokens, cotangent, segments, qkv_weight, fc1_weight, fc2_weight, out_weight, small):
    part, width = tokens.shape
    wr, fr = qkv_weight.shape[0], fc2_weight.shape[0]
    nd, dl = 2 * nz, width // nc
    length, fl = part * nc, 2 * nz * fr
    f32, b16 = jnp.float32, jnp.bfloat16
    tables = [jnp.asarray(t) for t in turn_tables(length, width // HEADS, 128)]
    seg_row = jnp.broadcast_to(segments.reshape(1, length), (8, length))
    seg_col = jnp.broadcast_to(segments.reshape(length, 1), (length, 128))
    gathered = [
        ((nc, part, width), b16),
        ((nc, part, width), b16),
        ((nd, nc * wr, 3 * dl), b16),
        ((nd, nc * wr, fl), b16),
        ((nd, fr, width), b16),
        ((2, nc * wr, width), b16),
        ((nd, nc) + small.shape, f32),
    ]
    shapes = gathered[1:] + [
        ((length, width), b16),
        ((length, fl), b16),
        ((length, fl), f32),
        ((length, dl), b16),
        ((length, 3 * dl), b16),
    ]
    work = gathered + [
        ((nd * nc, small.shape[1]), f32),
        ((8, width), f32),
        ((1, 3 * dl), f32),
        ((1, fl), f32),
        ((length, width), b16),
        ((length, dl), b16),
        ((length, dl), b16),
        ((length, dl), b16),
        ((length, dl), b16),
        ((length, dl), b16),
        ((length, fl), b16),
        ((length, fl), f32),
        ((length, 3 * dl), b16),
        ((256, dl), f32),
        ((length, dl), f32),
        ((length, dl), f32),
        ((256, dl), f32),
        ((256, 768), f32),
    ]
    hbm, vmem = pl.BlockSpec(memory_space=pl.ANY), pl.BlockSpec(memory_space=pltpu.VMEM)
    return pl.pallas_call(
        functools.partial(forward_kernel, nz, nc, marks),
        out_shape=[jax.ShapeDtypeStruct(s, t) for s, t in shapes],
        in_specs=[hbm] * 7 + [vmem] * 5,
        out_specs=[hbm] * len(shapes),
        scratch_shapes=[pltpu.VMEM(s, t) for s, t in work]
        + [
            pltpu.SemaphoreType.DMA((7, nc)),
            pltpu.SemaphoreType.DMA((7, nc)),
            pltpu.SemaphoreType.DMA((7, nz)),
            pltpu.SemaphoreType.DMA((7, nz)),
            pltpu.SemaphoreType.DMA((7, nz)),
            pltpu.SemaphoreType.DMA((7, nz)),
            pltpu.SemaphoreType.DMA((7,)),
            pltpu.SemaphoreType.DMA((len(shapes),)),
        ],
        compiler_params=pltpu.CompilerParams(
            collective_id=0, has_side_effects=True, vmem_limit_bytes=60 * 2**20
        ),
        name="forward",
    )(tokens, cotangent, qkv_weight, fc1_weight, fc2_weight, out_weight, small, seg_row, seg_col, *tables)


def local(
    dp,
    ctx,
    tokens,
    segments,
    qkv_weight,
    qkv_bias,
    out_weight,
    out_bias,
    fc1_weight,
    fc1_bias,
    fc2_weight,
    fc2_bias,
    norm_gain,
    norm_shift,
    cotangent,
):
    f32, b16 = jnp.float32, jnp.bfloat16
    seqs, part, width = tokens.shape
    length = part * ctx
    rows = seqs * length
    ff = fc1_weight.shape[1]
    fl, dl = ff // ctx, width // ctx
    heads = HEADS // ctx
    head_dim = width // HEADS
    wr, fr = qkv_weight.shape[0], fc2_weight.shape[0]
    mine = lax.axis_index("ctx")
    devices = dp * ctx

    pieces = [fc1_bias, qkv_bias, norm_gain, norm_shift, out_bias, fc2_bias]
    marks = [0]
    for piece in pieces:
        marks.append(marks[-1] + piece.shape[0])
    direct = wr % 16 == 0 and dp == 2 * ctx and seqs == 1
    if direct:
        vector = jnp.concatenate(pieces).astype(f32)
        vector = jnp.pad(vector, (0, -marks[-1] % 128))[None]
        cot_all, w_qkv, w_fc1, w_fc2, w_out, small, normed, act, slope, attended, grad_mixed = forward_all(
            dp // 2,
            ctx,
            tuple(marks),
            tokens[0],
            cotangent[0],
            segments[0],
            qkv_weight,
            fc1_weight,
            fc2_weight,
            out_weight,
            vector,
        )
        w_qkv, w_fc1 = w_qkv.reshape(width, 3 * dl), w_fc1.reshape(width, fl)
        w_fc2, w_out = w_fc2.reshape(fl, width), w_out.reshape(dl, width)
        small = small.reshape(devices, -1)
    else:
        small = lax.all_gather(jnp.concatenate(pieces), BOTH, axis=0)
    parts = [small[:, a:b] for a, b in zip(marks, marks[1:])]
    b_qkv = lax.dynamic_index_in_dim(
        parts[1].reshape(3, ctx, dl), mine, 1, keepdims=False
    ).reshape(3 * dl)
    b_fc1 = lax.dynamic_index_in_dim(
        parts[0].reshape(dp, ctx, fr), mine, 1, keepdims=False
    ).reshape(fl)
    gain, shift, b_out, b_fc2 = [p.reshape(width).astype(f32) for p in parts[2:]]

    out_perm = [(b, (b % dp) * ctx + b // dp) for b in range(devices)]
    out_back = [(j, i) for i, j in out_perm]
    if not direct:
        send_qkv = jnp.moveaxis(qkv_weight.reshape(wr, 3, ctx, dl), 2, 0).reshape(ctx, wr, 3 * dl)
        send_fc1 = jnp.moveaxis(fc1_weight.reshape(wr, dp, ctx, fr), 2, 0).reshape(ctx, wr, fl)
        sent = lax.all_to_all(
            jnp.concatenate([send_qkv, send_fc1], axis=2), "ctx", split_axis=0, concat_axis=0
        )
        out_piece = lax.ppermute(out_weight, BOTH, out_perm)
        w_qkv = lax.all_gather(sent[:, :, : 3 * dl], "dp", axis=0).reshape(width, 3 * dl)
        w_fc1 = lax.all_gather(sent[:, :, 3 * dl :], "dp", axis=0).reshape(width, fl)
        w_fc2 = lax.all_gather(fc2_weight, "dp", axis=0).reshape(fl, width)
        w_out = lax.all_gather(out_piece, "dp", axis=0).reshape(dl, width)

        tokens_all = lax.all_gather(tokens, "ctx", axis=1, tiled=True)
        cot_all = lax.all_gather(cotangent, "ctx", axis=1, tiled=True)

    grad_out = cot_all.reshape(rows, width)
    if not direct:
        positions = jnp.arange(length, dtype=jnp.int32)
        cosine, sine = angles(positions, ROT)

        scaled_all, _ = normalise(tokens_all.astype(f32).reshape(rows, width))
        normed = (scaled_all * gain + shift).astype(b16)

        mixed = times(normed, w_qkv) + b_qkv.astype(f32)
        shape4 = (seqs, length, heads, head_dim)
        q = rotate(mixed[:, :dl].reshape(shape4), cosine, sine, ROT).astype(b16)
        k = rotate(mixed[:, dl : 2 * dl].reshape(shape4), cosine, sine, ROT).astype(b16)
        v = mixed[:, 2 * dl :].astype(b16).reshape(shape4)
        attended, attention_back = attention(q, k, v, segments, None, cosine, sine)
        attended = attended.reshape(rows, dl).astype(b16)

        hidden = times(normed, w_fc1) + b_fc1.astype(f32)
        act, gelu_back = jax.vjp(gelu_tanh, hidden)
        act = act.astype(b16)

    partial = times(attended, w_out) + times(act, w_fc2)
    summed = lax.psum_scatter(
        partial.astype(b16).reshape(seqs, length, width), "ctx", scatter_dimension=1, tiled=True
    )
    result = (tokens.astype(f32) + summed.astype(f32) + (b_out + b_fc2)).astype(b16)

    grad_act = times_transposed(grad_out, w_fc2)
    grad_hidden = (grad_act * slope if direct else gelu_back(grad_act)[0]).astype(b16)
    grad_fc2 = contract_rows(act, grad_out)
    grad_fc2 = lax.psum_scatter(grad_fc2.astype(b16), "dp", scatter_dimension=0, tiled=True)
    grad_fc1 = contract_rows(normed, grad_hidden)
    grad_fc1_b = jnp.sum(grad_hidden, axis=0, dtype=f32)
    grad_fc1 = lax.psum_scatter(grad_fc1.astype(b16), "dp", scatter_dimension=0, tiled=True)
    grad_out_w = contract_rows(attended, grad_out)
    grad_out_w = lax.psum_scatter(grad_out_w.astype(b16), "dp", scatter_dimension=0, tiled=True)
    if not direct:
        grad_attended = times_transposed(grad_out, w_out).astype(b16).reshape(shape4)
        grad_q, grad_k, grad_v = attention_back(grad_attended)
        grad_mixed = jnp.concatenate(
            [
                rotate(grad_q, cosine, -sine, ROT).reshape(rows, dl),
                rotate(grad_k, cosine, -sine, ROT).reshape(rows, dl),
                grad_v.reshape(rows, dl),
            ],
            axis=1,
        ).astype(b16)
    grad_normed = times_transposed(grad_hidden, w_fc1) + times_transposed(grad_mixed, w_qkv)
    grad_normed = lax.psum_scatter(
        grad_normed.astype(b16).reshape(seqs, length, width), "ctx", scatter_dimension=1, tiled=True
    ).astype(f32)
    grad_qkv = contract_rows(normed, grad_mixed)
    grad_qkv_b = jnp.sum(grad_mixed, axis=0, dtype=f32)
    grad_qkv = lax.psum_scatter(grad_qkv.astype(b16), "dp", scatter_dimension=0, tiled=True)

    back = lax.all_to_all(
        jnp.concatenate([grad_qkv, grad_fc1], axis=1).reshape(ctx, wr, 3 * dl + fl),
        "ctx",
        split_axis=0,
        concat_axis=0,
    ).astype(f32)
    grad_qkv = jnp.moveaxis(back[:, :, : 3 * dl].reshape(ctx, wr, 3, dl), 0, 2).reshape(
        wr, 3 * width
    )
    grad_fc1 = jnp.moveaxis(back[:, :, 3 * dl :].reshape(ctx, wr, dp, fr), 0, 2).reshape(wr, ff)
    grad_out_w = lax.ppermute(grad_out_w, BOTH, out_back).astype(f32)
    grad_fc2 = grad_fc2.astype(f32)

    grad_normed = grad_normed.reshape(seqs, part, width)
    own = tokens.astype(f32)
    cot = cotangent.astype(f32)
    scaled, inverse = normalise(own)
    grad_gain = jnp.sum(grad_normed * scaled, axis=(0, 1))
    grad_shift = jnp.sum(grad_normed, axis=(0, 1))
    grad_scaled = grad_normed * gain
    grad_input = inverse * (
        grad_scaled
        - jnp.mean(grad_scaled, axis=-1, keepdims=True)
        - scaled * jnp.mean(grad_scaled * scaled, axis=-1, keepdims=True)
    )
    grad_tokens = (cot + grad_input).astype(b16)

    wide_qkv_b = lax.dynamic_update_index_in_dim(
        jnp.zeros((3, ctx, dl), f32), grad_qkv_b.reshape(3, dl), mine, 1
    )
    wide_fc1_b = lax.dynamic_update_index_in_dim(
        jnp.zeros((dp, ctx, fr), f32), grad_fc1_b.reshape(dp, fr), mine, 1
    )
    bias_out = jnp.sum(cot, axis=(0, 1))
    sums = jnp.concatenate(
        [
            x.reshape(devices, -1)
            for x in (wide_qkv_b, wide_fc1_b, bias_out, grad_gain, grad_shift)
        ],
        axis=1,
    )
    sums = lax.psum_scatter(sums, BOTH, scatter_dimension=0, tiled=True)[0]
    at = [0, 3 * wr, marks[2], marks[2] + wr, marks[2] + 2 * wr, marks[2] + 3 * wr]
    g_qkv_b, g_fc1_b, g_bias, g_gain, g_shift = [sums[a:b] for a, b in zip(at, at[1:])]
    return (
        result,
        grad_tokens,
        grad_qkv,
        g_qkv_b,
        grad_out_w,
        g_bias,
        grad_fc1,
        g_fc1_b,
        grad_fc2,
        g_bias,
        g_gain,
        g_shift,
    )


def solution(mesh):
    sizes = (mesh.shape["dp"], mesh.shape["ctx"])
    seq, mat, vec = P("dp", "ctx", None), P(BOTH, None), P(BOTH)
    placed = (seq, P("dp", None), mat, vec, mat, vec, mat, vec, mat, vec, vec, vec, seq)
    return jax.shard_map(
        lambda *args: local(*sizes, *args),
        mesh=mesh,
        in_specs=placed,
        out_specs=(seq, seq, mat, vec, mat, vec, mat, vec, mat, vec, vec, vec),
        check_vma=False,
    )
```

```python
import functools

import jax
import jax.numpy as jnp
import numpy as np
from jax import lax
from jax.experimental import pallas as pl
from jax.experimental.pallas import tpu as pltpu
from jax.sharding import PartitionSpec as P

HEADS = 16
ROT = 32
epsilon = 1e-05
BOTH = ("dp", "ctx")
MESH = pl.DeviceIdType.MESH


def angles(positions, rotary):
    freq_table = 1.0 / 10000.0 ** (jnp.arange(0, rotary, 2, dtype=jnp.float32) / rotary)
    theta = positions.astype(jnp.float32)[:, None] * freq_table[None, :]
    return (jnp.cos(theta)[:, None, :], jnp.sin(theta)[:, None, :])


def rotate(tensor, cosine, sine_table, rotary):
    half_len = rotary // 2
    first_half = tensor[..., :half_len]
    second_half = tensor[..., half_len:rotary]
    return jnp.concatenate(
        [
            first_half * cosine - second_half * sine_table,
            second_half * cosine + first_half * sine_table,
            tensor[..., rotary:],
        ],
        axis=-1,
    )


def contract_rows(left, right):
    return lax.dot_general(
        left, right, (((0,), (0,)), ((), ())), preferred_element_type=jnp.float32
    )


def times_transposed(left, right):
    return lax.dot_general(
        left, right, (((1,), (1,)), ((), ())), preferred_element_type=jnp.float32
    )


def times(left, right):
    return jnp.dot(left, right, preferred_element_type=jnp.float32)


def gelu_tanh(hidden_in):
    return jax.nn.gelu(hidden_in, approximate=True)


def normalise(inputs):
    center = inputs - jnp.mean(inputs, axis=-1, keepdims=True)
    inverse = lax.rsqrt(jnp.mean(center * center, axis=-1, keepdims=True) + epsilon)
    return center * inverse, inverse


def attention(q, k, v, segments, back, cosine, sine):
    length, head_dim = q.shape[1], q.shape[3]
    scale = float(head_dim) ** (-0.5)
    index = jnp.arange(length, dtype=jnp.int32)
    allowed = (segments[:, :, None] == segments[:, None, :]) & (index[None, :] <= index[:, None])[
        None
    ]
    scores = jnp.einsum("sqhd,skhd->shqk", q, k, preferred_element_type=jnp.float32) * scale
    scores = jnp.where(allowed[:, None], scores, -1e30)
    row_max = jnp.max(scores, axis=-1, keepdims=True)
    log_total = row_max + jnp.log(jnp.sum(jnp.exp(scores - row_max), axis=-1, keepdims=True))
    probs = jnp.exp(scores - log_total)
    probs_low = probs.astype(jnp.bfloat16)
    attended = jnp.einsum("shqk,skhd->sqhd", probs_low, v, preferred_element_type=jnp.float32)

    def backward(grad_attended):
        grad_weights = jnp.einsum(
            "sqhd,skhd->shqk", grad_attended, v, preferred_element_type=jnp.float32
        )
        row_dot = jnp.sum(grad_weights * probs, axis=-1, keepdims=True)
        grad_scores = (probs * (grad_weights - row_dot)).astype(jnp.bfloat16)
        grad_q = (
            jnp.einsum("shqk,skhd->sqhd", grad_scores, k, preferred_element_type=jnp.float32)
            * scale
        )
        grad_k = (
            jnp.einsum("shqk,sqhd->skhd", grad_scores, q, preferred_element_type=jnp.float32)
            * scale
        )
        grad_v = jnp.einsum(
            "shqk,sqhd->skhd", probs_low, grad_attended, preferred_element_type=jnp.float32
        )
        return grad_q, grad_k, grad_v

    return attended, backward


def local(
    dp,
    ctx,
    tokens,
    segments,
    qkv_weight,
    qkv_bias,
    out_weight,
    out_bias,
    fc1_weight,
    fc1_bias,
    fc2_weight,
    fc2_bias,
    norm_gain,
    norm_shift,
    cotangent,
):
    f32, b16 = jnp.float32, jnp.bfloat16
    seqs, part, width = tokens.shape
    length = part * ctx
    rows = seqs * length
    ff = fc1_weight.shape[1]
    fl, dl = ff // ctx, width // ctx
    heads = HEADS // ctx
    head_dim = width // HEADS
    wr, fr = qkv_weight.shape[0], fc2_weight.shape[0]
    mine = lax.axis_index("ctx")
    devices = dp * ctx

    pieces = [qkv_bias, fc1_bias, out_bias, fc2_bias, norm_gain, norm_shift]
    marks = [0]
    for piece in pieces:
        marks.append(marks[-1] + piece.shape[0])
    small = lax.all_gather(jnp.concatenate(pieces), BOTH, axis=0)
    parts = [small[:, a:b] for a, b in zip(marks, marks[1:])]
    b_qkv = lax.dynamic_index_in_dim(
        parts[0].reshape(3, ctx, dl), mine, 1, keepdims=False
    ).reshape(3 * dl)
    b_fc1 = lax.dynamic_index_in_dim(
        parts[1].reshape(dp, ctx, fr), mine, 1, keepdims=False
    ).reshape(fl)
    b_out, b_fc2, gain, shift = [p.reshape(width).astype(f32) for p in parts[2:]]

    send_qkv = jnp.moveaxis(qkv_weight.reshape(wr, 3, ctx, dl), 2, 0).reshape(ctx, wr, 3 * dl)
    send_fc1 = jnp.moveaxis(fc1_weight.reshape(wr, dp, ctx, fr), 2, 0).reshape(ctx, wr, fl)
    sent = lax.all_to_all(
        jnp.concatenate([send_qkv, send_fc1], axis=2), "ctx", split_axis=0, concat_axis=0
    )
    out_perm = [(b, (b % dp) * ctx + b // dp) for b in range(devices)]
    out_back = [(j, i) for i, j in out_perm]
    out_piece = lax.ppermute(out_weight, BOTH, out_perm)
    w_qkv = lax.all_gather(sent[:, :, : 3 * dl], "dp", axis=0).reshape(width, 3 * dl)
    w_fc1 = lax.all_gather(sent[:, :, 3 * dl :], "dp", axis=0).reshape(width, fl)
    w_fc2 = lax.all_gather(fc2_weight, "dp", axis=0).reshape(fl, width)
    w_out = lax.all_gather(out_piece, "dp", axis=0).reshape(dl, width)

    tokens_all = lax.all_gather(tokens, "ctx", axis=1, tiled=True)
    cot_all = lax.all_gather(cotangent, "ctx", axis=1, tiled=True)

    positions = jnp.arange(length, dtype=jnp.int32)
    cosine, sine = angles(positions, ROT)

    scaled_all, _ = normalise(tokens_all.astype(f32).reshape(rows, width))
    normed = (scaled_all * gain + shift).astype(b16)
    grad_out = cot_all.reshape(rows, width)

    mixed = times(normed, w_qkv) + b_qkv.astype(f32)
    shape4 = (seqs, length, heads, head_dim)
    q = rotate(mixed[:, :dl].reshape(shape4), cosine, sine, ROT).astype(b16)
    k = rotate(mixed[:, dl : 2 * dl].reshape(shape4), cosine, sine, ROT).astype(b16)
    v = mixed[:, 2 * dl :].astype(b16).reshape(shape4)
    attended, attention_back = attention(q, k, v, segments, None, cosine, sine)
    attended = attended.reshape(rows, dl).astype(b16)

    hidden = times(normed, w_fc1) + b_fc1.astype(f32)
    act, gelu_back = jax.vjp(gelu_tanh, hidden)
    act = act.astype(b16)
    partial = times(attended, w_out) + times(act, w_fc2)
    summed = lax.psum_scatter(
        partial.astype(b16).reshape(seqs, length, width), "ctx", scatter_dimension=1, tiled=True
    )
    result = (tokens.astype(f32) + summed.astype(f32) + (b_out + b_fc2)).astype(b16)

    grad_act = times_transposed(grad_out, w_fc2)
    grad_hidden = gelu_back(grad_act)[0].astype(b16)
    grad_fc2 = contract_rows(act, grad_out)
    grad_fc2 = lax.psum_scatter(grad_fc2.astype(b16), "dp", scatter_dimension=0, tiled=True)
    grad_fc1 = contract_rows(normed, grad_hidden)
    grad_fc1_b = jnp.sum(grad_hidden, axis=0, dtype=f32)
    grad_fc1 = lax.psum_scatter(grad_fc1.astype(b16), "dp", scatter_dimension=0, tiled=True)
    grad_out_w = contract_rows(attended, grad_out)
    grad_out_w = lax.psum_scatter(grad_out_w.astype(b16), "dp", scatter_dimension=0, tiled=True)
    grad_attended = times_transposed(grad_out, w_out).astype(b16).reshape(shape4)
    grad_q, grad_k, grad_v = attention_back(grad_attended)
    grad_mixed = jnp.concatenate(
        [
            rotate(grad_q, cosine, -sine, ROT).reshape(rows, dl),
            rotate(grad_k, cosine, -sine, ROT).reshape(rows, dl),
            grad_v.reshape(rows, dl),
        ],
        axis=1,
    ).astype(b16)
    grad_normed = times_transposed(grad_hidden, w_fc1) + times_transposed(grad_mixed, w_qkv)
    grad_normed = lax.psum_scatter(
        grad_normed.astype(b16).reshape(seqs, length, width), "ctx", scatter_dimension=1, tiled=True
    ).astype(f32)
    grad_qkv = contract_rows(normed, grad_mixed)
    grad_qkv_b = jnp.sum(grad_mixed, axis=0, dtype=f32)
    grad_qkv = lax.psum_scatter(grad_qkv.astype(b16), "dp", scatter_dimension=0, tiled=True)

    back = lax.all_to_all(
        jnp.concatenate([grad_qkv, grad_fc1], axis=1).reshape(ctx, wr, 3 * dl + fl),
        "ctx",
        split_axis=0,
        concat_axis=0,
    ).astype(f32)
    grad_qkv = jnp.moveaxis(back[:, :, : 3 * dl].reshape(ctx, wr, 3, dl), 0, 2).reshape(
        wr, 3 * width
    )
    grad_fc1 = jnp.moveaxis(back[:, :, 3 * dl :].reshape(ctx, wr, dp, fr), 0, 2).reshape(wr, ff)
    grad_out_w = lax.ppermute(grad_out_w, BOTH, out_back).astype(f32)
    grad_fc2 = grad_fc2.astype(f32)

    grad_normed = grad_normed.reshape(seqs, part, width)
    own = tokens.astype(f32)
    cot = cotangent.astype(f32)
    scaled, inverse = normalise(own)
    grad_gain = jnp.sum(grad_normed * scaled, axis=(0, 1))
    grad_shift = jnp.sum(grad_normed, axis=(0, 1))
    grad_scaled = grad_normed * gain
    grad_input = inverse * (
        grad_scaled
        - jnp.mean(grad_scaled, axis=-1, keepdims=True)
        - scaled * jnp.mean(grad_scaled * scaled, axis=-1, keepdims=True)
    )
    grad_tokens = (cot + grad_input).astype(b16)

    wide_qkv_b = lax.dynamic_update_index_in_dim(
        jnp.zeros((3, ctx, dl), f32), grad_qkv_b.reshape(3, dl), mine, 1
    )
    wide_fc1_b = lax.dynamic_update_index_in_dim(
        jnp.zeros((dp, ctx, fr), f32), grad_fc1_b.reshape(dp, fr), mine, 1
    )
    bias_out = jnp.sum(cot, axis=(0, 1))
    sums = jnp.concatenate(
        [
            x.reshape(devices, -1)
            for x in (wide_qkv_b, wide_fc1_b, bias_out, grad_gain, grad_shift)
        ],
        axis=1,
    )
    sums = lax.psum_scatter(sums, BOTH, scatter_dimension=0, tiled=True)[0]
    at = [0, marks[1], marks[2], marks[3], marks[3] + wr, marks[3] + 2 * wr]
    g_qkv_b, g_fc1_b, g_bias, g_gain, g_shift = [sums[a:b] for a, b in zip(at, at[1:])]
    return (
        result,
        grad_tokens,
        grad_qkv,
        g_qkv_b,
        grad_out_w,
        g_bias,
        grad_fc1,
        g_fc1_b,
        grad_fc2,
        g_bias,
        g_gain,
        g_shift,
    )


def dot(left, right, contract):
    return lax.dot_general(
        left, right, ((contract[:1], contract[1:]), ((), ())), preferred_element_type=jnp.float32
    )


NORMAL, RIGHT_T, LEFT_T = (1, 0), (1, 1), (0, 0)


def turn_tables(length, head_dim, lanes):
    half = ROT // 2
    freq = np.float32(1.0) / np.power(
        np.float32(10000.0), np.arange(0, ROT, 2, dtype=np.float32) / np.float32(ROT)
    )
    theta = np.arange(length, dtype=np.float32)[:, None] * freq[None, :]
    cosine, sine = np.cos(theta), np.sin(theta)
    keep = np.ones((length, head_dim), np.float32)
    keep[:, :half] = cosine
    keep[:, half:ROT] = cosine
    ahead = np.zeros((length, head_dim), np.float32)
    ahead[:, :half] = -sine
    behind = np.zeros((length, head_dim), np.float32)
    behind[:, half:ROT] = sine
    return [np.tile(t, (1, lanes // head_dim)) for t in (keep, ahead, behind)]


def turn(x, keep, ahead, behind):
    half, lanes = ROT // 2, x.shape[1]
    return (
        x * keep
        + pltpu.roll(x, lanes - half, axis=1) * ahead
        + pltpu.roll(x, half, axis=1) * behind
    )


def layer_kernel(
    nz, nc, marks,
    tok_ref, cot_ref, qkv_ref, fc1_ref, fc2_ref, out_ref, small_ref,
    seg_row_ref, seg_col_ref, keep_ref, ahead_ref, behind_ref,
    o_result, o_tokens, o_qkv, o_out, o_fc1, o_fc2, o_sums,
    tok_all, cot_all, w_qkv, w_fc1, w_fc2, w_out, small_all,
    small_rows, vec_d, b_qkv, b_fc1, normed, q_s, k_s, v_s, attended, g_att, act, slope, gmixed,
    acc_q, acc_k, acc_v, acc_a, bias_s, g_hidden,
    give_qkv, give_fc1, give_fc2, give_out, got_qkv, got_fc1, got_fc2, got_out,
    own_qkv, own_fc1, own_fc2, own_out_g, far_qkv, far_fc1, far_fc2, far_out,
    part_got, part_own, norm_got, norm_own,
    swap_qkv, swap_fc1, swap_out, swapped_qkv, swapped_fc1, swapped_out,
    sums, sums_sib, sums_z, sums_mine,
    ctx_send, ctx_recv, z_send, z_recv, sib_send, sib_recv, loc,
    back_z_send, back_z_recv, back_sib_send, back_sib_recv, back_ctx_send, back_ctx_recv,
):
    f32, b16 = jnp.float32, jnp.bfloat16
    d, c = lax.axis_index("dp"), lax.axis_index("ctx")
    z, k = d // 2, lax.rem(d, 2)
    other = 2 * z + 1 - k
    wr, width = out_ref.shape
    dl = width // nc
    fr = fc2_ref.shape[0]
    nd = 2 * nz
    part = tok_ref.shape[0]
    length = part * nc
    head_dim = width // HEADS
    heads = HEADS // nc
    fl = nd * fr

    def ctx_to(j):
        return lax.rem(c + j, nc)

    def ctx_from(j):
        return lax.rem(c + nc - j, nc)

    def z_to(j):
        return 2 * lax.rem(z + j, nz) + k

    def z_from(j):
        return 2 * lax.rem(z + nz - j, nz) + k

    barrier = pltpu.get_barrier_semaphore()
    for j in range(1, nc):
        pl.semaphore_signal(barrier, inc=1, device_id=(d, ctx_to(j)), device_id_type=MESH)
    for j in range(1, nz):
        pl.semaphore_signal(barrier, inc=1, device_id=(z_to(j), c), device_id_type=MESH)
    pl.semaphore_signal(barrier, inc=1, device_id=(other, c), device_id_type=MESH)
    pl.semaphore_wait(barrier, nc + nz - 1)

    def remote(src, dst, send, recv, device):
        return pltpu.make_async_remote_copy(
            src_ref=src, dst_ref=dst, send_sem=send, recv_sem=recv,
            device_id=device, device_id_type=MESH,
        )

    def rows(at):
        return pl.ds(pl.multiple_of(at * wr, wr), wr)

    def lanes(at, size):
        return pl.ds(pl.multiple_of(at * size, size), size)

    SMALL, QKV, FC1, TOK, COT, OUT, FC2 = range(7)

    def ctx_pieces(array, to):
        if array == SMALL:
            return [(small_ref, small_all.at[d, c])]
        if array == QKV:
            return [
                (qkv_ref.at[:, lanes(t * nc + to, dl)], w_qkv.at[d, rows(c), pl.ds(t * dl, dl)])
                for t in range(3)
            ]
        if array == FC1:
            return [
                (fc1_ref.at[:, lanes(g * nc + to, fr)], w_fc1.at[d, rows(c), pl.ds(g * fr, fr)])
                for g in range(nd)
            ]
        if array == TOK:
            return [(tok_ref, tok_all.at[c])]
        return [(cot_ref, cot_all.at[c])]

    def ctx_whole(array, sub):
        return {
            SMALL: lambda: small_all.at[d, sub],
            QKV: lambda: w_qkv.at[d, rows(sub), :],
            FC1: lambda: w_fc1.at[d, rows(sub), :],
            TOK: lambda: tok_all.at[sub],
            COT: lambda: cot_all.at[sub],
        }[array]()

    def ctx_start(array):
        for j in range(1, nc):
            for src, dst in ctx_pieces(array, ctx_to(j)):
                remote(src, dst, ctx_send.at[array, j], ctx_recv.at[array, j], (d, ctx_to(j))).start()
        for src, dst in ctx_pieces(array, c):
            pltpu.make_async_copy(src, dst, loc.at[array]).start()

    def ctx_arrive(array, j):
        got = ctx_whole(array, ctx_from(j))
        if j == 0:
            pltpu.make_async_copy(got, got, loc.at[array]).wait()
        else:
            remote(got, got, ctx_send.at[array, j], ctx_recv.at[array, j], (d, ctx_to(j))).wait_recv()

    def ctx_sent(array):
        for j in range(1, nc):
            got = ctx_whole(array, ctx_from(j))
            remote(got, got, ctx_send.at[array, j], ctx_recv.at[array, j], (d, ctx_to(j))).wait_send()

    def ctx_finish(array):
        for j in range(nc):
            ctx_arrive(array, j)

    blocks = {SMALL: small_all, QKV: w_qkv, FC1: w_fc1, FC2: w_fc2}

    def z_copy(array, j, own):
        block = blocks[array].at[own]
        src = fc2_ref if array == FC2 else block
        return remote(src, block, z_send.at[array, j], z_recv.at[array, j], (z_to(j), c))

    def sib_copy(array, j, at):
        block = blocks[array].at[at]
        src = fc2_ref if array == FC2 and j == 0 else block
        return remote(src, block, sib_send.at[array, j], sib_recv.at[array, j], (other, c))

    def z_start(array):
        for j in range(1, nz):
            z_copy(array, j, d).start()
        sib_copy(array, 0, d).start()

    def z_pass_on(array):
        for j in range(1, nz):
            z_copy(array, j, z_from(j)).wait_recv()
            sib_copy(array, j, z_from(j)).start()

    def z_finish(array):
        for j in range(nz):
            sib_copy(array, j, lax.rem(z + nz - j, nz) * 2 + 1 - k).wait_recv()

    def z_sent(array):
        for j in range(1, nz):
            z_copy(array, j, d).wait_send()
        for j in range(nz):
            sib_copy(array, j, d if j == 0 else z_from(j)).wait_send()

    def out_copy(j, to, sub):
        return remote(out_ref, w_out.at[k, rows(sub), :], ctx_send.at[OUT, j], ctx_recv.at[OUT, j], (d, to))

    half = w_out.at[k]

    def out_z(j, to):
        return remote(half, half, z_send.at[OUT, j], z_recv.at[OUT, j], (to, c))

    def out_sib(which):
        piece = w_out.at[which]
        return remote(piece, piece, sib_send.at[OUT, 0], sib_recv.at[OUT, 0], (other, c))

    ctx_start(SMALL)
    ctx_start(QKV)
    own_out = pltpu.make_async_copy(out_ref, w_out.at[k, rows(c), :], loc.at[OUT])

    @pl.when(z == c)
    def _():
        own_out.start()

    for j in range(1, nc):
        @pl.when(ctx_to(j) == z)
        def _():
            out_copy(j, z, c).start()

    ctx_start(TOK)
    ctx_start(FC1)
    copy_fc2 = pltpu.make_async_copy(fc2_ref, w_fc2.at[d], loc.at[FC2])
    copy_fc2.start()

    ctx_finish(SMALL)
    z_start(SMALL)
    ctx_finish(QKV)
    z_start(QKV)

    @pl.when(z == c)
    def _():
        for j in range(1, nc):
            out_copy(j, z, ctx_from(j)).wait_recv()
        own_out.wait()
        for j in range(1, nz):
            out_z(j, z_to(j)).start()
        out_sib(k).start()

    ctx_start(COT)
    ctx_finish(FC1)
    z_pass_on(SMALL)
    z_finish(SMALL)

    def collect(p, carry):
        small_rows[pl.ds(p, 1), :] = small_all[p // nc, lax.rem(p, nc)]
        return carry

    lax.fori_loop(0, nd * nc, collect, 0)
    table = small_rows[...]
    pack = table.shape[1]

    def vector(mark, size, first, count):
        entry = lax.broadcasted_iota(jnp.int32, (1, count), 1).astype(f32) + first
        owner = jnp.floor((entry + 0.5) * (1.0 / size))
        lane = entry - owner * size + mark
        pick = lax.broadcasted_iota(jnp.int32, (pack, count), 0).astype(f32) == lane
        found = dot(table.astype(b16), jnp.where(pick, 1.0, 0.0).astype(b16), NORMAL)
        here = lax.broadcasted_iota(jnp.int32, (nd * nc, count), 0).astype(f32) == owner
        return jnp.sum(jnp.where(here, found, 0.0), axis=0, keepdims=True)

    for i in range(2):
        vec_d[pl.ds(i, 1), :] = vector(marks[2 + i], wr, 0.0, width)
    vec_d[2:3, :] = vector(marks[4], wr, 0.0, width) + vector(marks[5], wr, 0.0, width)
    for t in range(3):
        b_qkv[:, pl.ds(t * dl, dl)] = vector(marks[1], 3 * wr, (t * width + c * dl).astype(f32), dl)
    for g in range(nd):
        b_fc1[:, pl.ds(g * fr, fr)] = small_all[g, c][:, :fr]

    z_pass_on(QKV)
    z_start(FC1)
    z_finish(QKV)

    chunk = 32

    def block_rows(b):
        return pl.ds(pl.multiple_of(b * part, part), part)

    def normalise_block(b):
        def step(i, carry):
            at = pl.multiple_of(i * chunk, chunk)
            x = tok_all[b, pl.ds(at, chunk), :].astype(f32)
            x = x - jnp.mean(x, axis=-1, keepdims=True)
            x = x * lax.rsqrt(jnp.mean(x * x, axis=-1, keepdims=True) + epsilon)
            normed[pl.ds(pl.multiple_of(b * part, part) + at, chunk), :] = (
                x * vec_d[0:1, :] + vec_d[1:2, :]
            ).astype(b16)
            return carry

        lax.fori_loop(0, part // chunk, step, 0)

    def qkv_block(b):
        at = block_rows(b)
        x = normed[at, :]
        keep = jnp.tile(keep_ref[at, :], (1, dl // keep_ref.shape[1]))
        ahead = jnp.tile(ahead_ref[at, :], (1, dl // keep_ref.shape[1]))
        behind = jnp.tile(behind_ref[at, :], (1, dl // keep_ref.shape[1]))
        for t, to in enumerate((q_s, k_s, v_s)):
            w = w_qkv[:, :, pl.ds(t * dl, dl)].reshape(width, dl)
            y = dot(x, w, NORMAL) + b_qkv[:, pl.ds(t * dl, dl)]
            if t < 2:
                y = turn(y, keep, ahead, behind)
            to[at, :] = y.astype(b16)

    for j in range(nc):
        ctx_arrive(TOK, j)
        normalise_block(ctx_from(j))
        qkv_block(ctx_from(j))

    z_pass_on(FC1)
    z_start(FC2)
    z_finish(FC1)

    def hidden_block(b, carry):
        at = block_rows(b)
        x = normed[at, :]
        for g in range(0, fl, 256):
            w = w_fc1[:, :, pl.ds(g, 256)].reshape(width, 256)
            h = dot(x, w, NORMAL) + b_fc1[:, pl.ds(g, 256)]
            s = h * h
            t = jnp.tanh(h * (0.7978845608028654 + (0.7978845608028654 * 0.044715) * s))
            half_t = 0.5 + 0.5 * t
            act[at, pl.ds(g, 256)] = (h * half_t).astype(b16)
            slope[at, pl.ds(g, 256)] = half_t + 0.5 * h * (1.0 - t * t) * (
                0.7978845608028654 + (3 * 0.7978845608028654 * 0.044715) * s
            )
        return carry

    lax.fori_loop(0, nc, hidden_block, 0)

    ctx_finish(COT)

    gives = {QKV: give_qkv, FC1: give_fc1, FC2: give_fc2, OUT: give_out}
    gots = {QKV: got_qkv, FC1: got_fc1, FC2: got_fc2, OUT: got_out}
    owns = {QKV: own_qkv, FC1: own_fc1, FC2: own_fc2, OUT: own_out_g}
    fars = {QKV: far_qkv, FC1: far_fc1, FC2: far_fc2, OUT: far_out}

    def cotangents():
        return cot_all[...].reshape(length, width)

    def weight_gradient(array, left, right):
        give, own = gives[array], owns[array]
        size = give.shape[1]

        def step(i, carry):
            both = dot(left[:, lanes(i, 2 * size)], right(), LEFT_T)
            low, high = both[:size], both[size:]
            own[i] = jnp.where(k == 0, low, high)
            give[i] = jnp.where(k == 0, high, low).astype(b16)
            return carry

        lax.fori_loop(0, give.shape[0], step, 0)
        to_sibling(array).start()

    def to_sibling(array):
        return remote(
            gives[array], gots[array], back_sib_send.at[array], back_sib_recv.at[array], (other, c)
        )

    def z_other(j):
        return lax.rem(z + j, nz)

    def to_owner(array, j):
        block = gives[array].at[0 if array == OUT else z_other(j)]
        return remote(
            block, fars[array].at[j - 1], back_z_send.at[array, j], back_z_recv.at[array, j], (z_to(j), c)
        )

    def add_sibling(array):
        to_sibling(array).wait()
        give, got, own = gives[array], gots[array], owns[array]
        for j in range(1, nz):
            if array == OUT:
                @pl.when(z_other(j) == c)
                def _():
                    give[0] = (own[0] + got[0].astype(f32)).astype(b16)
                    to_owner(OUT, j).start()
            else:
                at = z_other(j)
                give[at] = (own[at] + got[at].astype(f32)).astype(b16)
                to_owner(array, j).start()

    def total(array):
        at = 0 if array == OUT else z
        x = owns[array][at] + gots[array][at].astype(f32)
        for j in range(1, nz):
            x = x + fars[array][j - 1].astype(f32)
        return x

    PART, NORM, SUMS = TOK, COT, SMALL

    def over_ctx(array, src, dst, j, to):
        return remote(src, dst, back_ctx_send.at[array, j], back_ctx_recv.at[array, j], (d, to))

    weight_gradient(FC2, act, cotangents)

    for j in range(1, nz):
        @pl.when(lax.rem(z + nz - j, nz) == c)
        def _():
            out_z(j, z_to(j)).wait_recv()
            out_sib(k).start()
    out_sib(1 - k).wait_recv()

    w_o = w_out[...].reshape(dl, width)

    def g_att_block(b, carry):
        g_att[block_rows(b), :] = dot(cot_all[b], w_o, RIGHT_T).astype(b16)
        return carry

    lax.fori_loop(0, nc, g_att_block, 0)
    add_sibling(FC2)

    tile = 256
    reach = 512 // tile
    scale = float(head_dim) ** (-0.5)
    acc_k[...] = jnp.zeros_like(acc_k)
    acc_v[...] = jnp.zeros_like(acc_v)
    for i in range(length // tile):
        first = max(0, i - reach) * tile
        count = (i + 1) * tile - first
        at = pl.ds(i * tile, tile)
        to = pl.ds(first, count)
        same = seg_col_ref[at, :1] == seg_row_ref[:1, to]
        row = lax.broadcasted_iota(jnp.int32, (tile, count), 0) + (i * tile - first)
        col = lax.broadcasted_iota(jnp.int32, (tile, count), 1)
        bias_s[:, :count] = jnp.where(same & (col <= row), 0.0, -1e30)
        acc_q[...] = jnp.zeros_like(acc_q)
        acc_a[...] = jnp.zeros_like(acc_a)

        def head_step(h, carry):
            lane = lax.broadcasted_iota(jnp.int32, (1, dl), 1)
            mine = (lane >= h * head_dim) & (lane < (h + 1) * head_dim)
            only = jnp.where(mine, 1.0, 0.0)
            only_low = only.astype(b16)
            qh = q_s[at, :] * only_low
            gh = g_att[at, :] * only_low
            keys, values = k_s[to, :], v_s[to, :]
            s = dot(qh, keys, RIGHT_T) * scale + bias_s[:, :count]
            e = jnp.exp(s - jnp.max(s, axis=-1, keepdims=True))
            p = e * (1.0 / jnp.sum(e, axis=-1, keepdims=True))
            p_low = p.astype(b16)
            acc_a[...] += dot(p_low, values, NORMAL) * only
            gw = dot(gh, values, RIGHT_T)
            gs = (p * (gw - jnp.sum(gw * p, axis=-1, keepdims=True))).astype(b16)
            acc_q[...] += dot(gs, keys, NORMAL) * only
            acc_k[to, :] += dot(gs, qh, LEFT_T)
            acc_v[to, :] += dot(p_low, gh, LEFT_T)
            return carry

        lax.fori_loop(0, heads, head_step, 0)
        attended[at, :] = acc_a[...].astype(b16)
        wide = (1, dl // keep_ref.shape[1])
        gmixed[at, pl.ds(0, dl)] = turn(
            acc_q[...] * scale,
            jnp.tile(keep_ref[at, :], wide),
            -jnp.tile(ahead_ref[at, :], wide),
            -jnp.tile(behind_ref[at, :], wide),
        ).astype(b16)

    def finish_block(b, carry):
        at = block_rows(b)
        wide = (1, dl // keep_ref.shape[1])
        gmixed[at, pl.ds(dl, dl)] = turn(
            acc_k[at, :] * scale,
            jnp.tile(keep_ref[at, :], wide),
            -jnp.tile(ahead_ref[at, :], wide),
            -jnp.tile(behind_ref[at, :], wide),
        ).astype(b16)
        gmixed[at, pl.ds(2 * dl, dl)] = acc_v[at, :].astype(b16)
        return carry

    lax.fori_loop(0, nc, finish_block, 0)

    weight_gradient(QKV, normed, lambda: gmixed[...])
    weight_gradient(OUT, attended, cotangents)

    copy_fc2.wait()
    z_pass_on(FC2)
    z_finish(FC2)

    def hidden_gradient(b, carry):
        at = block_rows(b)
        g = cot_all[b]
        for i in range(nd):
            to = pl.ds(i * fr, fr)
            g_hidden[at, to] = (dot(g, w_fc2[i], RIGHT_T) * slope[at, to]).astype(b16)
        return carry

    lax.fori_loop(0, nc, hidden_gradient, 0)
    add_sibling(QKV)
    add_sibling(OUT)
    weight_gradient(FC1, normed, lambda: g_hidden[...])

    def result_term(b):
        at = block_rows(b)
        return dot(attended[at, :], w_out[...].reshape(dl, width), NORMAL) + dot(
            act[at, :], w_fc2[...].reshape(fl, width), NORMAL
        )

    for j in range(1, nc):
        b = ctx_to(j)
        tok_all[b] = result_term(b).astype(b16)
        over_ctx(PART, tok_all.at[b], part_got.at[j - 1], j, b).start()
    part_own[...] = result_term(c)
    add_sibling(FC1)

    def normed_term(b):
        at = block_rows(b)
        return dot(g_hidden[at, :], w_fc1[...].reshape(width, fl), RIGHT_T) + dot(
            gmixed[at, :], w_qkv[...].reshape(width, 3 * dl), RIGHT_T
        )

    for j in range(1, nc):
        b = ctx_to(j)
        cot_all[b] = normed_term(b).astype(b16)
        over_ctx(NORM, cot_all.at[b], norm_got.at[j - 1], j, b).start()
    norm_own[...] = normed_term(c)

    ones = jnp.ones((8, length), b16)
    sums[0, :, pl.ds(0, 3 * dl)] = dot(ones, gmixed[...], NORMAL)[:1]
    sums[0, :, pl.ds(3 * dl, fl)] = dot(ones, g_hidden[...], NORMAL)[:1]
    at_sum = 3 * dl + fl
    sums[0, :, pl.ds(at_sum, width)] = dot(ones[:, :part], cot_all[c], NORMAL)[:1]

    for j in range(1, nc):
        over_ctx(PART, tok_all.at[c], part_got.at[j - 1], j, c).wait_recv()

    def result_step(i, carry):
        at = pl.ds(pl.multiple_of(i * chunk, chunk), chunk)
        y = tok_all[c, at, :].astype(f32) + part_own[at, :] + vec_d[2:3, :]
        for j in range(1, nc):
            y = y + part_got[j - 1, at, :].astype(f32)
        o_result[at, :] = y.astype(b16)
        return carry

    lax.fori_loop(0, part // chunk, result_step, 0)

    for j in range(1, nc):
        over_ctx(NORM, cot_all.at[c], norm_got.at[j - 1], j, c).wait_recv()

    def norm_step(i, carry):
        gain_sum, shift_sum = carry
        at = pl.ds(pl.multiple_of(i * chunk, chunk), chunk)
        x = tok_all[c, at, :].astype(f32)
        x = x - jnp.mean(x, axis=-1, keepdims=True)
        inverse = lax.rsqrt(jnp.mean(x * x, axis=-1, keepdims=True) + epsilon)
        x = x * inverse
        g = norm_own[at, :]
        for j in range(1, nc):
            g = g + norm_got[j - 1, at, :].astype(f32)
        v = g * vec_d[0:1, :]
        y = inverse * (
            v - jnp.mean(v, axis=-1, keepdims=True) - x * jnp.mean(v * x, axis=-1, keepdims=True)
        )
        o_tokens[at, :] = (cot_all[c, at, :].astype(f32) + y).astype(b16)
        return (
            gain_sum + jnp.sum(g * x, axis=0, keepdims=True),
            shift_sum + jnp.sum(g, axis=0, keepdims=True),
        )

    zero = jnp.zeros((1, width), f32)
    gain_sum, shift_sum = lax.fori_loop(0, part // chunk, norm_step, (zero, zero))
    sums[0, :, pl.ds(at_sum + width, width)] = gain_sum
    sums[0, :, pl.ds(at_sum + 2 * width, width)] = shift_sum

    sum_sib = remote(sums.at[0], sums_sib.at[0], back_sib_send.at[SUMS], back_sib_recv.at[SUMS], (other, c))
    sum_sib.start()
    sum_sib.wait()
    sums[1] = sums[0] + sums_sib[0]

    def sum_z(j):
        return remote(
            sums.at[1], sums_z.at[j - 1], back_z_send.at[SUMS, j], back_z_recv.at[SUMS, j], (z_to(j), c)
        )

    for j in range(1, nz):
        sum_z(j).start()

    def from_owner(array):
        for j in range(1, nz):
            to_owner(array, j).wait_recv()

    from_owner(FC2)
    o_fc2[...] = total(FC2)

    swaps = {QKV: (swap_qkv, swapped_qkv), FC1: (swap_fc1, swapped_fc1)}

    def place(array, source, x):
        if array == QKV:
            for t in range(3):
                o_qkv[:, lanes(t * nc + source, dl)] = x[:, t * dl : (t + 1) * dl]
        else:
            for g in range(nd):
                o_fc1[:, lanes(g * nc + source, fr)] = x[:, g * fr : (g + 1) * fr]

    def swap_start(array):
        from_owner(array)
        src, dst = swaps[array]
        own = owns[array]
        own[z] = total(array)
        for j in range(1, nc):
            src[j - 1] = own[z, rows(ctx_to(j)), :].astype(b16)
            over_ctx(array, src.at[j - 1], dst.at[j - 1], j, ctx_to(j)).start()
        place(array, c, own[z, rows(c), :])

    def swap_finish(array):
        src, dst = swaps[array]
        for j in range(1, nc):
            over_ctx(array, src.at[j - 1], dst.at[j - 1], j, ctx_to(j)).wait_recv()
            place(array, ctx_from(j), dst[j - 1].astype(f32))

    swap_start(QKV)

    @pl.when(z == c)
    def _():
        from_owner(OUT)
        own_out_g[0] = total(OUT)
        for j in range(1, nc):
            swap_out[j - 1] = own_out_g[0, rows(ctx_to(j)), :].astype(b16)
            over_ctx(OUT, swap_out.at[j - 1], swapped_out.at[0], j, ctx_to(j)).start()
        o_out[...] = own_out_g[0, rows(c), :]

    for j in range(1, nz):
        sum_z(j).wait()
    mine_sum = sums[1]
    for j in range(1, nz):
        mine_sum = mine_sum + sums_z[j - 1]
    sums_mine[0] = mine_sum
    o_sums[c] = mine_sum
    for j in range(1, nc):
        over_ctx(SUMS, sums_mine.at[0], o_sums.at[c], j, ctx_to(j)).start()

    swap_finish(QKV)
    for j in range(1, nc):
        @pl.when(ctx_from(j) == z)
        def _():
            over_ctx(OUT, swap_out.at[0], swapped_out.at[0], j, ctx_to(j)).wait_recv()
            o_out[...] = swapped_out[0].astype(f32)
    for j in range(1, nc):
        over_ctx(SUMS, sums_mine.at[0], o_sums.at[ctx_from(j)], j, ctx_to(j)).wait_recv()

    swap_start(FC1)
    swap_finish(FC1)

    for array in (SMALL, QKV, FC1, FC2):
        z_sent(array)
    for array in (SMALL, QKV, FC1, TOK, COT):
        ctx_sent(array)
    for j in range(1, nc):
        @pl.when(ctx_to(j) == z)
        def _():
            out_copy(j, z, c).wait_send()

    @pl.when(z == c)
    def _():
        for j in range(1, nz):
            out_z(j, z_to(j)).wait_send()

    out_sib(k).wait_send()
    for array in (QKV, FC1, FC2):
        for j in range(1, nz):
            to_owner(array, j).wait_send()
    for j in range(1, nz):
        @pl.when(z_other(j) == c)
        def _():
            to_owner(OUT, j).wait_send()
    for j in range(1, nc):
        over_ctx(PART, tok_all.at[c], part_got.at[j - 1], j, c).wait_send()
        over_ctx(NORM, cot_all.at[c], norm_got.at[j - 1], j, c).wait_send()
        over_ctx(SUMS, sums_mine.at[0], o_sums.at[c], j, ctx_to(j)).wait_send()
        for array in (QKV, FC1):
            over_ctx(array, swaps[array][0].at[j - 1], swaps[array][1].at[j - 1], j, c).wait_send()

    @pl.when(z == c)
    def _():
        for j in range(1, nc):
            over_ctx(OUT, swap_out.at[j - 1], swapped_out.at[0], j, ctx_to(j)).wait_send()


def layer_all(nz, nc, marks, tokens, cotangent, segments, qkv_weight, fc1_weight, fc2_weight, out_weight, small):
    part, width = tokens.shape
    wr, fr = qkv_weight.shape[0], fc2_weight.shape[0]
    nd, dl = 2 * nz, width // nc
    length, fl = part * nc, 2 * nz * fr
    cw = nc * wr
    f32, b16 = jnp.float32, jnp.bfloat16
    tables = [jnp.asarray(t) for t in turn_tables(length, width // HEADS, 128)]
    seg_row = jnp.broadcast_to(segments.reshape(1, length), (8, length))
    seg_col = jnp.broadcast_to(segments.reshape(length, 1), (length, 128))
    pack = small.shape[1]
    total = 3 * dl + fl + 3 * width
    tile, window = 256, 768
    results = [
        ((part, width), b16),
        ((part, width), b16),
        ((wr, 3 * width), f32),
        ((wr, width), f32),
        ((wr, fl * nc), f32),
        ((fr, width), f32),
        ((nc, 1, total), f32),
    ]
    work = [
        ((nc, part, width), b16),
        ((nc, part, width), b16),
        ((nd, cw, 3 * dl), b16),
        ((nd, cw, fl), b16),
        ((nd, fr, width), b16),
        ((2, cw, width), b16),
        ((nd, nc, 1, pack), f32),
        ((nd * nc, pack), f32),
        ((8, width), f32),
        ((1, 3 * dl), f32),
        ((1, fl), f32),
        ((length, width), b16),
        ((length, dl), b16),
        ((length, dl), b16),
        ((length, dl), b16),
        ((length, dl), b16),
        ((length, dl), b16),
        ((length, fl), b16),
        ((length, fl), f32),
        ((length, 3 * dl), b16),
        ((tile, dl), f32),
        ((length, dl), f32),
        ((length, dl), f32),
        ((tile, dl), f32),
        ((tile, window), f32),
        ((length, fl), b16),
    ]
    grads = [(nz, cw, 3 * dl), (nz, cw, fl), (nz, fr, width), (1, cw, width)]
    fars = [(nz - 1,) + g[1:] for g in grads]
    work += [(g, b16) for g in grads] + [(g, b16) for g in grads] + [(g, f32) for g in grads]
    work += [(g, b16) for g in fars]
    work += [((nc - 1, part, width), b16), ((part, width), f32)] * 2
    work += [((nc - 1, wr, n), b16) for n in (3 * dl, fl, width)]
    work += [((nc - 1, wr, n), b16) for n in (3 * dl, fl)] + [((1, wr, width), b16)]
    work += [((n, 1, total), f32) for n in (2, 1, nz - 1, 1)]
    dma = pltpu.SemaphoreType.DMA
    sems = [(7, nc), (7, nc), (7, nz), (7, nz), (7, nz), (7, nz), (7,)]
    sems += [(7, nz), (7, nz), (7,), (7,), (7, nc), (7, nc)]
    hbm, vmem = pl.BlockSpec(memory_space=pl.ANY), pl.BlockSpec(memory_space=pltpu.VMEM)
    return pl.pallas_call(
        functools.partial(layer_kernel, nz, nc, marks),
        out_shape=[jax.ShapeDtypeStruct(s, t) for s, t in results],
        in_specs=[hbm] * 7 + [vmem] * 5,
        out_specs=[vmem] * len(results),
        scratch_shapes=[pltpu.VMEM(s, t) for s, t in work] + [dma(s) for s in sems],
        compiler_params=pltpu.CompilerParams(
            collective_id=0, has_side_effects=True, vmem_limit_bytes=62 * 2**20
        ),
        name="layer",
    )(tokens, cotangent, qkv_weight, fc1_weight, fc2_weight, out_weight, small, seg_row, seg_col, *tables)


def local_direct(
    dp,
    ctx,
    tokens,
    segments,
    qkv_weight,
    qkv_bias,
    out_weight,
    out_bias,
    fc1_weight,
    fc1_bias,
    fc2_weight,
    fc2_bias,
    norm_gain,
    norm_shift,
    cotangent,
):
    width = tokens.shape[-1]
    dl, fl = width // ctx, fc1_weight.shape[1] // ctx
    wr, fr = qkv_weight.shape[0], fc2_weight.shape[0]
    pieces = [fc1_bias, qkv_bias, norm_gain, norm_shift, out_bias, fc2_bias]
    marks = [0]
    for piece in pieces:
        marks.append(marks[-1] + piece.shape[0])
    vector = jnp.concatenate(pieces).astype(jnp.float32)
    vector = jnp.pad(vector, (0, -marks[-1] % 128))[None]
    result, grad_tokens, grad_qkv, grad_out, grad_fc1, grad_fc2, sums = layer_all(
        dp // 2,
        ctx,
        tuple(marks),
        tokens[0],
        cotangent[0],
        segments[0],
        qkv_weight,
        fc1_weight,
        fc2_weight,
        out_weight,
        vector,
    )
    sums = sums[:, 0]
    mine, group = lax.axis_index("ctx"), lax.axis_index("dp")
    place = group * ctx + mine
    whole_qkv = jnp.moveaxis(sums[:, : 3 * dl].reshape(ctx, 3, dl), 0, 1).reshape(3 * width)
    g_qkv_b = lax.dynamic_slice_in_dim(whole_qkv, place * 3 * wr, 3 * wr)
    g_fc1_b = lax.dynamic_slice(sums, (mine, 3 * dl + group * fr), (1, fr))[0]
    wide = jnp.sum(sums[:, 3 * dl + fl :], axis=0).reshape(3, width)
    wide = lax.dynamic_slice(wide, (0, place * wr), (3, wr))
    return (
        result[None],
        grad_tokens[None],
        grad_qkv,
        g_qkv_b,
        grad_out,
        wide[0],
        grad_fc1,
        g_fc1_b,
        grad_fc2,
        wide[0],
        wide[1],
        wide[2],
    )


def solution(mesh):
    sizes = (mesh.shape["dp"], mesh.shape["ctx"])
    seq, mat, vec = P("dp", "ctx", None), P(BOTH, None), P(BOTH)

    def spread(*args):
        dp, ctx = sizes
        tokens, qkv_weight, fc2_weight = args[0], args[2], args[8]
        direct = (
            dp == 2 * ctx
            and tokens.shape[0] == 1
            and tokens.shape[1] % 256 == 0
            and qkv_weight.shape[0] % 32 == 0
            and fc2_weight.shape[0] % 128 == 0
        )
        return (local_direct if direct else local)(*sizes, *args)

    placed = (seq, P("dp", None), mat, vec, mat, vec, mat, vec, mat, vec, vec, vec, seq)
    return jax.shard_map(
        spread,
        mesh=mesh,
        in_specs=placed,
        out_specs=(seq, seq, mat, vec, mat, vec, mat, vec, mat, vec, vec, vec),
        check_vma=False,
    )
```

```python
import functools

import jax
import jax.numpy as jnp
import numpy as np
from jax import lax
from jax.experimental import pallas as pl
from jax.experimental.pallas import tpu as pltpu
from jax.sharding import PartitionSpec as P

HEADS = 16
ROT = 32
epsilon = 1e-05
BOTH = ("dp", "ctx")
MESH = pl.DeviceIdType.MESH


def angles(positions, rotary):
    freq_table = 1.0 / 10000.0 ** (jnp.arange(0, rotary, 2, dtype=jnp.float32) / rotary)
    theta = positions.astype(jnp.float32)[:, None] * freq_table[None, :]
    return (jnp.cos(theta)[:, None, :], jnp.sin(theta)[:, None, :])


def rotate(tensor, cosine, sine_table, rotary):
    half_len = rotary // 2
    first_half = tensor[..., :half_len]
    second_half = tensor[..., half_len:rotary]
    return jnp.concatenate(
        [
            first_half * cosine - second_half * sine_table,
            second_half * cosine + first_half * sine_table,
            tensor[..., rotary:],
        ],
        axis=-1,
    )


def contract_rows(left, right):
    return lax.dot_general(
        left, right, (((0,), (0,)), ((), ())), preferred_element_type=jnp.float32
    )


def times_transposed(left, right):
    return lax.dot_general(
        left, right, (((1,), (1,)), ((), ())), preferred_element_type=jnp.float32
    )


def times(left, right):
    return jnp.dot(left, right, preferred_element_type=jnp.float32)


def gelu_tanh(hidden_in):
    return jax.nn.gelu(hidden_in, approximate=True)


def normalise(inputs):
    center = inputs - jnp.mean(inputs, axis=-1, keepdims=True)
    inverse = lax.rsqrt(jnp.mean(center * center, axis=-1, keepdims=True) + epsilon)
    return center * inverse, inverse


def attention(q, k, v, segments, back, cosine, sine):
    length, head_dim = q.shape[1], q.shape[3]
    scale = float(head_dim) ** (-0.5)
    index = jnp.arange(length, dtype=jnp.int32)
    allowed = (segments[:, :, None] == segments[:, None, :]) & (index[None, :] <= index[:, None])[
        None
    ]
    scores = jnp.einsum("sqhd,skhd->shqk", q, k, preferred_element_type=jnp.float32) * scale
    scores = jnp.where(allowed[:, None], scores, -1e30)
    row_max = jnp.max(scores, axis=-1, keepdims=True)
    log_total = row_max + jnp.log(jnp.sum(jnp.exp(scores - row_max), axis=-1, keepdims=True))
    probs = jnp.exp(scores - log_total)
    probs_low = probs.astype(jnp.bfloat16)
    attended = jnp.einsum("shqk,skhd->sqhd", probs_low, v, preferred_element_type=jnp.float32)

    def backward(grad_attended):
        grad_weights = jnp.einsum(
            "sqhd,skhd->shqk", grad_attended, v, preferred_element_type=jnp.float32
        )
        row_dot = jnp.sum(grad_weights * probs, axis=-1, keepdims=True)
        grad_scores = (probs * (grad_weights - row_dot)).astype(jnp.bfloat16)
        grad_q = (
            jnp.einsum("shqk,skhd->sqhd", grad_scores, k, preferred_element_type=jnp.float32)
            * scale
        )
        grad_k = (
            jnp.einsum("shqk,sqhd->skhd", grad_scores, q, preferred_element_type=jnp.float32)
            * scale
        )
        grad_v = jnp.einsum(
            "shqk,sqhd->skhd", probs_low, grad_attended, preferred_element_type=jnp.float32
        )
        return grad_q, grad_k, grad_v

    return attended, backward


def local(
    dp,
    ctx,
    tokens,
    segments,
    qkv_weight,
    qkv_bias,
    out_weight,
    out_bias,
    fc1_weight,
    fc1_bias,
    fc2_weight,
    fc2_bias,
    norm_gain,
    norm_shift,
    cotangent,
):
    f32, b16 = jnp.float32, jnp.bfloat16
    seqs, part, width = tokens.shape
    length = part * ctx
    rows = seqs * length
    ff = fc1_weight.shape[1]
    fl, dl = ff // ctx, width // ctx
    heads = HEADS // ctx
    head_dim = width // HEADS
    wr, fr = qkv_weight.shape[0], fc2_weight.shape[0]
    mine = lax.axis_index("ctx")
    devices = dp * ctx

    pieces = [qkv_bias, fc1_bias, out_bias, fc2_bias, norm_gain, norm_shift]
    marks = [0]
    for piece in pieces:
        marks.append(marks[-1] + piece.shape[0])
    small = lax.all_gather(jnp.concatenate(pieces), BOTH, axis=0)
    parts = [small[:, a:b] for a, b in zip(marks, marks[1:])]
    b_qkv = lax.dynamic_index_in_dim(
        parts[0].reshape(3, ctx, dl), mine, 1, keepdims=False
    ).reshape(3 * dl)
    b_fc1 = lax.dynamic_index_in_dim(
        parts[1].reshape(dp, ctx, fr), mine, 1, keepdims=False
    ).reshape(fl)
    b_out, b_fc2, gain, shift = [p.reshape(width).astype(f32) for p in parts[2:]]

    send_qkv = jnp.moveaxis(qkv_weight.reshape(wr, 3, ctx, dl), 2, 0).reshape(ctx, wr, 3 * dl)
    send_fc1 = jnp.moveaxis(fc1_weight.reshape(wr, dp, ctx, fr), 2, 0).reshape(ctx, wr, fl)
    sent = lax.all_to_all(
        jnp.concatenate([send_qkv, send_fc1], axis=2), "ctx", split_axis=0, concat_axis=0
    )
    out_perm = [(b, (b % dp) * ctx + b // dp) for b in range(devices)]
    out_back = [(j, i) for i, j in out_perm]
    out_piece = lax.ppermute(out_weight, BOTH, out_perm)
    w_qkv = lax.all_gather(sent[:, :, : 3 * dl], "dp", axis=0).reshape(width, 3 * dl)
    w_fc1 = lax.all_gather(sent[:, :, 3 * dl :], "dp", axis=0).reshape(width, fl)
    w_fc2 = lax.all_gather(fc2_weight, "dp", axis=0).reshape(fl, width)
    w_out = lax.all_gather(out_piece, "dp", axis=0).reshape(dl, width)

    tokens_all = lax.all_gather(tokens, "ctx", axis=1, tiled=True)
    cot_all = lax.all_gather(cotangent, "ctx", axis=1, tiled=True)

    positions = jnp.arange(length, dtype=jnp.int32)
    cosine, sine = angles(positions, ROT)

    scaled_all, _ = normalise(tokens_all.astype(f32).reshape(rows, width))
    normed = (scaled_all * gain + shift).astype(b16)
    grad_out = cot_all.reshape(rows, width)

    mixed = times(normed, w_qkv) + b_qkv.astype(f32)
    shape4 = (seqs, length, heads, head_dim)
    q = rotate(mixed[:, :dl].reshape(shape4), cosine, sine, ROT).astype(b16)
    k = rotate(mixed[:, dl : 2 * dl].reshape(shape4), cosine, sine, ROT).astype(b16)
    v = mixed[:, 2 * dl :].astype(b16).reshape(shape4)
    attended, attention_back = attention(q, k, v, segments, None, cosine, sine)
    attended = attended.reshape(rows, dl).astype(b16)

    hidden = times(normed, w_fc1) + b_fc1.astype(f32)
    act, gelu_back = jax.vjp(gelu_tanh, hidden)
    act = act.astype(b16)
    partial = times(attended, w_out) + times(act, w_fc2)
    summed = lax.psum_scatter(
        partial.astype(b16).reshape(seqs, length, width), "ctx", scatter_dimension=1, tiled=True
    )
    result = (tokens.astype(f32) + summed.astype(f32) + (b_out + b_fc2)).astype(b16)

    grad_act = times_transposed(grad_out, w_fc2)
    grad_hidden = gelu_back(grad_act)[0].astype(b16)
    grad_fc2 = contract_rows(act, grad_out)
    grad_fc2 = lax.psum_scatter(grad_fc2.astype(b16), "dp", scatter_dimension=0, tiled=True)
    grad_fc1 = contract_rows(normed, grad_hidden)
    grad_fc1_b = jnp.sum(grad_hidden, axis=0, dtype=f32)
    grad_fc1 = lax.psum_scatter(grad_fc1.astype(b16), "dp", scatter_dimension=0, tiled=True)
    grad_out_w = contract_rows(attended, grad_out)
    grad_out_w = lax.psum_scatter(grad_out_w.astype(b16), "dp", scatter_dimension=0, tiled=True)
    grad_attended = times_transposed(grad_out, w_out).astype(b16).reshape(shape4)
    grad_q, grad_k, grad_v = attention_back(grad_attended)
    grad_mixed = jnp.concatenate(
        [
            rotate(grad_q, cosine, -sine, ROT).reshape(rows, dl),
            rotate(grad_k, cosine, -sine, ROT).reshape(rows, dl),
            grad_v.reshape(rows, dl),
        ],
        axis=1,
    ).astype(b16)
    grad_normed = times_transposed(grad_hidden, w_fc1) + times_transposed(grad_mixed, w_qkv)
    grad_normed = lax.psum_scatter(
        grad_normed.astype(b16).reshape(seqs, length, width), "ctx", scatter_dimension=1, tiled=True
    ).astype(f32)
    grad_qkv = contract_rows(normed, grad_mixed)
    grad_qkv_b = jnp.sum(grad_mixed, axis=0, dtype=f32)
    grad_qkv = lax.psum_scatter(grad_qkv.astype(b16), "dp", scatter_dimension=0, tiled=True)

    back = lax.all_to_all(
        jnp.concatenate([grad_qkv, grad_fc1], axis=1).reshape(ctx, wr, 3 * dl + fl),
        "ctx",
        split_axis=0,
        concat_axis=0,
    ).astype(f32)
    grad_qkv = jnp.moveaxis(back[:, :, : 3 * dl].reshape(ctx, wr, 3, dl), 0, 2).reshape(
        wr, 3 * width
    )
    grad_fc1 = jnp.moveaxis(back[:, :, 3 * dl :].reshape(ctx, wr, dp, fr), 0, 2).reshape(wr, ff)
    grad_out_w = lax.ppermute(grad_out_w, BOTH, out_back).astype(f32)
    grad_fc2 = grad_fc2.astype(f32)

    grad_normed = grad_normed.reshape(seqs, part, width)
    own = tokens.astype(f32)
    cot = cotangent.astype(f32)
    scaled, inverse = normalise(own)
    grad_gain = jnp.sum(grad_normed * scaled, axis=(0, 1))
    grad_shift = jnp.sum(grad_normed, axis=(0, 1))
    grad_scaled = grad_normed * gain
    grad_input = inverse * (
        grad_scaled
        - jnp.mean(grad_scaled, axis=-1, keepdims=True)
        - scaled * jnp.mean(grad_scaled * scaled, axis=-1, keepdims=True)
    )
    grad_tokens = (cot + grad_input).astype(b16)

    wide_qkv_b = lax.dynamic_update_index_in_dim(
        jnp.zeros((3, ctx, dl), f32), grad_qkv_b.reshape(3, dl), mine, 1
    )
    wide_fc1_b = lax.dynamic_update_index_in_dim(
        jnp.zeros((dp, ctx, fr), f32), grad_fc1_b.reshape(dp, fr), mine, 1
    )
    bias_out = jnp.sum(cot, axis=(0, 1))
    sums = jnp.concatenate(
        [
            x.reshape(devices, -1)
            for x in (wide_qkv_b, wide_fc1_b, bias_out, grad_gain, grad_shift)
        ],
        axis=1,
    )
    sums = lax.psum_scatter(sums, BOTH, scatter_dimension=0, tiled=True)[0]
    at = [0, marks[1], marks[2], marks[3], marks[3] + wr, marks[3] + 2 * wr]
    g_qkv_b, g_fc1_b, g_bias, g_gain, g_shift = [sums[a:b] for a, b in zip(at, at[1:])]
    return (
        result,
        grad_tokens,
        grad_qkv,
        g_qkv_b,
        grad_out_w,
        g_bias,
        grad_fc1,
        g_fc1_b,
        grad_fc2,
        g_bias,
        g_gain,
        g_shift,
    )


def dot(left, right, contract):
    return lax.dot_general(
        left, right, ((contract[:1], contract[1:]), ((), ())), preferred_element_type=jnp.float32
    )


NORMAL, RIGHT_T, LEFT_T = (1, 0), (1, 1), (0, 0)


def turn_tables(length, head_dim, lanes):
    half = ROT // 2
    freq = np.float32(1.0) / np.power(
        np.float32(10000.0), np.arange(0, ROT, 2, dtype=np.float32) / np.float32(ROT)
    )
    theta = np.arange(length, dtype=np.float32)[:, None] * freq[None, :]
    cosine, sine = np.cos(theta), np.sin(theta)
    keep = np.ones((length, head_dim), np.float32)
    keep[:, :half] = cosine
    keep[:, half:ROT] = cosine
    ahead = np.zeros((length, head_dim), np.float32)
    ahead[:, :half] = -sine
    behind = np.zeros((length, head_dim), np.float32)
    behind[:, half:ROT] = sine
    return [np.tile(t, (1, lanes // head_dim)) for t in (keep, ahead, behind)]


def turn(x, keep, ahead, behind):
    half, lanes = ROT // 2, x.shape[1]
    return (
        x * keep
        + pltpu.roll(x, lanes - half, axis=1) * ahead
        + pltpu.roll(x, half, axis=1) * behind
    )


DELTAS = (-2, 2, -1, 1)
SLOTS = (0, 0, 1, 2)
PASSED = 4


def layer_kernel(
    nz, nc, marks,
    tok_ref, cot_ref, qkv_ref, fc1_ref, fc2_ref, out_ref, small_ref,
    seg_ref, keep_ref, ahead_ref, behind_ref,
    o_result, o_tokens, o_qkv, o_out, o_fc1, o_fc2, o_sums,
    tok_all, cot_all, w_qkv, w_fc1, w_fc2, w_out, small_all,
    small_rows, vec_d, b_qkv, b_fc1, normed, q_s, k_s, v_s, attended, g_att, act, slope, gmixed,
    acc_q, acc_k, acc_v, acc_a, bias_s, g_hidden,
    give_qkv, give_fc1, give_fc2, give_out, got_qkv, got_fc1, got_fc2, got_out,
    own_qkv, own_fc1, own_fc2, own_out_g, far_qkv, far_fc1, far_fc2, far_out,
    pass_qkv, pass_fc1, pass_fc2, pass_out, log_s, seg_col,
    part_got, part_own, norm_got, norm_own,
    swap_qkv, swap_fc1, swap_out, swapped_qkv, swapped_fc1, swapped_out,
    sums, sums_sib, sums_z,
    ctx_send, ctx_recv, z_send, z_recv, sib_send, sib_recv, loc,
    back_z_send, back_z_recv, back_sib_send, back_sib_recv, back_ctx_send, back_ctx_recv,
):
    f32, b16 = jnp.float32, jnp.bfloat16
    d, c = lax.axis_index("dp"), lax.axis_index("ctx")
    z, k = d // 2, lax.rem(d, 2)
    other = 2 * z + 1 - k
    wr, width = out_ref.shape
    dl = width // nc
    fr = fc2_ref.shape[0]
    nd = 2 * nz
    part = tok_ref.shape[0]
    length = part * nc
    head_dim = width // HEADS
    heads = HEADS // nc
    fl = nd * fr

    def ctx_to(j):
        return lax.rem(c + j, nc)

    def ctx_from(j):
        return lax.rem(c + nc - j, nc)

    def exists(delta):
        return (z + delta >= 0) & (z + delta < nz)

    def plane(delta):
        return 2 * jnp.clip(z + delta, 0, nz - 1) + k

    barrier = pltpu.get_barrier_semaphore()
    for j in range(1, nc):
        pl.semaphore_signal(barrier, inc=1, device_id=(d, ctx_to(j)), device_id_type=MESH)
    for delta in DELTAS:
        @pl.when(exists(delta))
        def _():
            pl.semaphore_signal(barrier, inc=1, device_id=(plane(delta), c), device_id_type=MESH)
    pl.semaphore_signal(barrier, inc=1, device_id=(other, c), device_id_type=MESH)
    planes = jnp.minimum(z, 2) + jnp.minimum(nz - 1 - z, 2)
    pl.semaphore_wait(barrier, nc + planes)

    def remote(src, dst, send, recv, device):
        return pltpu.make_async_remote_copy(
            src_ref=src, dst_ref=dst, send_sem=send, recv_sem=recv,
            device_id=device, device_id_type=MESH,
        )

    def rows(at):
        return pl.ds(pl.multiple_of(at * wr, wr), wr)

    def lanes(at, size):
        return pl.ds(pl.multiple_of(at * size, size), size)

    SMALL, QKV, FC1, TOK, COT, OUT, FC2, FC2B = range(8)
    part_fc2 = fr // 2

    def ctx_pieces(array, to):
        if array == SMALL:
            return [(small_ref, small_all.at[d, c])]
        if array == QKV:
            return [
                (qkv_ref.at[:, lanes(t * nc + to, dl)], w_qkv.at[d, rows(c), pl.ds(t * dl, dl)])
                for t in range(3)
            ]
        if array == FC1:
            return [
                (fc1_ref.at[:, lanes(g * nc + to, fr)], w_fc1.at[d, rows(c), pl.ds(g * fr, fr)])
                for g in range(nd)
            ]
        if array == TOK:
            return [(tok_ref, tok_all.at[c])]
        return [(cot_ref, cot_all.at[c])]

    def ctx_whole(array, sub):
        return {
            SMALL: lambda: small_all.at[d, sub],
            QKV: lambda: w_qkv.at[d, rows(sub), :],
            FC1: lambda: w_fc1.at[d, rows(sub), :],
            TOK: lambda: tok_all.at[sub],
            COT: lambda: cot_all.at[sub],
        }[array]()

    def ctx_start(array):
        for j in range(1, nc):
            for src, dst in ctx_pieces(array, ctx_to(j)):
                remote(src, dst, ctx_send.at[array, j], ctx_recv.at[array, j], (d, ctx_to(j))).start()
        for src, dst in ctx_pieces(array, c):
            pltpu.make_async_copy(src, dst, loc.at[array]).start()

    def ctx_arrive(array, j):
        got = ctx_whole(array, ctx_from(j))
        if j == 0:
            pltpu.make_async_copy(got, got, loc.at[array]).wait()
        else:
            remote(got, got, ctx_send.at[array, j], ctx_recv.at[array, j], (d, ctx_to(j))).wait_recv()

    def ctx_sent(array):
        for j in range(1, nc):
            got = ctx_whole(array, ctx_from(j))
            remote(got, got, ctx_send.at[array, j], ctx_recv.at[array, j], (d, ctx_to(j))).wait_send()

    def ctx_finish(array):
        for j in range(nc):
            ctx_arrive(array, j)

    def block_of(array, at):
        if array in (FC2, FC2B):
            return w_fc2.at[at, pl.ds(0 if array == FC2 else part_fc2, part_fc2), :]
        return {SMALL: small_all, QKV: w_qkv, FC1: w_fc1}[array].at[at]

    near_low, near_high = z == 1, z == nz - 2

    def z_copy(array, n, delta, owner):
        block = block_of(array, owner)
        src = block
        if array in (FC2, FC2B) and n < PASSED:
            src = fc2_ref.at[pl.ds(0 if array == FC2 else part_fc2, part_fc2), :]
        return remote(src, block, z_send.at[array, n], z_recv.at[array, n], (plane(delta), c))

    def z_got(array, n, owner):
        block = block_of(array, owner)
        return remote(block, block, z_send.at[array, n], z_recv.at[array, n], (d, c))

    def sib_copy(array, at):
        block = block_of(array, 2 * at + k)
        return remote(block, block, sib_send.at[array, at], sib_recv.at[array, at], (other, c))

    def z_own(array):
        for n, delta in enumerate(DELTAS):
            @pl.when(exists(delta))
            def _():
                z_copy(array, n, delta, d).start()
        if array not in (FC2, FC2B):
            sib_copy(array, z).start()

    def z_forward(array):
        @pl.when(near_high)
        def _():
            z_got(array, DELTAS.index(2), k).wait_recv()
            z_copy(array, PASSED, 1, k).start()

        @pl.when(near_low)
        def _():
            z_got(array, DELTAS.index(-2), d + 4).wait_recv()
            z_copy(array, PASSED, -1, d + 4).start()

    def z_arrive(array):
        for n, delta in enumerate(DELTAS):
            done = near_high if delta == 2 else near_low if delta == -2 else None
            wanted = exists(-delta) if done is None else exists(-delta) & jnp.logical_not(done)

            @pl.when(wanted)
            def _():
                z_got(array, n, plane(-delta)).wait_recv()

        @pl.when(z == 0)
        def _():
            z_got(array, PASSED, 2 * (nz - 1) + k).wait_recv()

        @pl.when(z == nz - 1)
        def _():
            z_got(array, PASSED, k).wait_recv()

        for at in range(nz):
            if array in (FC2, FC2B):
                sib_copy(array, at).start()
            else:
                @pl.when(z != at)
                def _():
                    sib_copy(array, at).start()

    def z_finish(array):
        for at in range(nz):
            block = block_of(array, 2 * at + 1 - k)
            remote(block, block, sib_send.at[array, at], sib_recv.at[array, at], (other, c)).wait_recv()

    def z_sent(array):
        for n, delta in enumerate(DELTAS):
            @pl.when(exists(delta))
            def _():
                z_copy(array, n, delta, d).wait_send()

        @pl.when(near_high | near_low)
        def _():
            z_copy(array, PASSED, 1, k).wait_send()

        for at in range(nz):
            sib_copy(array, at).wait_send()

    def out_copy(j, to, sub):
        return remote(out_ref, w_out.at[k, rows(sub), :], ctx_send.at[OUT, j], ctx_recv.at[OUT, j], (d, to))

    half = w_out.at[k]

    def out_z(n, delta):
        return remote(half, half, z_send.at[OUT, n], z_recv.at[OUT, n], (plane(delta), c))

    def out_sib(which):
        piece = w_out.at[which]
        return remote(piece, piece, sib_send.at[OUT, 0], sib_recv.at[OUT, 0], (other, c))

    ctx_start(SMALL)
    ctx_start(QKV)
    z_own(FC2)
    own_out = pltpu.make_async_copy(out_ref, w_out.at[k, rows(c), :], loc.at[OUT])

    @pl.when(z == c)
    def _():
        own_out.start()

    for j in range(1, nc):
        @pl.when(ctx_to(j) == z)
        def _():
            out_copy(j, z, c).start()

    ctx_start(FC1)
    ctx_start(TOK)
    copy_fc2 = pltpu.make_async_copy(fc2_ref, w_fc2.at[d], loc.at[FC2])
    copy_fc2.start()

    ctx_finish(SMALL)
    z_own(SMALL)
    ctx_finish(QKV)
    z_own(QKV)

    @pl.when(z == c)
    def _():
        for j in range(1, nc):
            out_copy(j, z, ctx_from(j)).wait_recv()
        own_out.wait()
        for n, delta in enumerate(DELTAS):
            @pl.when(exists(delta))
            def _():
                out_z(n, delta).start()
        out_sib(k).start()

    ctx_finish(FC1)
    ctx_start(COT)
    z_forward(SMALL)
    z_arrive(SMALL)
    z_forward(FC2)
    z_forward(QKV)
    z_own(FC1)
    z_finish(SMALL)

    def collect(p, carry):
        small_rows[pl.ds(p, 1), :] = small_all[p // nc, lax.rem(p, nc)]
        return carry

    lax.fori_loop(0, nd * nc, collect, 0)
    table = small_rows[...]
    pack = table.shape[1]

    def vector(mark, size, first, count):
        entry = lax.broadcasted_iota(jnp.int32, (1, count), 1).astype(f32) + first
        owner = jnp.floor((entry + 0.5) * (1.0 / size))
        lane = entry - owner * size + mark
        pick = lax.broadcasted_iota(jnp.int32, (pack, count), 0).astype(f32) == lane
        found = dot(table.astype(b16), jnp.where(pick, 1.0, 0.0).astype(b16), NORMAL)
        here = lax.broadcasted_iota(jnp.int32, (nd * nc, count), 0).astype(f32) == owner
        return jnp.sum(jnp.where(here, found, 0.0), axis=0, keepdims=True)

    for i in range(2):
        vec_d[pl.ds(i, 1), :] = vector(marks[2 + i], wr, 0.0, width)
    vec_d[2:3, :] = vector(marks[4], wr, 0.0, width) + vector(marks[5], wr, 0.0, width)
    for t in range(3):
        b_qkv[:, pl.ds(t * dl, dl)] = vector(marks[1], 3 * wr, (t * width + c * dl).astype(f32), dl)
    for g in range(nd):
        b_fc1[:, pl.ds(g * fr, fr)] = small_all[g, c][:, :fr]

    z_arrive(QKV)
    z_finish(QKV)

    seg_col[...] = jnp.broadcast_to(seg_ref[...].astype(f32), (128, length)).T

    chunk = 32

    def block_rows(b):
        return pl.ds(pl.multiple_of(b * part, part), part)

    def normalise_block(b):
        def step(i, carry):
            at = pl.multiple_of(i * chunk, chunk)
            x = tok_all[b, pl.ds(at, chunk), :].astype(f32)
            x = x - jnp.mean(x, axis=-1, keepdims=True)
            x = x * lax.rsqrt(jnp.mean(x * x, axis=-1, keepdims=True) + epsilon)
            normed[pl.ds(pl.multiple_of(b * part, part) + at, chunk), :] = (
                x * vec_d[0:1, :] + vec_d[1:2, :]
            ).astype(b16)
            return carry

        lax.fori_loop(0, part // chunk, step, 0)

    def qkv_block(b):
        at = block_rows(b)
        x = normed[at, :]
        keep = jnp.tile(keep_ref[at, :], (1, dl // keep_ref.shape[1]))
        ahead = jnp.tile(ahead_ref[at, :], (1, dl // keep_ref.shape[1]))
        behind = jnp.tile(behind_ref[at, :], (1, dl // keep_ref.shape[1]))
        for t, to in enumerate((q_s, k_s, v_s)):
            w = w_qkv[:, :, pl.ds(t * dl, dl)].reshape(width, dl)
            y = dot(x, w, NORMAL) + b_qkv[:, pl.ds(t * dl, dl)]
            if t < 2:
                y = turn(y, keep, ahead, behind)
            to[at, :] = y.astype(b16)

    for j in range(nc):
        ctx_arrive(TOK, j)
        normalise_block(ctx_from(j))
        qkv_block(ctx_from(j))

    z_forward(FC1)
    z_own(FC2B)

    tile = 256
    reach = 512 // tile
    scale = float(head_dim) ** (-0.5)

    def spans(i):
        first = max(0, i - reach) * tile
        count = (i + 1) * tile - first
        return pl.ds(i * tile, tile), pl.ds(first, count), count

    def mask(i):
        at, to, count = spans(i)
        same = seg_col[at, :1] == seg_ref[:1, to].astype(f32)
        row = lax.broadcasted_iota(jnp.int32, (tile, count), 0) + (tile * i - to.start)
        col = lax.broadcasted_iota(jnp.int32, (tile, count), 1)
        bias_s[:, :count] = jnp.where(same & (col <= row), 0.0, -1e30)

    def only_head(h):
        lane = lax.broadcasted_iota(jnp.int32, (1, dl), 1)
        return jnp.where((lane >= h * head_dim) & (lane < (h + 1) * head_dim), 1.0, 0.0)

    for i in range(length // tile):
        at, to, count = spans(i)
        mask(i)
        acc_a[...] = jnp.zeros_like(acc_a)

        def forward_step(h, carry):
            only = only_head(h)
            s = dot(q_s[at, :] * only.astype(b16), k_s[to, :], RIGHT_T) * scale + bias_s[:, :count]
            top = jnp.max(s, axis=-1, keepdims=True)
            e = jnp.exp(s - top)
            sum_e = jnp.sum(e, axis=-1, keepdims=True)
            log_s[h, at, :] = top + jnp.log(sum_e)
            p_low = (e * (1.0 / sum_e)).astype(b16)
            acc_a[...] += dot(p_low, v_s[to, :], NORMAL) * only
            return carry

        lax.fori_loop(0, heads, forward_step, 0, unroll=True)
        attended[at, :] = acc_a[...].astype(b16)

    z_arrive(FC1)
    z_finish(FC1)

    def hidden_block(b, carry):
        at = block_rows(b)
        x = normed[at, :]
        for g in range(0, fl, 256):
            w = w_fc1[:, :, pl.ds(g, 256)].reshape(width, 256)
            h = dot(x, w, NORMAL) + b_fc1[:, pl.ds(g, 256)]
            s = h * h
            t = jnp.tanh(h * (0.7978845608028654 + (0.7978845608028654 * 0.044715) * s))
            half_t = 0.5 + 0.5 * t
            act[at, pl.ds(g, 256)] = (h * half_t).astype(b16)
            slope[at, pl.ds(g, 256)] = half_t + 0.5 * h * (1.0 - t * t) * (
                0.7978845608028654 + (3 * 0.7978845608028654 * 0.044715) * s
            )
        return carry

    lax.fori_loop(0, nc, hidden_block, 0)

    z_forward(FC2B)
    ctx_finish(COT)

    gives = {QKV: give_qkv, FC1: give_fc1, FC2: give_fc2, OUT: give_out}
    gots = {QKV: got_qkv, FC1: got_fc1, FC2: got_fc2, OUT: got_out}
    owns = {QKV: own_qkv, FC1: own_fc1, FC2: own_fc2, OUT: own_out_g}
    fars = {QKV: far_qkv, FC1: far_fc1, FC2: far_fc2, OUT: far_out}
    passes = {QKV: pass_qkv, FC1: pass_fc1, FC2: pass_fc2, OUT: pass_out}

    def cotangents():
        return cot_all[...].reshape(length, width)

    def weight_gradient(array, left, right):
        give, own = gives[array], owns[array]
        size = give.shape[1]

        def step(i, carry):
            both = dot(left[:, lanes(i, 2 * size)], right(), LEFT_T)
            low, high = both[:size], both[size:]
            own[i] = jnp.where(k == 0, low, high)
            give[i] = jnp.where(k == 0, high, low).astype(b16)
            return carry

        lax.fori_loop(0, give.shape[0], step, 0)
        to_sibling(array).start()

    def to_sibling(array):
        return remote(
            gives[array], gots[array], back_sib_send.at[array], back_sib_recv.at[array], (other, c)
        )

    def to_owner(array, n, delta):
        block = gives[array].at[0 if array == OUT else jnp.clip(z + delta, 0, nz - 1)]
        return remote(
            block, fars[array].at[SLOTS[n]], back_z_send.at[array, n], back_z_recv.at[array, n], (plane(delta), c)
        )

    def to_pass(array, delta):
        block = gives[array].at[0 if array == OUT else jnp.clip(z + 3 * delta, 0, nz - 1)]
        return remote(
            block, passes[array], back_z_send.at[array, PASSED], back_z_recv.at[array, PASSED], (plane(delta), c)
        )

    def wanted(array, at):
        return (at == c) if array == OUT else True

    def mix(array, at):
        i = 0 if array == OUT else at
        gives[array][i] = (owns[array][i] + gots[array][i].astype(f32)).astype(b16)

    def add_sibling(array):
        to_sibling(array).wait()
        for delta in (-1, 1):
            far = z + 3 * delta

            @pl.when((z == (nz - 1 if delta < 0 else 0)) & wanted(array, far))
            def _():
                mix(array, far)
                to_pass(array, delta).start()
        for n, delta in enumerate(DELTAS):
            hold = {-2: near_high, 2: near_low}.get(delta)
            go = exists(delta) & wanted(array, z + delta)
            if hold is not None:
                go = go & jnp.logical_not(hold)

            @pl.when(go)
            def _():
                mix(array, z + delta)
                to_owner(array, n, delta).start()

    def pass_back(array):
        for near, delta in ((near_high, -2), (near_low, 2)):
            @pl.when(near & wanted(array, z + delta))
            def _():
                to_pass(array, delta).wait_recv()
                i = 0 if array == OUT else z + delta
                gives[array][i] = (
                    owns[array][i] + gots[array][i].astype(f32) + passes[array][...].astype(f32)
                ).astype(b16)
                to_owner(array, DELTAS.index(delta), delta).start()

    def gather_total(array):
        at = 0 if array == OUT else z
        own = owns[array]
        own[at] = own[at] + gots[array][at].astype(f32)
        for n, delta in enumerate(DELTAS):
            @pl.when(exists(-delta))
            def _():
                to_owner(array, n, delta).wait_recv()
                own[at] = own[at] + fars[array][SLOTS[n]].astype(f32)

    def owner_sent(array):
        for n, delta in enumerate(DELTAS):
            @pl.when(exists(delta) & wanted(array, z + delta))
            def _():
                to_owner(array, n, delta).wait_send()
        for delta in (-1, 1):
            @pl.when((z == (nz - 1 if delta < 0 else 0)) & wanted(array, z + 3 * delta))
            def _():
                to_pass(array, delta).wait_send()

    PART, NORM, SUMS = TOK, COT, SMALL

    def over_ctx(array, src, dst, j, to):
        return remote(src, dst, back_ctx_send.at[array, j], back_ctx_recv.at[array, j], (d, to))

    weight_gradient(FC2, act, cotangents)

    for n, delta in enumerate(DELTAS):
        @pl.when(z - delta == c)
        def _():
            out_z(n, delta).wait_recv()
            out_sib(k).start()

    for at, near, delta in ((0, near_high, 1), (nz - 1, near_low, -1)):
        @pl.when((c == at) & near)
        def _():
            out_z(PASSED, delta).start()

        @pl.when((c == at) & (z == nz - 1 - at))
        def _():
            out_z(PASSED, delta).wait_recv()
            out_sib(k).start()
    out_sib(1 - k).wait_recv()

    w_o = w_out[...].reshape(dl, width)

    def g_att_block(b, carry):
        g_att[block_rows(b), :] = dot(cot_all[b], w_o, RIGHT_T).astype(b16)
        return carry

    lax.fori_loop(0, nc, g_att_block, 0)
    copy_fc2.wait()
    z_arrive(FC2)
    z_arrive(FC2B)
    add_sibling(FC2)
    z_finish(FC2)
    z_finish(FC2B)

    def result_term(b):
        at = block_rows(b)
        return dot(attended[at, :], w_out[...].reshape(dl, width), NORMAL) + dot(
            act[at, :], w_fc2[...].reshape(fl, width), NORMAL
        )

    for j in range(1, nc):
        b = ctx_to(j)
        tok_all[b] = result_term(b).astype(b16)
        over_ctx(PART, tok_all.at[b], part_got.at[j - 1], j, b).start()
    part_own[...] = result_term(c)

    acc_k[...] = jnp.zeros_like(acc_k)
    acc_v[...] = jnp.zeros_like(acc_v)
    wide = (1, dl // keep_ref.shape[1])
    for i in range(length // tile):
        at, to, count = spans(i)
        mask(i)
        acc_q[...] = jnp.zeros_like(acc_q)

        def backward_step(h, carry):
            only = only_head(h)
            only_low = only.astype(b16)
            qh = q_s[at, :] * only_low
            gh = g_att[at, :] * only_low
            keys, values = k_s[to, :], v_s[to, :]
            p = jnp.exp(dot(qh, keys, RIGHT_T) * scale + bias_s[:, :count] - log_s[h, at, :])
            gw = dot(gh, values, RIGHT_T)
            gs = (p * (gw - jnp.sum(gw * p, axis=-1, keepdims=True))).astype(b16)
            acc_q[...] += dot(gs, keys, NORMAL) * only
            acc_k[to, :] += dot(gs, qh, LEFT_T)
            acc_v[to, :] += dot(p.astype(b16), gh, LEFT_T)
            return carry

        lax.fori_loop(0, heads, backward_step, 0, unroll=True)
        gmixed[at, pl.ds(0, dl)] = turn(
            acc_q[...] * scale,
            jnp.tile(keep_ref[at, :], wide),
            -jnp.tile(ahead_ref[at, :], wide),
            -jnp.tile(behind_ref[at, :], wide),
        ).astype(b16)

    def finish_block(b, carry):
        at = block_rows(b)
        gmixed[at, pl.ds(dl, dl)] = turn(
            acc_k[at, :] * scale,
            jnp.tile(keep_ref[at, :], wide),
            -jnp.tile(ahead_ref[at, :], wide),
            -jnp.tile(behind_ref[at, :], wide),
        ).astype(b16)
        gmixed[at, pl.ds(2 * dl, dl)] = acc_v[at, :].astype(b16)
        return carry

    lax.fori_loop(0, nc, finish_block, 0)

    pass_back(FC2)
    weight_gradient(QKV, normed, lambda: gmixed[...])
    weight_gradient(OUT, attended, cotangents)
    add_sibling(QKV)
    add_sibling(OUT)

    def hidden_gradient(b, carry):
        at = block_rows(b)
        g = cot_all[b]
        for i in range(nd):
            to = pl.ds(i * fr, fr)
            g_hidden[at, to] = (dot(g, w_fc2[i], RIGHT_T) * slope[at, to]).astype(b16)
        return carry

    lax.fori_loop(0, nc, hidden_gradient, 0)

    def normed_term(b):
        at = block_rows(b)
        return dot(g_hidden[at, :], w_fc1[...].reshape(width, fl), RIGHT_T) + dot(
            gmixed[at, :], w_qkv[...].reshape(width, 3 * dl), RIGHT_T
        )

    for j in range(1, nc):
        b = ctx_to(j)
        cot_all[b] = normed_term(b).astype(b16)
        over_ctx(NORM, cot_all.at[b], norm_got.at[j - 1], j, b).start()
    norm_own[...] = normed_term(c)

    ones = jnp.ones((8, length), b16)
    sums[0, :, pl.ds(0, 3 * dl)] = dot(ones, gmixed[...], NORMAL)[:1]
    sums[0, :, pl.ds(3 * dl, fl)] = dot(ones, g_hidden[...], NORMAL)[:1]
    at_sum = 3 * dl + fl
    sums[0, :, pl.ds(at_sum, width)] = dot(ones[:, :part], cot_all[c], NORMAL)[:1]

    weight_gradient(FC1, normed, lambda: g_hidden[...])
    add_sibling(FC1)
    for j in range(1, nc):
        over_ctx(PART, tok_all.at[c], part_got.at[j - 1], j, c).wait_recv()

    def result_step(i, carry):
        at = pl.ds(pl.multiple_of(i * chunk, chunk), chunk)
        y = tok_all[c, at, :].astype(f32) + part_own[at, :] + vec_d[2:3, :]
        for j in range(1, nc):
            y = y + part_got[j - 1, at, :].astype(f32)
        o_result[at, :] = y.astype(b16)
        return carry

    lax.fori_loop(0, part // chunk, result_step, 0)

    pass_back(QKV)
    pass_back(OUT)
    gather_total(FC2)
    o_fc2[...] = own_fc2[z]

    swaps = {QKV: (swap_qkv, swapped_qkv), FC1: (swap_fc1, swapped_fc1)}

    def place(array, source, x):
        if array == QKV:
            for t in range(3):
                o_qkv[:, lanes(t * nc + source, dl)] = x[:, t * dl : (t + 1) * dl]
        else:
            for g in range(nd):
                o_fc1[:, lanes(g * nc + source, fr)] = x[:, g * fr : (g + 1) * fr]

    def swap_start(array):
        gather_total(array)
        src, dst = swaps[array]
        own = owns[array]
        for j in range(1, nc):
            src[j - 1] = own[z, rows(ctx_to(j)), :].astype(b16)
            over_ctx(array, src.at[j - 1], dst.at[j - 1], j, ctx_to(j)).start()
        place(array, c, own[z, rows(c), :])

    def swap_finish(array):
        src, dst = swaps[array]
        for j in range(1, nc):
            over_ctx(array, src.at[j - 1], dst.at[j - 1], j, ctx_to(j)).wait_recv()
            place(array, ctx_from(j), dst[j - 1].astype(f32))

    swap_start(QKV)

    @pl.when(z == c)
    def _():
        gather_total(OUT)
        for j in range(1, nc):
            swap_out[j - 1] = own_out_g[0, rows(ctx_to(j)), :].astype(b16)
            over_ctx(OUT, swap_out.at[j - 1], swapped_out.at[0], j, ctx_to(j)).start()
        o_out[...] = own_out_g[0, rows(c), :]

    pass_back(FC1)
    for j in range(1, nc):
        over_ctx(NORM, cot_all.at[c], norm_got.at[j - 1], j, c).wait_recv()

    def norm_step(i, carry):
        gain_sum, shift_sum = carry
        at = pl.ds(pl.multiple_of(i * chunk, chunk), chunk)
        x = tok_all[c, at, :].astype(f32)
        x = x - jnp.mean(x, axis=-1, keepdims=True)
        inverse = lax.rsqrt(jnp.mean(x * x, axis=-1, keepdims=True) + epsilon)
        x = x * inverse
        g = norm_own[at, :]
        for j in range(1, nc):
            g = g + norm_got[j - 1, at, :].astype(f32)
        v = g * vec_d[0:1, :]
        y = inverse * (
            v - jnp.mean(v, axis=-1, keepdims=True) - x * jnp.mean(v * x, axis=-1, keepdims=True)
        )
        o_tokens[at, :] = (cot_all[c, at, :].astype(f32) + y).astype(b16)
        return (
            gain_sum + jnp.sum(g * x, axis=0, keepdims=True),
            shift_sum + jnp.sum(g, axis=0, keepdims=True),
        )

    zero = jnp.zeros((1, width), f32)
    gain_sum, shift_sum = lax.fori_loop(0, part // chunk, norm_step, (zero, zero))
    sums[0, :, pl.ds(at_sum + width, width)] = gain_sum
    sums[0, :, pl.ds(at_sum + 2 * width, width)] = shift_sum

    sum_sib = remote(sums.at[0], sums_sib.at[0], back_sib_send.at[SUMS], back_sib_recv.at[SUMS], (other, c))
    sum_sib.start()
    sum_sib.wait()
    sums[1] = sums[0] + sums_sib[0]
    for n, partner in enumerate((z + 1 - 2 * lax.rem(z, 2), lax.rem(z + 2, nz))):
        trade = remote(
            sums.at[n + 1], sums_z.at[n], back_z_send.at[SUMS, n], back_z_recv.at[SUMS, n], (2 * partner + k, c)
        )
        trade.start()
        trade.wait()
        sums[n + 2] = sums[n + 1] + sums_z[n]
    sums_mine = sums.at[3]
    o_sums[c] = sums[3]
    for j in range(1, nc):
        over_ctx(SUMS, sums_mine, o_sums.at[c], j, ctx_to(j)).start()

    swap_finish(QKV)
    for j in range(1, nc):
        @pl.when(ctx_from(j) == z)
        def _():
            over_ctx(OUT, swap_out.at[0], swapped_out.at[0], j, ctx_to(j)).wait_recv()
            o_out[...] = swapped_out[0].astype(f32)

    swap_start(FC1)
    for j in range(1, nc):
        over_ctx(SUMS, sums_mine, o_sums.at[ctx_from(j)], j, ctx_to(j)).wait_recv()
    swap_finish(FC1)

    for array in (SMALL, QKV, FC1, FC2, FC2B):
        z_sent(array)
    for array in (SMALL, QKV, FC1, TOK, COT):
        ctx_sent(array)
    for j in range(1, nc):
        @pl.when(ctx_to(j) == z)
        def _():
            out_copy(j, z, c).wait_send()

    @pl.when(z == c)
    def _():
        for n, delta in enumerate(DELTAS):
            @pl.when(exists(delta))
            def _():
                out_z(n, delta).wait_send()

    @pl.when(((c == 0) & near_high) | ((c == nz - 1) & near_low))
    def _():
        out_z(PASSED, 1).wait_send()

    out_sib(k).wait_send()
    for array in (QKV, OUT, FC1, FC2):
        owner_sent(array)
    for j in range(1, nc):
        over_ctx(PART, tok_all.at[c], part_got.at[j - 1], j, c).wait_send()
        over_ctx(NORM, cot_all.at[c], norm_got.at[j - 1], j, c).wait_send()
        over_ctx(SUMS, sums_mine, o_sums.at[c], j, ctx_to(j)).wait_send()
        for array in (QKV, FC1):
            over_ctx(array, swaps[array][0].at[j - 1], swaps[array][1].at[j - 1], j, c).wait_send()

    @pl.when(z == c)
    def _():
        for j in range(1, nc):
            over_ctx(OUT, swap_out.at[j - 1], swapped_out.at[0], j, ctx_to(j)).wait_send()


def layer_all(nz, nc, marks, tokens, cotangent, segments, qkv_weight, fc1_weight, fc2_weight, out_weight, small):
    part, width = tokens.shape
    wr, fr = qkv_weight.shape[0], fc2_weight.shape[0]
    nd, dl = 2 * nz, width // nc
    length, fl = part * nc, 2 * nz * fr
    cw = nc * wr
    f32, b16 = jnp.float32, jnp.bfloat16
    tables = [jnp.asarray(t) for t in turn_tables(length, width // HEADS, 128)]
    pack = small.shape[1]
    total = 3 * dl + fl + 3 * width
    tile, window = 256, 768
    results = [
        ((part, width), b16),
        ((part, width), b16),
        ((wr, 3 * width), f32),
        ((wr, width), f32),
        ((wr, fl * nc), f32),
        ((fr, width), f32),
        ((nc, 1, total), f32),
    ]
    work = [
        ((nc, part, width), b16),
        ((nc, part, width), b16),
        ((nd, cw, 3 * dl), b16),
        ((nd, cw, fl), b16),
        ((nd, fr, width), b16),
        ((2, cw, width), b16),
        ((nd, nc, 1, pack), f32),
        ((nd * nc, pack), f32),
        ((8, width), f32),
        ((1, 3 * dl), f32),
        ((1, fl), f32),
        ((length, width), b16),
        ((length, dl), b16),
        ((length, dl), b16),
        ((length, dl), b16),
        ((length, dl), b16),
        ((length, dl), b16),
        ((length, fl), b16),
        ((length, fl), f32),
        ((length, 3 * dl), b16),
        ((tile, dl), f32),
        ((length, dl), f32),
        ((length, dl), f32),
        ((tile, dl), f32),
        ((tile, window), f32),
        ((length, fl), b16),
    ]
    grads = [(nz, cw, 3 * dl), (nz, cw, fl), (nz, fr, width), (1, cw, width)]
    fars = [(3,) + g[1:] for g in grads]
    work += [(g, b16) for g in grads] + [(g, b16) for g in grads] + [(g, f32) for g in grads]
    work += [(g, b16) for g in fars] + [(g[1:], b16) for g in grads]
    work += [((HEADS // nc, length, 1), f32), ((length, 128), f32)]
    work += [((nc - 1, part, width), b16), ((part, width), f32)] * 2
    work += [((nc - 1, wr, n), b16) for n in (3 * dl, fl, width)]
    work += [((nc - 1, wr, n), b16) for n in (3 * dl, fl)] + [((1, wr, width), b16)]
    work += [((n, 1, total), f32) for n in (4, 1, 2)]
    dma = pltpu.SemaphoreType.DMA
    sems = [(7, nc), (7, nc), (8, 5), (8, 5), (8, nz), (8, nz), (7,)]
    sems += [(7, 5), (7, 5), (7,), (7,), (7, nc), (7, nc)]
    hbm, vmem = pl.BlockSpec(memory_space=pl.ANY), pl.BlockSpec(memory_space=pltpu.VMEM)
    return pl.pallas_call(
        functools.partial(layer_kernel, nz, nc, marks),
        out_shape=[jax.ShapeDtypeStruct(s, t) for s, t in results],
        in_specs=[hbm] * 7 + [vmem] * 4,
        out_specs=[vmem] * len(results),
        scratch_shapes=[pltpu.VMEM(s, t) for s, t in work] + [dma(s) for s in sems],
        compiler_params=pltpu.CompilerParams(
            collective_id=0, has_side_effects=True, vmem_limit_bytes=62 * 2**20
        ),
        name="layer",
    )(tokens, cotangent, qkv_weight, fc1_weight, fc2_weight, out_weight, small, segments.reshape(1, length), *tables)


def finish_kernel(
    dl, fr, wr,
    result, tokens, qkv, out, fc1, fc2, sums,
    o_result, o_tokens, o_qkv, o_out, o_fc1, o_fc2, o_qkv_b, o_out_b, o_fc1_b, o_fc2_b, o_gain, o_shift,
    row,
):
    moves = [(result, o_result), (tokens, o_tokens), (qkv, o_qkv), (out, o_out), (fc1, o_fc1), (fc2, o_fc2)]
    for source, to in moves:
        to[...] = source[...]
    nc, total = sums.shape[0], sums.shape[2]
    mine, group = lax.axis_index("ctx"), lax.axis_index("dp")
    place = group * nc + mine
    width = dl * nc
    fl = total - 3 * dl - 3 * width

    def piece(values, size):
        length = values.shape[1]
        return pltpu.roll(values, length - place * size, axis=1)[0, :size]

    for t in range(3):
        for rank in range(nc):
            row[:, pl.ds(t * width + rank * dl, dl)] = sums[rank][:, t * dl : (t + 1) * dl]
    o_qkv_b[...] = piece(row[...], 3 * wr)
    at = pl.ds(pl.multiple_of(3 * dl + group * fr, fr), fr)
    o_fc1_b[...] = sums[mine, :, at][0]
    for n, outs in enumerate(((o_out_b, o_fc2_b), (o_gain,), (o_shift,))):
        first = 3 * dl + fl + n * width
        whole = sums[0][:, first : first + width]
        for rank in range(1, nc):
            whole = whole + sums[rank][:, first : first + width]
        for to in outs:
            to[...] = piece(whole, wr)


def finish_all(dl, fr, wr, arrays):
    f32 = jnp.float32
    vmem = pl.BlockSpec(memory_space=pltpu.VMEM)
    vectors = [3 * wr, wr, fr, wr, wr, wr]
    nc = arrays[6].shape[0]
    return pl.pallas_call(
        functools.partial(finish_kernel, dl, fr, wr),
        out_shape=[jax.ShapeDtypeStruct(a.shape, a.dtype) for a in arrays[:6]]
        + [jax.ShapeDtypeStruct((n,), f32) for n in vectors],
        in_specs=[vmem] * 7,
        out_specs=[vmem] * 12,
        scratch_shapes=[pltpu.VMEM((1, 3 * dl * nc), f32)],
        name="finish",
    )(*arrays)


def local_direct(
    dp,
    ctx,
    tokens,
    segments,
    qkv_weight,
    qkv_bias,
    out_weight,
    out_bias,
    fc1_weight,
    fc1_bias,
    fc2_weight,
    fc2_bias,
    norm_gain,
    norm_shift,
    cotangent,
):
    width = tokens.shape[-1]
    dl, fl = width // ctx, fc1_weight.shape[1] // ctx
    wr, fr = qkv_weight.shape[0], fc2_weight.shape[0]
    pieces = [fc1_bias, qkv_bias, norm_gain, norm_shift, out_bias, fc2_bias]
    marks = [0]
    for piece in pieces:
        marks.append(marks[-1] + piece.shape[0])
    vector = jnp.concatenate(pieces).astype(jnp.float32)
    vector = jnp.pad(vector, (0, -marks[-1] % 128))[None]
    arrays = layer_all(
        dp // 2,
        ctx,
        tuple(marks),
        tokens[0],
        cotangent[0],
        segments[0],
        qkv_weight,
        fc1_weight,
        fc2_weight,
        out_weight,
        vector,
    )
    result, grad_tokens, *rest = finish_all(dl, fr, wr, arrays)
    grad_qkv, grad_out, grad_fc1, grad_fc2, g_qkv_b, g_out_b, g_fc1_b, g_fc2_b, g_gain, g_shift = rest
    return (
        result[None],
        grad_tokens[None],
        grad_qkv,
        g_qkv_b,
        grad_out,
        g_out_b,
        grad_fc1,
        g_fc1_b,
        grad_fc2,
        g_fc2_b,
        g_gain,
        g_shift,
    )


def solution(mesh):
    sizes = (mesh.shape["dp"], mesh.shape["ctx"])
    seq, mat, vec = P("dp", "ctx", None), P(BOTH, None), P(BOTH)

    def spread(*args):
        dp, ctx = sizes
        tokens, qkv_weight, fc2_weight = args[0], args[2], args[8]
        direct = (
            dp == 8
            and ctx == 4
            and tokens.shape[0] == 1
            and tokens.shape[1] % 256 == 0
            and qkv_weight.shape[0] % 32 == 0
            and fc2_weight.shape[0] % 128 == 0
        )
        return (local_direct if direct else local)(*sizes, *args)

    placed = (seq, P("dp", None), mat, vec, mat, vec, mat, vec, mat, vec, vec, vec, seq)
    return jax.shard_map(
        spread,
        mesh=mesh,
        in_specs=placed,
        out_specs=(seq, seq, mat, vec, mat, vec, mat, vec, mat, vec, vec, vec),
        check_vma=False,
    )
```

```python
import functools

import jax
import jax.numpy as jnp
import numpy as np
from jax import lax
from jax.experimental import pallas as pl
from jax.experimental.pallas import tpu as pltpu
from jax.sharding import PartitionSpec as P

HEADS = 16
ROT = 32
epsilon = 1e-05
BOTH = ("dp", "ctx")
MESH = pl.DeviceIdType.MESH


def angles(positions, rotary):
    freq_table = 1.0 / 10000.0 ** (jnp.arange(0, rotary, 2, dtype=jnp.float32) / rotary)
    theta = positions.astype(jnp.float32)[:, None] * freq_table[None, :]
    return (jnp.cos(theta)[:, None, :], jnp.sin(theta)[:, None, :])


def rotate(tensor, cosine, sine_table, rotary):
    half_len = rotary // 2
    first_half = tensor[..., :half_len]
    second_half = tensor[..., half_len:rotary]
    return jnp.concatenate(
        [
            first_half * cosine - second_half * sine_table,
            second_half * cosine + first_half * sine_table,
            tensor[..., rotary:],
        ],
        axis=-1,
    )


def contract_rows(left, right):
    return lax.dot_general(
        left, right, (((0,), (0,)), ((), ())), preferred_element_type=jnp.float32
    )


def times_transposed(left, right):
    return lax.dot_general(
        left, right, (((1,), (1,)), ((), ())), preferred_element_type=jnp.float32
    )


def times(left, right):
    return jnp.dot(left, right, preferred_element_type=jnp.float32)


def gelu_tanh(hidden_in):
    return jax.nn.gelu(hidden_in, approximate=True)


def normalise(inputs):
    center = inputs - jnp.mean(inputs, axis=-1, keepdims=True)
    inverse = lax.rsqrt(jnp.mean(center * center, axis=-1, keepdims=True) + epsilon)
    return center * inverse, inverse


def attention(q, k, v, segments, back, cosine, sine):
    length, head_dim = q.shape[1], q.shape[3]
    scale = float(head_dim) ** (-0.5)
    index = jnp.arange(length, dtype=jnp.int32)
    allowed = (segments[:, :, None] == segments[:, None, :]) & (index[None, :] <= index[:, None])[
        None
    ]
    scores = jnp.einsum("sqhd,skhd->shqk", q, k, preferred_element_type=jnp.float32) * scale
    scores = jnp.where(allowed[:, None], scores, -1e30)
    row_max = jnp.max(scores, axis=-1, keepdims=True)
    log_total = row_max + jnp.log(jnp.sum(jnp.exp(scores - row_max), axis=-1, keepdims=True))
    probs = jnp.exp(scores - log_total)
    probs_low = probs.astype(jnp.bfloat16)
    attended = jnp.einsum("shqk,skhd->sqhd", probs_low, v, preferred_element_type=jnp.float32)

    def backward(grad_attended):
        grad_weights = jnp.einsum(
            "sqhd,skhd->shqk", grad_attended, v, preferred_element_type=jnp.float32
        )
        row_dot = jnp.sum(grad_weights * probs, axis=-1, keepdims=True)
        grad_scores = (probs * (grad_weights - row_dot)).astype(jnp.bfloat16)
        grad_q = (
            jnp.einsum("shqk,skhd->sqhd", grad_scores, k, preferred_element_type=jnp.float32)
            * scale
        )
        grad_k = (
            jnp.einsum("shqk,sqhd->skhd", grad_scores, q, preferred_element_type=jnp.float32)
            * scale
        )
        grad_v = jnp.einsum(
            "shqk,sqhd->skhd", probs_low, grad_attended, preferred_element_type=jnp.float32
        )
        return grad_q, grad_k, grad_v

    return attended, backward


def local(
    dp,
    ctx,
    tokens,
    segments,
    qkv_weight,
    qkv_bias,
    out_weight,
    out_bias,
    fc1_weight,
    fc1_bias,
    fc2_weight,
    fc2_bias,
    norm_gain,
    norm_shift,
    cotangent,
):
    f32, b16 = jnp.float32, jnp.bfloat16
    seqs, part, width = tokens.shape
    length = part * ctx
    rows = seqs * length
    ff = fc1_weight.shape[1]
    fl, dl = ff // ctx, width // ctx
    heads = HEADS // ctx
    head_dim = width // HEADS
    wr, fr = qkv_weight.shape[0], fc2_weight.shape[0]
    mine = lax.axis_index("ctx")
    devices = dp * ctx

    pieces = [qkv_bias, fc1_bias, out_bias, fc2_bias, norm_gain, norm_shift]
    marks = [0]
    for piece in pieces:
        marks.append(marks[-1] + piece.shape[0])
    small = lax.all_gather(jnp.concatenate(pieces), BOTH, axis=0)
    parts = [small[:, a:b] for a, b in zip(marks, marks[1:])]
    b_qkv = lax.dynamic_index_in_dim(
        parts[0].reshape(3, ctx, dl), mine, 1, keepdims=False
    ).reshape(3 * dl)
    b_fc1 = lax.dynamic_index_in_dim(
        parts[1].reshape(dp, ctx, fr), mine, 1, keepdims=False
    ).reshape(fl)
    b_out, b_fc2, gain, shift = [p.reshape(width).astype(f32) for p in parts[2:]]

    send_qkv = jnp.moveaxis(qkv_weight.reshape(wr, 3, ctx, dl), 2, 0).reshape(ctx, wr, 3 * dl)
    send_fc1 = jnp.moveaxis(fc1_weight.reshape(wr, dp, ctx, fr), 2, 0).reshape(ctx, wr, fl)
    sent = lax.all_to_all(
        jnp.concatenate([send_qkv, send_fc1], axis=2), "ctx", split_axis=0, concat_axis=0
    )
    out_perm = [(b, (b % dp) * ctx + b // dp) for b in range(devices)]
    out_back = [(j, i) for i, j in out_perm]
    out_piece = lax.ppermute(out_weight, BOTH, out_perm)
    w_qkv = lax.all_gather(sent[:, :, : 3 * dl], "dp", axis=0).reshape(width, 3 * dl)
    w_fc1 = lax.all_gather(sent[:, :, 3 * dl :], "dp", axis=0).reshape(width, fl)
    w_fc2 = lax.all_gather(fc2_weight, "dp", axis=0).reshape(fl, width)
    w_out = lax.all_gather(out_piece, "dp", axis=0).reshape(dl, width)

    tokens_all = lax.all_gather(tokens, "ctx", axis=1, tiled=True)
    cot_all = lax.all_gather(cotangent, "ctx", axis=1, tiled=True)

    positions = jnp.arange(length, dtype=jnp.int32)
    cosine, sine = angles(positions, ROT)

    scaled_all, _ = normalise(tokens_all.astype(f32).reshape(rows, width))
    normed = (scaled_all * gain + shift).astype(b16)
    grad_out = cot_all.reshape(rows, width)

    mixed = times(normed, w_qkv) + b_qkv.astype(f32)
    shape4 = (seqs, length, heads, head_dim)
    q = rotate(mixed[:, :dl].reshape(shape4), cosine, sine, ROT).astype(b16)
    k = rotate(mixed[:, dl : 2 * dl].reshape(shape4), cosine, sine, ROT).astype(b16)
    v = mixed[:, 2 * dl :].astype(b16).reshape(shape4)
    attended, attention_back = attention(q, k, v, segments, None, cosine, sine)
    attended = attended.reshape(rows, dl).astype(b16)

    hidden = times(normed, w_fc1) + b_fc1.astype(f32)
    act, gelu_back = jax.vjp(gelu_tanh, hidden)
    act = act.astype(b16)
    partial = times(attended, w_out) + times(act, w_fc2)
    summed = lax.psum_scatter(
        partial.astype(b16).reshape(seqs, length, width), "ctx", scatter_dimension=1, tiled=True
    )
    result = (tokens.astype(f32) + summed.astype(f32) + (b_out + b_fc2)).astype(b16)

    grad_act = times_transposed(grad_out, w_fc2)
    grad_hidden = gelu_back(grad_act)[0].astype(b16)
    grad_fc2 = contract_rows(act, grad_out)
    grad_fc2 = lax.psum_scatter(grad_fc2.astype(b16), "dp", scatter_dimension=0, tiled=True)
    grad_fc1 = contract_rows(normed, grad_hidden)
    grad_fc1_b = jnp.sum(grad_hidden, axis=0, dtype=f32)
    grad_fc1 = lax.psum_scatter(grad_fc1.astype(b16), "dp", scatter_dimension=0, tiled=True)
    grad_out_w = contract_rows(attended, grad_out)
    grad_out_w = lax.psum_scatter(grad_out_w.astype(b16), "dp", scatter_dimension=0, tiled=True)
    grad_attended = times_transposed(grad_out, w_out).astype(b16).reshape(shape4)
    grad_q, grad_k, grad_v = attention_back(grad_attended)
    grad_mixed = jnp.concatenate(
        [
            rotate(grad_q, cosine, -sine, ROT).reshape(rows, dl),
            rotate(grad_k, cosine, -sine, ROT).reshape(rows, dl),
            grad_v.reshape(rows, dl),
        ],
        axis=1,
    ).astype(b16)
    grad_normed = times_transposed(grad_hidden, w_fc1) + times_transposed(grad_mixed, w_qkv)
    grad_normed = lax.psum_scatter(
        grad_normed.astype(b16).reshape(seqs, length, width), "ctx", scatter_dimension=1, tiled=True
    ).astype(f32)
    grad_qkv = contract_rows(normed, grad_mixed)
    grad_qkv_b = jnp.sum(grad_mixed, axis=0, dtype=f32)
    grad_qkv = lax.psum_scatter(grad_qkv.astype(b16), "dp", scatter_dimension=0, tiled=True)

    back = lax.all_to_all(
        jnp.concatenate([grad_qkv, grad_fc1], axis=1).reshape(ctx, wr, 3 * dl + fl),
        "ctx",
        split_axis=0,
        concat_axis=0,
    ).astype(f32)
    grad_qkv = jnp.moveaxis(back[:, :, : 3 * dl].reshape(ctx, wr, 3, dl), 0, 2).reshape(
        wr, 3 * width
    )
    grad_fc1 = jnp.moveaxis(back[:, :, 3 * dl :].reshape(ctx, wr, dp, fr), 0, 2).reshape(wr, ff)
    grad_out_w = lax.ppermute(grad_out_w, BOTH, out_back).astype(f32)
    grad_fc2 = grad_fc2.astype(f32)

    grad_normed = grad_normed.reshape(seqs, part, width)
    own = tokens.astype(f32)
    cot = cotangent.astype(f32)
    scaled, inverse = normalise(own)
    grad_gain = jnp.sum(grad_normed * scaled, axis=(0, 1))
    grad_shift = jnp.sum(grad_normed, axis=(0, 1))
    grad_scaled = grad_normed * gain
    grad_input = inverse * (
        grad_scaled
        - jnp.mean(grad_scaled, axis=-1, keepdims=True)
        - scaled * jnp.mean(grad_scaled * scaled, axis=-1, keepdims=True)
    )
    grad_tokens = (cot + grad_input).astype(b16)

    wide_qkv_b = lax.dynamic_update_index_in_dim(
        jnp.zeros((3, ctx, dl), f32), grad_qkv_b.reshape(3, dl), mine, 1
    )
    wide_fc1_b = lax.dynamic_update_index_in_dim(
        jnp.zeros((dp, ctx, fr), f32), grad_fc1_b.reshape(dp, fr), mine, 1
    )
    bias_out = jnp.sum(cot, axis=(0, 1))
    sums = jnp.concatenate(
        [
            x.reshape(devices, -1)
            for x in (wide_qkv_b, wide_fc1_b, bias_out, grad_gain, grad_shift)
        ],
        axis=1,
    )
    sums = lax.psum_scatter(sums, BOTH, scatter_dimension=0, tiled=True)[0]
    at = [0, marks[1], marks[2], marks[3], marks[3] + wr, marks[3] + 2 * wr]
    g_qkv_b, g_fc1_b, g_bias, g_gain, g_shift = [sums[a:b] for a, b in zip(at, at[1:])]
    return (
        result,
        grad_tokens,
        grad_qkv,
        g_qkv_b,
        grad_out_w,
        g_bias,
        grad_fc1,
        g_fc1_b,
        grad_fc2,
        g_bias,
        g_gain,
        g_shift,
    )


def dot(left, right, contract):
    return lax.dot_general(
        left, right, ((contract[:1], contract[1:]), ((), ())), preferred_element_type=jnp.float32
    )


NORMAL, RIGHT_T, LEFT_T = (1, 0), (1, 1), (0, 0)


def turn_tables(length, head_dim, lanes):
    half = ROT // 2
    freq = np.float32(1.0) / np.power(
        np.float32(10000.0), np.arange(0, ROT, 2, dtype=np.float32) / np.float32(ROT)
    )
    theta = np.arange(length, dtype=np.float32)[:, None] * freq[None, :]
    cosine, sine = np.cos(theta), np.sin(theta)
    keep = np.ones((length, head_dim), np.float32)
    keep[:, :half] = cosine
    keep[:, half:ROT] = cosine
    ahead = np.zeros((length, head_dim), np.float32)
    ahead[:, :half] = -sine
    behind = np.zeros((length, head_dim), np.float32)
    behind[:, half:ROT] = sine
    return [np.tile(t, (1, lanes // head_dim)) for t in (keep, ahead, behind)]


def turn(x, keep, ahead, behind):
    half, lanes = ROT // 2, x.shape[1]
    return (
        x * keep
        + pltpu.roll(x, lanes - half, axis=1) * ahead
        + pltpu.roll(x, half, axis=1) * behind
    )


DELTAS = (-2, 2, -1, 1)
SLOTS = (0, 0, 1, 2)
PASSED = 4


def layer_kernel(
    nz, nc, marks,
    tok_ref, cot_ref, qkv_ref, fc1_ref, fc2_ref, out_ref, small_ref,
    seg_ref, keep_hbm, ahead_hbm, behind_hbm,
    o_result, o_tokens, o_qkv, o_out, o_fc1, o_fc2, o_sums,
    tok_all, cot_all, w_qkv, w_fc1, w_fc2, w_out, small_all,
    small_rows, vec_d, b_qkv, b_fc1, normed, q_s, k_s, v_s, attended, g_att, act, slope, gmixed,
    acc_q, acc_k, acc_v, acc_a, bias_s, g_hidden,
    give_qkv, give_fc1, give_fc2, give_out, got_qkv, got_fc1, got_fc2, got_out,
    own_qkv, own_fc1, own_fc2, own_out_g, far_qkv, far_fc1, far_fc2, far_out,
    pass_qkv, pass_fc1, pass_fc2, pass_out, log_s, seg_col, keep_ref, ahead_ref, behind_ref,
    part_got, part_own, norm_got, norm_own,
    swap_qkv, swap_fc1, swapped_qkv, swapped_fc1, out_planes, give_column, own_column, column_got,
    sums, sums_sib, sums_z,
    ctx_send, ctx_recv, z_send, z_recv, sib_send, sib_recv, loc,
    back_z_send, back_z_recv, back_sib_send, back_sib_recv, back_ctx_send, back_ctx_recv,
):
    f32, b16 = jnp.float32, jnp.bfloat16
    d, c = lax.axis_index("dp"), lax.axis_index("ctx")
    z, k = d // 2, lax.rem(d, 2)
    other = 2 * z + 1 - k
    wr, width = out_ref.shape
    dl = width // nc
    fr = fc2_ref.shape[0]
    nd = 2 * nz
    part = tok_ref.shape[0]
    length = part * nc
    head_dim = width // HEADS
    heads = HEADS // nc
    fl = nd * fr

    def ctx_to(j):
        return lax.rem(c + j, nc)

    def ctx_from(j):
        return lax.rem(c + nc - j, nc)

    def exists(delta):
        return (z + delta >= 0) & (z + delta < nz)

    def plane(delta):
        return 2 * jnp.clip(z + delta, 0, nz - 1) + k

    barrier = pltpu.get_barrier_semaphore()
    for j in range(1, nc):
        pl.semaphore_signal(barrier, inc=1, device_id=(d, ctx_to(j)), device_id_type=MESH)
    for delta in DELTAS:
        @pl.when(exists(delta))
        def _():
            pl.semaphore_signal(barrier, inc=1, device_id=(plane(delta), c), device_id_type=MESH)
    pl.semaphore_signal(barrier, inc=1, device_id=(other, c), device_id_type=MESH)
    planes = jnp.minimum(z, 2) + jnp.minimum(nz - 1 - z, 2)
    pl.semaphore_wait(barrier, nc + planes)

    def remote(src, dst, send, recv, device):
        return pltpu.make_async_remote_copy(
            src_ref=src, dst_ref=dst, send_sem=send, recv_sem=recv,
            device_id=device, device_id_type=MESH,
        )

    def rows(at):
        return pl.ds(pl.multiple_of(at * wr, wr), wr)

    def lanes(at, size):
        return pl.ds(pl.multiple_of(at * size, size), size)

    SMALL, QKV, FC1, TOK, COT, OUT, FC2 = range(7)

    def ctx_pieces(array, to):
        if array == SMALL:
            return [(small_ref, small_all.at[d, c])]
        if array == QKV:
            return [
                (qkv_ref.at[:, lanes(t * nc + to, dl)], w_qkv.at[d, rows(c), pl.ds(t * dl, dl)])
                for t in range(3)
            ]
        if array == FC1:
            return [
                (fc1_ref.at[:, lanes(g * nc + to, fr)], w_fc1.at[d, rows(c), pl.ds(g * fr, fr)])
                for g in range(nd)
            ]
        if array == TOK:
            return [(tok_ref, tok_all.at[c])]
        return [(cot_ref, cot_all.at[c])]

    def ctx_whole(array, sub):
        return {
            SMALL: lambda: small_all.at[d, sub],
            QKV: lambda: w_qkv.at[d, rows(sub), :],
            FC1: lambda: w_fc1.at[d, rows(sub), :],
            TOK: lambda: tok_all.at[sub],
            COT: lambda: cot_all.at[sub],
        }[array]()

    def ctx_start(array):
        for j in range(1, nc):
            for src, dst in ctx_pieces(array, ctx_to(j)):
                remote(src, dst, ctx_send.at[array, j], ctx_recv.at[array, j], (d, ctx_to(j))).start()
        for src, dst in ctx_pieces(array, c):
            pltpu.make_async_copy(src, dst, loc.at[array]).start()

    def ctx_arrive(array, j):
        got = ctx_whole(array, ctx_from(j))
        if j == 0:
            pltpu.make_async_copy(got, got, loc.at[array]).wait()
        else:
            remote(got, got, ctx_send.at[array, j], ctx_recv.at[array, j], (d, ctx_to(j))).wait_recv()

    def ctx_sent(array):
        for j in range(1, nc):
            got = ctx_whole(array, ctx_from(j))
            remote(got, got, ctx_send.at[array, j], ctx_recv.at[array, j], (d, ctx_to(j))).wait_send()

    def ctx_finish(array):
        for j in range(nc):
            ctx_arrive(array, j)

    side, across, corner = c + 1 - 2 * lax.rem(c, 2), lax.rem(c + 2, nc), nc - 1 - c
    first_half, second_half = pl.ds(0, part // 2), pl.ds(part // 2, part // 2)

    def pair_copy(array, n):
        store = tok_all if array == TOK else cot_all
        src = tok_ref if array == TOK else cot_ref
        if n == 1:
            dst, to = store.at[c], side
        elif n == 2:
            dst, to = store.at[c], across
        elif n == 3:
            src = store.at[side, first_half, :]
            dst, to = src, across
        else:
            src = store.at[across, second_half, :]
            dst, to = src, side
        return remote(src, dst, ctx_send.at[array, n], ctx_recv.at[array, n], (d, to))

    def pair_start(array):
        store, src = (tok_all, tok_ref) if array == TOK else (cot_all, cot_ref)
        pair_copy(array, 1).start()
        pair_copy(array, 2).start()
        pltpu.make_async_copy(src, store.at[c], loc.at[array]).start()

    def pair_got(array, n):
        store = tok_all if array == TOK else cot_all
        got = {
            0: lambda: store.at[corner, second_half, :],
            1: lambda: store.at[side],
            2: lambda: store.at[across],
            3: lambda: store.at[corner, first_half, :],
        }[n]()
        remote(got, got, ctx_send.at[array, n], ctx_recv.at[array, n], (d, side)).wait_recv()

    def pair_forward(array):
        pair_got(array, 1)
        pair_copy(array, 3).start()
        pair_got(array, 2)
        pair_copy(array, 0).start()

    def pair_own(array):
        store = tok_all if array == TOK else cot_all
        pltpu.make_async_copy(store.at[c], store.at[c], loc.at[array]).wait()

    def block_of(array, at):
        if array == OUT:
            return out_planes.at[lax.div(at, 2)]
        return {SMALL: small_all, QKV: w_qkv, FC1: w_fc1, FC2: w_fc2}[array].at[at]

    near_low, near_high = z == 1, z == nz - 2

    def z_copy(array, n, delta, owner):
        block = block_of(array, owner)
        src = block
        if array in (FC2, OUT) and n < PASSED:
            src = fc2_ref if array == FC2 else out_ref
        return remote(src, block, z_send.at[array, n], z_recv.at[array, n], (plane(delta), c))

    def z_got(array, n, owner):
        block = block_of(array, owner)
        return remote(block, block, z_send.at[array, n], z_recv.at[array, n], (d, c))

    def sib_copy(array, at):
        block = block_of(array, 2 * at + k)
        return remote(block, block, sib_send.at[array, at], sib_recv.at[array, at], (other, c))

    def z_own(array):
        for n, delta in enumerate(DELTAS):
            @pl.when(exists(delta))
            def _():
                z_copy(array, n, delta, d).start()
        if array not in (FC2, OUT):
            sib_copy(array, z).start()

    def z_forward(array):
        @pl.when(near_high)
        def _():
            z_got(array, DELTAS.index(2), k).wait_recv()
            z_copy(array, PASSED, 1, k).start()

        @pl.when(near_low)
        def _():
            z_got(array, DELTAS.index(-2), d + 4).wait_recv()
            z_copy(array, PASSED, -1, d + 4).start()

    def z_arrive(array):
        for n, delta in enumerate(DELTAS):
            done = near_high if delta == 2 else near_low if delta == -2 else None
            wanted = exists(-delta) if done is None else exists(-delta) & jnp.logical_not(done)

            @pl.when(wanted)
            def _():
                z_got(array, n, plane(-delta)).wait_recv()

        @pl.when(z == 0)
        def _():
            z_got(array, PASSED, 2 * (nz - 1) + k).wait_recv()

        @pl.when(z == nz - 1)
        def _():
            z_got(array, PASSED, k).wait_recv()

        if array == OUT:
            return
        for at in range(nz):
            if array == FC2:
                sib_copy(array, at).start()
            else:
                @pl.when(z != at)
                def _():
                    sib_copy(array, at).start()

    def z_finish(array):
        for at in range(nz):
            block = block_of(array, 2 * at + 1 - k)
            remote(block, block, sib_send.at[array, at], sib_recv.at[array, at], (other, c)).wait_recv()

    def z_sent(array):
        for n, delta in enumerate(DELTAS):
            @pl.when(exists(delta))
            def _():
                z_copy(array, n, delta, d).wait_send()

        @pl.when(near_high | near_low)
        def _():
            z_copy(array, PASSED, 1, k).wait_send()

        if array != OUT:
            for at in range(nz):
                sib_copy(array, at).wait_send()

    def out_copy(j, to, sub):
        piece = out_planes.at[to]
        return remote(piece, w_out.at[k, rows(sub), :], ctx_send.at[OUT, j], ctx_recv.at[OUT, j], (d, to))

    def own_out():
        return pltpu.make_async_copy(out_planes.at[c], w_out.at[k, rows(c), :], loc.at[OUT])

    def out_sib(which):
        piece = w_out.at[which]
        return remote(piece, piece, sib_send.at[OUT, 0], sib_recv.at[OUT, 0], (other, c))

    ctx_start(SMALL)
    ctx_start(QKV)
    z_own(OUT)
    tables = [(keep_hbm, keep_ref), (ahead_hbm, ahead_ref), (behind_hbm, behind_ref)]
    tables = [pltpu.make_async_copy(a, b, loc.at[8 + n]) for n, (a, b) in enumerate(tables)]
    for copy in tables:
        copy.start()
    copy_out = pltpu.make_async_copy(out_ref, out_planes.at[z], loc.at[7])
    copy_out.start()
    ctx_start(FC1)
    pair_start(TOK)
    copy_fc2 = pltpu.make_async_copy(fc2_ref, w_fc2.at[d], loc.at[FC2])
    copy_fc2.start()

    ctx_finish(SMALL)
    z_own(SMALL)
    ctx_finish(QKV)
    z_own(QKV)
    z_forward(OUT)
    z_forward(SMALL)
    ctx_finish(FC1)
    z_own(FC1)
    z_arrive(OUT)
    copy_out.wait()
    own_out().start()
    for j in range(1, nc):
        out_copy(j, ctx_to(j), c).start()
    pair_start(COT)
    z_arrive(SMALL)
    z_forward(QKV)
    z_own(FC2)
    z_finish(SMALL)

    def collect(p, carry):
        small_rows[pl.ds(p, 1), :] = small_all[p // nc, lax.rem(p, nc)]
        return carry

    lax.fori_loop(0, nd * nc, collect, 0)
    table = small_rows[...]
    pack = table.shape[1]

    def vector(mark, size, first, count):
        entry = lax.broadcasted_iota(jnp.int32, (1, count), 1).astype(f32) + first
        owner = jnp.floor((entry + 0.5) * (1.0 / size))
        lane = entry - owner * size + mark
        pick = lax.broadcasted_iota(jnp.int32, (pack, count), 0).astype(f32) == lane
        found = dot(table.astype(b16), jnp.where(pick, 1.0, 0.0).astype(b16), NORMAL)
        here = lax.broadcasted_iota(jnp.int32, (nd * nc, count), 0).astype(f32) == owner
        return jnp.sum(jnp.where(here, found, 0.0), axis=0, keepdims=True)

    for i in range(2):
        vec_d[pl.ds(i, 1), :] = vector(marks[2 + i], wr, 0.0, width)
    vec_d[2:3, :] = vector(marks[4], wr, 0.0, width) + vector(marks[5], wr, 0.0, width)
    for t in range(3):
        b_qkv[:, pl.ds(t * dl, dl)] = vector(marks[1], 3 * wr, (t * width + c * dl).astype(f32), dl)
    for g in range(nd):
        b_fc1[:, pl.ds(g * fr, fr)] = small_all[g, c][:, :fr]

    z_arrive(QKV)
    z_finish(QKV)

    seg_col[...] = jnp.broadcast_to(seg_ref[...].astype(f32), (128, length)).T

    chunk = 32

    def block_rows(b):
        return pl.ds(pl.multiple_of(b * part, part), part)

    def normalise_block(b):
        def step(i, carry):
            at = pl.multiple_of(i * chunk, chunk)
            x = tok_all[b, pl.ds(at, chunk), :].astype(f32)
            x = x - jnp.mean(x, axis=-1, keepdims=True)
            x = x * lax.rsqrt(jnp.mean(x * x, axis=-1, keepdims=True) + epsilon)
            normed[pl.ds(pl.multiple_of(b * part, part) + at, chunk), :] = (
                x * vec_d[0:1, :] + vec_d[1:2, :]
            ).astype(b16)
            return carry

        lax.fori_loop(0, part // chunk, step, 0)

    def qkv_block(b):
        at = block_rows(b)
        x = normed[at, :]
        keep = jnp.tile(keep_ref[at, :], (1, dl // keep_ref.shape[1]))
        ahead = jnp.tile(ahead_ref[at, :], (1, dl // keep_ref.shape[1]))
        behind = jnp.tile(behind_ref[at, :], (1, dl // keep_ref.shape[1]))
        for t, to in enumerate((q_s, k_s, v_s)):
            w = w_qkv[:, :, pl.ds(t * dl, dl)].reshape(width, dl)
            y = dot(x, w, NORMAL) + b_qkv[:, pl.ds(t * dl, dl)]
            if t < 2:
                y = turn(y, keep, ahead, behind)
            to[at, :] = y.astype(b16)

    for copy in tables:
        copy.wait()
    pair_own(TOK)
    normalise_block(c)
    qkv_block(c)
    pair_forward(TOK)
    normalise_block(side)
    qkv_block(side)
    normalise_block(across)
    qkv_block(across)
    pair_got(TOK, 3)
    pair_got(TOK, 0)
    normalise_block(corner)
    qkv_block(corner)

    z_forward(FC1)
    pair_forward(COT)

    tile = 256
    reach = 512 // tile
    scale = float(head_dim) ** (-0.5)

    def spans(i):
        first = max(0, i - reach) * tile
        count = (i + 1) * tile - first
        return pl.ds(i * tile, tile), pl.ds(first, count), count

    def mask(i):
        at, to, count = spans(i)
        same = seg_col[at, :1] == seg_ref[:1, to].astype(f32)
        row = lax.broadcasted_iota(jnp.int32, (tile, count), 0) + (tile * i - to.start)
        col = lax.broadcasted_iota(jnp.int32, (tile, count), 1)
        bias_s[:, :count] = jnp.where(same & (col <= row), 0.0, -1e30)

    def only_head(h):
        lane = lax.broadcasted_iota(jnp.int32, (1, dl), 1)
        return jnp.where((lane >= h * head_dim) & (lane < (h + 1) * head_dim), 1.0, 0.0)

    for i in range(length // tile):
        at, to, count = spans(i)
        mask(i)
        acc_a[...] = jnp.zeros_like(acc_a)

        def forward_step(h, carry):
            only = only_head(h)
            s = dot(q_s[at, :] * only.astype(b16), k_s[to, :], RIGHT_T) * scale + bias_s[:, :count]
            top = jnp.max(s, axis=-1, keepdims=True)
            e = jnp.exp(s - top)
            sum_e = jnp.sum(e, axis=-1, keepdims=True)
            log_s[h, at, :] = top + jnp.log(sum_e)
            p_low = (e * (1.0 / sum_e)).astype(b16)
            acc_a[...] += dot(p_low, v_s[to, :], NORMAL) * only
            return carry

        lax.fori_loop(0, heads, forward_step, 0, unroll=True)
        attended[at, :] = acc_a[...].astype(b16)

    z_arrive(FC1)
    z_finish(FC1)

    def hidden_block(b, carry):
        at = block_rows(b)
        x = normed[at, :]
        for g in range(0, fl, 256):
            w = w_fc1[:, :, pl.ds(g, 256)].reshape(width, 256)
            h = dot(x, w, NORMAL) + b_fc1[:, pl.ds(g, 256)]
            s = h * h
            t = jnp.tanh(h * (0.7978845608028654 + (0.7978845608028654 * 0.044715) * s))
            half_t = 0.5 + 0.5 * t
            act[at, pl.ds(g, 256)] = (h * half_t).astype(b16)
            slope[at, pl.ds(g, 256)] = half_t + 0.5 * h * (1.0 - t * t) * (
                0.7978845608028654 + (3 * 0.7978845608028654 * 0.044715) * s
            )
        return carry

    lax.fori_loop(0, nc, hidden_block, 0)

    z_forward(FC2)
    pair_own(COT)
    pair_got(COT, 3)
    pair_got(COT, 0)

    COLUMN = 7
    gives = {QKV: give_qkv, FC1: give_fc1, FC2: give_fc2, OUT: give_out, COLUMN: give_column}
    gots = {QKV: got_qkv, FC1: got_fc1, FC2: got_fc2, OUT: got_out}
    owns = {QKV: own_qkv, FC1: own_fc1, FC2: own_fc2, OUT: own_out_g, COLUMN: own_column}
    fars = {QKV: far_qkv, FC1: far_fc1, FC2: far_fc2, COLUMN: far_out}
    passes = {QKV: pass_qkv, FC1: pass_fc1, FC2: pass_fc2, COLUMN: pass_out}

    def cotangents():
        return cot_all[...].reshape(length, width)

    def weight_gradient(array, left, right):
        give, own = gives[array], owns[array]
        size = give.shape[1]

        def step(i, carry):
            both = dot(left[:, lanes(i, 2 * size)], right(), LEFT_T)
            low, high = both[:size], both[size:]
            own[i] = jnp.where(k == 0, low, high)
            give[i] = jnp.where(k == 0, high, low).astype(b16)
            return carry

        lax.fori_loop(0, give.shape[0], step, 0)
        to_sibling(array).start()

    def to_sibling(array):
        return remote(
            gives[array], gots[array], back_sib_send.at[array], back_sib_recv.at[array], (other, c)
        )

    def to_owner(array, n, delta):
        block = gives[array].at[jnp.clip(z + delta, 0, nz - 1)]
        return remote(
            block, fars[array].at[SLOTS[n]], back_z_send.at[array, n], back_z_recv.at[array, n], (plane(delta), c)
        )

    def to_pass(array, delta):
        block = gives[array].at[jnp.clip(z + 3 * delta, 0, nz - 1)]
        return remote(
            block, passes[array], back_z_send.at[array, PASSED], back_z_recv.at[array, PASSED], (plane(delta), c)
        )

    def both_cores(array, at):
        if array == COLUMN:
            return own_column[at]
        return owns[array][at] + gots[array][at].astype(f32)

    def send_back(array):
        for delta in (-1, 1):
            far = jnp.clip(z + 3 * delta, 0, nz - 1)

            @pl.when(z == (nz - 1 if delta < 0 else 0))
            def _():
                gives[array][far] = both_cores(array, far).astype(b16)
                to_pass(array, delta).start()
        for n, delta in enumerate(DELTAS):
            hold = {-2: near_high, 2: near_low}.get(delta)
            go = exists(delta) if hold is None else exists(delta) & jnp.logical_not(hold)
            at = jnp.clip(z + delta, 0, nz - 1)

            @pl.when(go)
            def _():
                gives[array][at] = both_cores(array, at).astype(b16)
                to_owner(array, n, delta).start()

    def add_sibling(array):
        to_sibling(array).wait()
        send_back(array)

    def pass_back(array):
        for near, delta in ((near_high, -2), (near_low, 2)):
            at = jnp.clip(z + delta, 0, nz - 1)

            @pl.when(near)
            def _():
                to_pass(array, delta).wait_recv()
                gives[array][at] = (both_cores(array, at) + passes[array][...].astype(f32)).astype(b16)
                to_owner(array, DELTAS.index(delta), delta).start()

    def gather_total(array):
        own = owns[array]
        own[z] = both_cores(array, z)
        for n, delta in enumerate(DELTAS):
            @pl.when(exists(-delta))
            def _():
                to_owner(array, n, delta).wait_recv()
                own[z] = own[z] + fars[array][SLOTS[n]].astype(f32)

    def owner_sent(array):
        for n, delta in enumerate(DELTAS):
            @pl.when(exists(delta))
            def _():
                to_owner(array, n, delta).wait_send()
        for delta in (-1, 1):
            @pl.when(z == (nz - 1 if delta < 0 else 0))
            def _():
                to_pass(array, delta).wait_send()

    def column_copy(j, to):
        return remote(
            give_out.at[0, rows(to), :], column_got.at[c], back_ctx_send.at[OUT, j], back_ctx_recv.at[OUT, j], (d, to)
        )

    def to_columns():
        to_sibling(OUT).wait()
        own_out_g[0] = own_out_g[0] + got_out[0].astype(f32)
        give_out[0] = own_out_g[0].astype(b16)
        for j in range(1, nc):
            column_copy(j, ctx_to(j)).start()
        own_column[c] = own_out_g[0, rows(c), :]

    def from_columns():
        for j in range(1, nc):
            source = ctx_from(j)
            got = column_got.at[source]
            remote(got, got, back_ctx_send.at[OUT, j], back_ctx_recv.at[OUT, j], (d, source)).wait_recv()
            own_column[source] = column_got[source].astype(f32)
        send_back(COLUMN)

    PART, NORM, SUMS = TOK, COT, SMALL

    def over_ctx(array, src, dst, j, to):
        return remote(src, dst, back_ctx_send.at[array, j], back_ctx_recv.at[array, j], (d, to))

    weight_gradient(FC2, act, cotangents)
    weight_gradient(OUT, attended, cotangents)

    own_out().wait()
    for j in range(1, nc):
        out_copy(j, ctx_to(j), ctx_from(j)).wait_recv()
    out_sib(k).start()
    out_sib(1 - k).wait_recv()

    w_o = w_out[...].reshape(dl, width)

    def g_att_block(b, carry):
        g_att[block_rows(b), :] = dot(cot_all[b], w_o, RIGHT_T).astype(b16)
        return carry

    lax.fori_loop(0, nc, g_att_block, 0)
    add_sibling(FC2)
    to_columns()

    acc_k[...] = jnp.zeros_like(acc_k)
    acc_v[...] = jnp.zeros_like(acc_v)
    wide = (1, dl // keep_ref.shape[1])
    def attend_back(i):
        at, to, count = spans(i)
        mask(i)
        acc_q[...] = jnp.zeros_like(acc_q)

        def backward_step(h, carry):
            only = only_head(h)
            only_low = only.astype(b16)
            qh = q_s[at, :] * only_low
            gh = g_att[at, :] * only_low
            keys, values = k_s[to, :], v_s[to, :]
            p = jnp.exp(dot(qh, keys, RIGHT_T) * scale + bias_s[:, :count] - log_s[h, at, :])
            gw = dot(gh, values, RIGHT_T)
            gs = (p * (gw - jnp.sum(gw * p, axis=-1, keepdims=True))).astype(b16)
            acc_q[...] += dot(gs, keys, NORMAL) * only
            acc_k[to, :] += dot(gs, qh, LEFT_T)
            acc_v[to, :] += dot(p.astype(b16), gh, LEFT_T)
            return carry

        lax.fori_loop(0, heads, backward_step, 0, unroll=True)
        gmixed[at, pl.ds(0, dl)] = turn(
            acc_q[...] * scale,
            jnp.tile(keep_ref[at, :], wide),
            -jnp.tile(ahead_ref[at, :], wide),
            -jnp.tile(behind_ref[at, :], wide),
        ).astype(b16)

    count_tiles = length // tile
    early = count_tiles // 2
    for i in range(early):
        attend_back(i)
    copy_fc2.wait()
    z_arrive(FC2)
    z_finish(FC2)

    def result_term(b):
        at = block_rows(b)
        return dot(attended[at, :], w_out[...].reshape(dl, width), NORMAL) + dot(
            act[at, :], w_fc2[...].reshape(fl, width), NORMAL
        )

    pair_copy(TOK, 3).wait_send()
    pair_copy(TOK, 0).wait_send()
    for j in range(1, nc):
        b = ctx_to(j)
        tok_all[b] = result_term(b).astype(b16)
        over_ctx(PART, tok_all.at[b], part_got.at[j - 1], j, b).start()
    part_own[...] = result_term(c)
    from_columns()
    for i in range(early, count_tiles):
        if i == count_tiles - 1:
            pass_back(FC2)
        attend_back(i)

    def finish_block(b, carry):
        at = block_rows(b)
        gmixed[at, pl.ds(dl, dl)] = turn(
            acc_k[at, :] * scale,
            jnp.tile(keep_ref[at, :], wide),
            -jnp.tile(ahead_ref[at, :], wide),
            -jnp.tile(behind_ref[at, :], wide),
        ).astype(b16)
        gmixed[at, pl.ds(2 * dl, dl)] = acc_v[at, :].astype(b16)
        return carry

    lax.fori_loop(0, nc, finish_block, 0)

    weight_gradient(QKV, normed, lambda: gmixed[...])
    ones = jnp.ones((8, length), b16)
    sums[0, :, pl.ds(0, 3 * dl)] = dot(ones, gmixed[...], NORMAL)[:1]
    at_sum = 3 * dl + fl
    sums[0, :, pl.ds(at_sum, width)] = dot(ones[:, :part], cot_all[c], NORMAL)[:1]
    pass_back(COLUMN)
    add_sibling(QKV)

    def hidden_gradient(b, carry):
        at = block_rows(b)
        g = cot_all[b]
        for i in range(nd):
            to = pl.ds(i * fr, fr)
            g_hidden[at, to] = (dot(g, w_fc2[i], RIGHT_T) * slope[at, to]).astype(b16)
        return carry

    lax.fori_loop(0, nc, hidden_gradient, 0)

    def normed_term(b):
        at = block_rows(b)
        return dot(g_hidden[at, :], w_fc1[...].reshape(width, fl), RIGHT_T) + dot(
            gmixed[at, :], w_qkv[...].reshape(width, 3 * dl), RIGHT_T
        )

    pair_copy(COT, 3).wait_send()
    pair_copy(COT, 0).wait_send()
    for j in range(1, nc):
        b = ctx_to(j)
        cot_all[b] = normed_term(b).astype(b16)
        over_ctx(NORM, cot_all.at[b], norm_got.at[j - 1], j, b).start()
    norm_own[...] = normed_term(c)

    pass_back(QKV)
    weight_gradient(FC1, normed, lambda: g_hidden[...])
    sums[0, :, pl.ds(3 * dl, fl)] = dot(ones, g_hidden[...], NORMAL)[:1]
    for j in range(1, nc):
        over_ctx(PART, tok_all.at[c], part_got.at[j - 1], j, c).wait_recv()

    def result_step(i, carry):
        at = pl.ds(pl.multiple_of(i * chunk, chunk), chunk)
        y = tok_all[c, at, :].astype(f32) + part_own[at, :] + vec_d[2:3, :]
        for j in range(1, nc):
            y = y + part_got[j - 1, at, :].astype(f32)
        o_result[at, :] = y.astype(b16)
        return carry

    lax.fori_loop(0, part // chunk, result_step, 0)
    add_sibling(FC1)
    gather_total(FC2)
    o_fc2[...] = own_fc2[z]

    swaps = {QKV: (swap_qkv, swapped_qkv), FC1: (swap_fc1, swapped_fc1)}

    def place(array, source, x):
        if array == QKV:
            for t in range(3):
                o_qkv[:, lanes(t * nc + source, dl)] = x[:, t * dl : (t + 1) * dl]
        else:
            for g in range(nd):
                o_fc1[:, lanes(g * nc + source, fr)] = x[:, g * fr : (g + 1) * fr]

    def swap_start(array):
        gather_total(array)
        src, dst = swaps[array]
        own = owns[array]
        for j in range(1, nc):
            src[j - 1] = own[z, rows(ctx_to(j)), :].astype(b16)
            over_ctx(array, src.at[j - 1], dst.at[j - 1], j, ctx_to(j)).start()
        place(array, c, own[z, rows(c), :])

    def swap_finish(array):
        src, dst = swaps[array]
        for j in range(1, nc):
            over_ctx(array, src.at[j - 1], dst.at[j - 1], j, ctx_to(j)).wait_recv()
            place(array, ctx_from(j), dst[j - 1].astype(f32))

    gather_total(COLUMN)
    o_out[...] = own_column[z]
    pass_back(FC1)
    swap_start(QKV)
    for j in range(1, nc):
        over_ctx(NORM, cot_all.at[c], norm_got.at[j - 1], j, c).wait_recv()

    def norm_step(i, carry):
        gain_sum, shift_sum = carry
        at = pl.ds(pl.multiple_of(i * chunk, chunk), chunk)
        x = tok_all[c, at, :].astype(f32)
        x = x - jnp.mean(x, axis=-1, keepdims=True)
        inverse = lax.rsqrt(jnp.mean(x * x, axis=-1, keepdims=True) + epsilon)
        x = x * inverse
        g = norm_own[at, :]
        for j in range(1, nc):
            g = g + norm_got[j - 1, at, :].astype(f32)
        v = g * vec_d[0:1, :]
        y = inverse * (
            v - jnp.mean(v, axis=-1, keepdims=True) - x * jnp.mean(v * x, axis=-1, keepdims=True)
        )
        o_tokens[at, :] = (cot_all[c, at, :].astype(f32) + y).astype(b16)
        return (
            gain_sum + jnp.sum(g * x, axis=0, keepdims=True),
            shift_sum + jnp.sum(g, axis=0, keepdims=True),
        )

    zero = jnp.zeros((1, width), f32)
    gain_sum, shift_sum = lax.fori_loop(0, part // chunk, norm_step, (zero, zero))
    sums[0, :, pl.ds(at_sum + width, width)] = gain_sum
    sums[0, :, pl.ds(at_sum + 2 * width, width)] = shift_sum

    sum_sib = remote(sums.at[0], sums_sib.at[0], back_sib_send.at[SUMS], back_sib_recv.at[SUMS], (other, c))
    sum_sib.start()
    sum_sib.wait()
    sums[1] = sums[0] + sums_sib[0]
    for n, partner in enumerate((z + 1 - 2 * lax.rem(z, 2), lax.rem(z + 2, nz))):
        trade = remote(
            sums.at[n + 1], sums_z.at[n], back_z_send.at[SUMS, n], back_z_recv.at[SUMS, n], (2 * partner + k, c)
        )
        trade.start()
        trade.wait()
        sums[n + 2] = sums[n + 1] + sums_z[n]
    sums_mine = sums.at[3]
    o_sums[c] = sums[3]
    for j in range(1, nc):
        over_ctx(SUMS, sums_mine, o_sums.at[c], j, ctx_to(j)).start()

    swap_finish(QKV)
    swap_start(FC1)
    for j in range(1, nc):
        over_ctx(SUMS, sums_mine, o_sums.at[ctx_from(j)], j, ctx_to(j)).wait_recv()
    swap_finish(FC1)

    for array in (SMALL, QKV, FC1, FC2, OUT):
        z_sent(array)
    for array in (SMALL, QKV, FC1):
        ctx_sent(array)
    for array in (TOK, COT):
        for n in (1, 2):
            pair_copy(array, n).wait_send()
    for j in range(1, nc):
        out_copy(j, ctx_to(j), c).wait_send()
        column_copy(j, ctx_to(j)).wait_send()
    out_sib(k).wait_send()
    for array in (QKV, COLUMN, FC1, FC2):
        owner_sent(array)
    for j in range(1, nc):
        over_ctx(PART, tok_all.at[c], part_got.at[j - 1], j, c).wait_send()
        over_ctx(NORM, cot_all.at[c], norm_got.at[j - 1], j, c).wait_send()
        over_ctx(SUMS, sums_mine, o_sums.at[c], j, ctx_to(j)).wait_send()
        for array in (QKV, FC1):
            over_ctx(array, swaps[array][0].at[j - 1], swaps[array][1].at[j - 1], j, c).wait_send()


def layer_all(nz, nc, marks, tokens, cotangent, segments, qkv_weight, fc1_weight, fc2_weight, out_weight, small):
    part, width = tokens.shape
    wr, fr = qkv_weight.shape[0], fc2_weight.shape[0]
    nd, dl = 2 * nz, width // nc
    length, fl = part * nc, 2 * nz * fr
    cw = nc * wr
    f32, b16 = jnp.float32, jnp.bfloat16
    tables = [jnp.asarray(t) for t in turn_tables(length, width // HEADS, 128)]
    pack = small.shape[1]
    total = 3 * dl + fl + 3 * width
    tile, window = 256, 768
    results = [
        ((part, width), b16),
        ((part, width), b16),
        ((wr, 3 * width), f32),
        ((wr, width), f32),
        ((wr, fl * nc), f32),
        ((fr, width), f32),
        ((nc, 1, total), f32),
    ]
    work = [
        ((nc, part, width), b16),
        ((nc, part, width), b16),
        ((nd, cw, 3 * dl), b16),
        ((nd, cw, fl), b16),
        ((nd, fr, width), b16),
        ((2, cw, width), b16),
        ((nd, nc, 1, pack), f32),
        ((nd * nc, pack), f32),
        ((8, width), f32),
        ((1, 3 * dl), f32),
        ((1, fl), f32),
        ((length, width), b16),
        ((length, dl), b16),
        ((length, dl), b16),
        ((length, dl), b16),
        ((length, dl), b16),
        ((length, dl), b16),
        ((length, fl), b16),
        ((length, fl), f32),
        ((length, 3 * dl), b16),
        ((tile, dl), f32),
        ((length, dl), f32),
        ((length, dl), f32),
        ((tile, dl), f32),
        ((tile, window), f32),
        ((length, fl), b16),
    ]
    grads = [(nz, cw, 3 * dl), (nz, cw, fl), (nz, fr, width), (1, cw, width)]
    passed = grads[:3] + [(nz, wr, width)]
    fars = [(3,) + g[1:] for g in passed]
    work += [(g, b16) for g in grads] + [(g, b16) for g in grads] + [(g, f32) for g in grads]
    work += [(g, b16) for g in fars] + [(g[1:], b16) for g in passed]
    work += [((HEADS // nc, length, 1), f32), ((length, 128), f32)] + [((length, 128), f32)] * 3
    work += [((nc - 1, part, width), b16), ((part, width), f32)] * 2
    work += [((nc - 1, wr, n), b16) for n in (3 * dl, fl)] * 2
    work += [((nz, wr, width), t) for t in (b16, b16, f32)] + [((nc, wr, width), b16)]
    work += [((n, 1, total), f32) for n in (4, 1, 2)]
    dma = pltpu.SemaphoreType.DMA
    sems = [(7, nc), (7, nc), (7, 5), (7, 5), (7, nz), (7, nz), (11,)]
    sems += [(8, 5), (8, 5), (7,), (7,), (7, nc), (7, nc)]
    hbm, vmem = pl.BlockSpec(memory_space=pl.ANY), pl.BlockSpec(memory_space=pltpu.VMEM)
    return pl.pallas_call(
        functools.partial(layer_kernel, nz, nc, marks),
        out_shape=[jax.ShapeDtypeStruct(s, t) for s, t in results],
        in_specs=[hbm] * 7 + [vmem] + [hbm] * 3,
        out_specs=[vmem] * len(results),
        scratch_shapes=[pltpu.VMEM(s, t) for s, t in work] + [dma(s) for s in sems],
        compiler_params=pltpu.CompilerParams(
            collective_id=0, has_side_effects=True, vmem_limit_bytes=62 * 2**20
        ),
        name="layer",
    )(tokens, cotangent, qkv_weight, fc1_weight, fc2_weight, out_weight, small, segments.reshape(1, length), *tables)


def finish_kernel(
    dl, fr, wr,
    result, tokens, qkv, out, fc1, fc2, sums,
    o_result, o_tokens, o_qkv, o_out, o_fc1, o_fc2, o_qkv_b, o_out_b, o_fc1_b, o_fc2_b, o_gain, o_shift,
    row,
):
    moves = [(result, o_result), (tokens, o_tokens), (qkv, o_qkv), (out, o_out), (fc1, o_fc1), (fc2, o_fc2)]
    for source, to in moves:
        to[...] = source[...]
    nc, total = sums.shape[0], sums.shape[2]
    mine, group = lax.axis_index("ctx"), lax.axis_index("dp")
    place = group * nc + mine
    width = dl * nc
    fl = total - 3 * dl - 3 * width

    def piece(values, size):
        length = values.shape[1]
        return pltpu.roll(values, length - place * size, axis=1)[0, :size]

    for t in range(3):
        for rank in range(nc):
            row[:, pl.ds(t * width + rank * dl, dl)] = sums[rank][:, t * dl : (t + 1) * dl]
    o_qkv_b[...] = piece(row[...], 3 * wr)
    at = pl.ds(pl.multiple_of(3 * dl + group * fr, fr), fr)
    o_fc1_b[...] = sums[mine, :, at][0]
    for n, outs in enumerate(((o_out_b, o_fc2_b), (o_gain,), (o_shift,))):
        first = 3 * dl + fl + n * width
        whole = sums[0][:, first : first + width]
        for rank in range(1, nc):
            whole = whole + sums[rank][:, first : first + width]
        for to in outs:
            to[...] = piece(whole, wr)


def finish_all(dl, fr, wr, arrays):
    f32 = jnp.float32
    vmem = pl.BlockSpec(memory_space=pltpu.VMEM)
    vectors = [3 * wr, wr, fr, wr, wr, wr]
    nc = arrays[6].shape[0]
    return pl.pallas_call(
        functools.partial(finish_kernel, dl, fr, wr),
        out_shape=[jax.ShapeDtypeStruct(a.shape, a.dtype) for a in arrays[:6]]
        + [jax.ShapeDtypeStruct((n,), f32) for n in vectors],
        in_specs=[vmem] * 7,
        out_specs=[vmem] * 12,
        scratch_shapes=[pltpu.VMEM((1, 3 * dl * nc), f32)],
        name="finish",
    )(*arrays)


def local_direct(
    dp,
    ctx,
    tokens,
    segments,
    qkv_weight,
    qkv_bias,
    out_weight,
    out_bias,
    fc1_weight,
    fc1_bias,
    fc2_weight,
    fc2_bias,
    norm_gain,
    norm_shift,
    cotangent,
):
    width = tokens.shape[-1]
    dl, fl = width // ctx, fc1_weight.shape[1] // ctx
    wr, fr = qkv_weight.shape[0], fc2_weight.shape[0]
    pieces = [fc1_bias, qkv_bias, norm_gain, norm_shift, out_bias, fc2_bias]
    marks = [0]
    for piece in pieces:
        marks.append(marks[-1] + piece.shape[0])
    vector = jnp.concatenate(pieces).astype(jnp.float32)
    vector = jnp.pad(vector, (0, -marks[-1] % 128))[None]
    arrays = layer_all(
        dp // 2,
        ctx,
        tuple(marks),
        tokens[0],
        cotangent[0],
        segments[0],
        qkv_weight,
        fc1_weight,
        fc2_weight,
        out_weight,
        vector,
    )
    result, grad_tokens, *rest = finish_all(dl, fr, wr, arrays)
    grad_qkv, grad_out, grad_fc1, grad_fc2, g_qkv_b, g_out_b, g_fc1_b, g_fc2_b, g_gain, g_shift = rest
    return (
        result[None],
        grad_tokens[None],
        grad_qkv,
        g_qkv_b,
        grad_out,
        g_out_b,
        grad_fc1,
        g_fc1_b,
        grad_fc2,
        g_fc2_b,
        g_gain,
        g_shift,
    )


def solution(mesh):
    sizes = (mesh.shape["dp"], mesh.shape["ctx"])
    seq, mat, vec = P("dp", "ctx", None), P(BOTH, None), P(BOTH)

    def spread(*args):
        dp, ctx = sizes
        tokens, qkv_weight, fc2_weight = args[0], args[2], args[8]
        direct = (
            dp == 8
            and ctx == 4
            and tokens.shape[0] == 1
            and tokens.shape[1] % 256 == 0
            and qkv_weight.shape[0] % 32 == 0
            and fc2_weight.shape[0] % 128 == 0
        )
        return (local_direct if direct else local)(*sizes, *args)

    placed = (seq, P("dp", None), mat, vec, mat, vec, mat, vec, mat, vec, vec, vec, seq)
    return jax.shard_map(
        spread,
        mesh=mesh,
        in_specs=placed,
        out_specs=(seq, seq, mat, vec, mat, vec, mat, vec, mat, vec, vec, vec),
        check_vma=False,
    )
```

```python
import functools

import jax
import jax.numpy as jnp
import numpy as np
from jax import lax
from jax.experimental import pallas as pl
from jax.experimental.pallas import tpu as pltpu
from jax.sharding import PartitionSpec as P

HEADS = 16
ROT = 32
epsilon = 1e-05
BOTH = ("dp", "ctx")
MESH = pl.DeviceIdType.MESH


def angles(positions, rotary):
    freq_table = 1.0 / 10000.0 ** (jnp.arange(0, rotary, 2, dtype=jnp.float32) / rotary)
    theta = positions.astype(jnp.float32)[:, None] * freq_table[None, :]
    return (jnp.cos(theta)[:, None, :], jnp.sin(theta)[:, None, :])


def rotate(tensor, cosine, sine_table, rotary):
    half_len = rotary // 2
    first_half = tensor[..., :half_len]
    second_half = tensor[..., half_len:rotary]
    return jnp.concatenate(
        [
            first_half * cosine - second_half * sine_table,
            second_half * cosine + first_half * sine_table,
            tensor[..., rotary:],
        ],
        axis=-1,
    )


def contract_rows(left, right):
    return lax.dot_general(
        left, right, (((0,), (0,)), ((), ())), preferred_element_type=jnp.float32
    )


def times_transposed(left, right):
    return lax.dot_general(
        left, right, (((1,), (1,)), ((), ())), preferred_element_type=jnp.float32
    )


def times(left, right):
    return jnp.dot(left, right, preferred_element_type=jnp.float32)


def gelu_tanh(hidden_in):
    return jax.nn.gelu(hidden_in, approximate=True)


def normalise(inputs):
    center = inputs - jnp.mean(inputs, axis=-1, keepdims=True)
    inverse = lax.rsqrt(jnp.mean(center * center, axis=-1, keepdims=True) + epsilon)
    return center * inverse, inverse


def attention(q, k, v, segments, back, cosine, sine):
    length, head_dim = q.shape[1], q.shape[3]
    scale = float(head_dim) ** (-0.5)
    index = jnp.arange(length, dtype=jnp.int32)
    allowed = (segments[:, :, None] == segments[:, None, :]) & (index[None, :] <= index[:, None])[
        None
    ]
    scores = jnp.einsum("sqhd,skhd->shqk", q, k, preferred_element_type=jnp.float32) * scale
    scores = jnp.where(allowed[:, None], scores, -1e30)
    row_max = jnp.max(scores, axis=-1, keepdims=True)
    log_total = row_max + jnp.log(jnp.sum(jnp.exp(scores - row_max), axis=-1, keepdims=True))
    probs = jnp.exp(scores - log_total)
    probs_low = probs.astype(jnp.bfloat16)
    attended = jnp.einsum("shqk,skhd->sqhd", probs_low, v, preferred_element_type=jnp.float32)

    def backward(grad_attended):
        grad_weights = jnp.einsum(
            "sqhd,skhd->shqk", grad_attended, v, preferred_element_type=jnp.float32
        )
        row_dot = jnp.sum(grad_weights * probs, axis=-1, keepdims=True)
        grad_scores = (probs * (grad_weights - row_dot)).astype(jnp.bfloat16)
        grad_q = (
            jnp.einsum("shqk,skhd->sqhd", grad_scores, k, preferred_element_type=jnp.float32)
            * scale
        )
        grad_k = (
            jnp.einsum("shqk,sqhd->skhd", grad_scores, q, preferred_element_type=jnp.float32)
            * scale
        )
        grad_v = jnp.einsum(
            "shqk,sqhd->skhd", probs_low, grad_attended, preferred_element_type=jnp.float32
        )
        return grad_q, grad_k, grad_v

    return attended, backward


def local(
    dp,
    ctx,
    tokens,
    segments,
    qkv_weight,
    qkv_bias,
    out_weight,
    out_bias,
    fc1_weight,
    fc1_bias,
    fc2_weight,
    fc2_bias,
    norm_gain,
    norm_shift,
    cotangent,
):
    f32, b16 = jnp.float32, jnp.bfloat16
    seqs, part, width = tokens.shape
    length = part * ctx
    rows = seqs * length
    ff = fc1_weight.shape[1]
    fl, dl = ff // ctx, width // ctx
    heads = HEADS // ctx
    head_dim = width // HEADS
    wr, fr = qkv_weight.shape[0], fc2_weight.shape[0]
    mine = lax.axis_index("ctx")
    devices = dp * ctx

    pieces = [qkv_bias, fc1_bias, out_bias, fc2_bias, norm_gain, norm_shift]
    marks = [0]
    for piece in pieces:
        marks.append(marks[-1] + piece.shape[0])
    small = lax.all_gather(jnp.concatenate(pieces), BOTH, axis=0)
    parts = [small[:, a:b] for a, b in zip(marks, marks[1:])]
    b_qkv = lax.dynamic_index_in_dim(
        parts[0].reshape(3, ctx, dl), mine, 1, keepdims=False
    ).reshape(3 * dl)
    b_fc1 = lax.dynamic_index_in_dim(
        parts[1].reshape(dp, ctx, fr), mine, 1, keepdims=False
    ).reshape(fl)
    b_out, b_fc2, gain, shift = [p.reshape(width).astype(f32) for p in parts[2:]]

    send_qkv = jnp.moveaxis(qkv_weight.reshape(wr, 3, ctx, dl), 2, 0).reshape(ctx, wr, 3 * dl)
    send_fc1 = jnp.moveaxis(fc1_weight.reshape(wr, dp, ctx, fr), 2, 0).reshape(ctx, wr, fl)
    sent = lax.all_to_all(
        jnp.concatenate([send_qkv, send_fc1], axis=2), "ctx", split_axis=0, concat_axis=0
    )
    out_perm = [(b, (b % dp) * ctx + b // dp) for b in range(devices)]
    out_back = [(j, i) for i, j in out_perm]
    out_piece = lax.ppermute(out_weight, BOTH, out_perm)
    w_qkv = lax.all_gather(sent[:, :, : 3 * dl], "dp", axis=0).reshape(width, 3 * dl)
    w_fc1 = lax.all_gather(sent[:, :, 3 * dl :], "dp", axis=0).reshape(width, fl)
    w_fc2 = lax.all_gather(fc2_weight, "dp", axis=0).reshape(fl, width)
    w_out = lax.all_gather(out_piece, "dp", axis=0).reshape(dl, width)

    tokens_all = lax.all_gather(tokens, "ctx", axis=1, tiled=True)
    cot_all = lax.all_gather(cotangent, "ctx", axis=1, tiled=True)

    positions = jnp.arange(length, dtype=jnp.int32)
    cosine, sine = angles(positions, ROT)

    scaled_all, _ = normalise(tokens_all.astype(f32).reshape(rows, width))
    normed = (scaled_all * gain + shift).astype(b16)
    grad_out = cot_all.reshape(rows, width)

    mixed = times(normed, w_qkv) + b_qkv.astype(f32)
    shape4 = (seqs, length, heads, head_dim)
    q = rotate(mixed[:, :dl].reshape(shape4), cosine, sine, ROT).astype(b16)
    k = rotate(mixed[:, dl : 2 * dl].reshape(shape4), cosine, sine, ROT).astype(b16)
    v = mixed[:, 2 * dl :].astype(b16).reshape(shape4)
    attended, attention_back = attention(q, k, v, segments, None, cosine, sine)
    attended = attended.reshape(rows, dl).astype(b16)

    hidden = times(normed, w_fc1) + b_fc1.astype(f32)
    act, gelu_back = jax.vjp(gelu_tanh, hidden)
    act = act.astype(b16)
    partial = times(attended, w_out) + times(act, w_fc2)
    summed = lax.psum_scatter(
        partial.astype(b16).reshape(seqs, length, width), "ctx", scatter_dimension=1, tiled=True
    )
    result = (tokens.astype(f32) + summed.astype(f32) + (b_out + b_fc2)).astype(b16)

    grad_act = times_transposed(grad_out, w_fc2)
    grad_hidden = gelu_back(grad_act)[0].astype(b16)
    grad_fc2 = contract_rows(act, grad_out)
    grad_fc2 = lax.psum_scatter(grad_fc2.astype(b16), "dp", scatter_dimension=0, tiled=True)
    grad_fc1 = contract_rows(normed, grad_hidden)
    grad_fc1_b = jnp.sum(grad_hidden, axis=0, dtype=f32)
    grad_fc1 = lax.psum_scatter(grad_fc1.astype(b16), "dp", scatter_dimension=0, tiled=True)
    grad_out_w = contract_rows(attended, grad_out)
    grad_out_w = lax.psum_scatter(grad_out_w.astype(b16), "dp", scatter_dimension=0, tiled=True)
    grad_attended = times_transposed(grad_out, w_out).astype(b16).reshape(shape4)
    grad_q, grad_k, grad_v = attention_back(grad_attended)
    grad_mixed = jnp.concatenate(
        [
            rotate(grad_q, cosine, -sine, ROT).reshape(rows, dl),
            rotate(grad_k, cosine, -sine, ROT).reshape(rows, dl),
            grad_v.reshape(rows, dl),
        ],
        axis=1,
    ).astype(b16)
    grad_normed = times_transposed(grad_hidden, w_fc1) + times_transposed(grad_mixed, w_qkv)
    grad_normed = lax.psum_scatter(
        grad_normed.astype(b16).reshape(seqs, length, width), "ctx", scatter_dimension=1, tiled=True
    ).astype(f32)
    grad_qkv = contract_rows(normed, grad_mixed)
    grad_qkv_b = jnp.sum(grad_mixed, axis=0, dtype=f32)
    grad_qkv = lax.psum_scatter(grad_qkv.astype(b16), "dp", scatter_dimension=0, tiled=True)

    back = lax.all_to_all(
        jnp.concatenate([grad_qkv, grad_fc1], axis=1).reshape(ctx, wr, 3 * dl + fl),
        "ctx",
        split_axis=0,
        concat_axis=0,
    ).astype(f32)
    grad_qkv = jnp.moveaxis(back[:, :, : 3 * dl].reshape(ctx, wr, 3, dl), 0, 2).reshape(
        wr, 3 * width
    )
    grad_fc1 = jnp.moveaxis(back[:, :, 3 * dl :].reshape(ctx, wr, dp, fr), 0, 2).reshape(wr, ff)
    grad_out_w = lax.ppermute(grad_out_w, BOTH, out_back).astype(f32)
    grad_fc2 = grad_fc2.astype(f32)

    grad_normed = grad_normed.reshape(seqs, part, width)
    own = tokens.astype(f32)
    cot = cotangent.astype(f32)
    scaled, inverse = normalise(own)
    grad_gain = jnp.sum(grad_normed * scaled, axis=(0, 1))
    grad_shift = jnp.sum(grad_normed, axis=(0, 1))
    grad_scaled = grad_normed * gain
    grad_input = inverse * (
        grad_scaled
        - jnp.mean(grad_scaled, axis=-1, keepdims=True)
        - scaled * jnp.mean(grad_scaled * scaled, axis=-1, keepdims=True)
    )
    grad_tokens = (cot + grad_input).astype(b16)

    wide_qkv_b = lax.dynamic_update_index_in_dim(
        jnp.zeros((3, ctx, dl), f32), grad_qkv_b.reshape(3, dl), mine, 1
    )
    wide_fc1_b = lax.dynamic_update_index_in_dim(
        jnp.zeros((dp, ctx, fr), f32), grad_fc1_b.reshape(dp, fr), mine, 1
    )
    bias_out = jnp.sum(cot, axis=(0, 1))
    sums = jnp.concatenate(
        [
            x.reshape(devices, -1)
            for x in (wide_qkv_b, wide_fc1_b, bias_out, grad_gain, grad_shift)
        ],
        axis=1,
    )
    sums = lax.psum_scatter(sums, BOTH, scatter_dimension=0, tiled=True)[0]
    at = [0, marks[1], marks[2], marks[3], marks[3] + wr, marks[3] + 2 * wr]
    g_qkv_b, g_fc1_b, g_bias, g_gain, g_shift = [sums[a:b] for a, b in zip(at, at[1:])]
    return (
        result,
        grad_tokens,
        grad_qkv,
        g_qkv_b,
        grad_out_w,
        g_bias,
        grad_fc1,
        g_fc1_b,
        grad_fc2,
        g_bias,
        g_gain,
        g_shift,
    )


def dot(left, right, contract):
    return lax.dot_general(
        left, right, ((contract[:1], contract[1:]), ((), ())), preferred_element_type=jnp.float32
    )


NORMAL, RIGHT_T, LEFT_T = (1, 0), (1, 1), (0, 0)


def turn_tables(length, head_dim, lanes):
    half = ROT // 2
    freq = np.float32(1.0) / np.power(
        np.float32(10000.0), np.arange(0, ROT, 2, dtype=np.float32) / np.float32(ROT)
    )
    theta = np.arange(length, dtype=np.float32)[:, None] * freq[None, :]
    cosine, sine = np.cos(theta), np.sin(theta)
    keep = np.ones((length, head_dim), np.float32)
    keep[:, :half] = cosine
    keep[:, half:ROT] = cosine
    ahead = np.zeros((length, head_dim), np.float32)
    ahead[:, :half] = -sine
    behind = np.zeros((length, head_dim), np.float32)
    behind[:, half:ROT] = sine
    return [np.tile(t, (1, lanes // head_dim)) for t in (keep, ahead, behind)]


def turn(x, keep, ahead, behind):
    half, lanes = ROT // 2, x.shape[1]
    return (
        x * keep
        + pltpu.roll(x, lanes - half, axis=1) * ahead
        + pltpu.roll(x, half, axis=1) * behind
    )


DELTAS = (-2, 2, -1, 1)
SLOTS = (0, 0, 1, 2)
PASSED = 4


def layer_kernel(
    nz, nc, marks,
    tok_ref, cot_ref, qkv_ref, fc1_ref, fc2_ref, out_ref, small_ref,
    seg_ref, keep_hbm, ahead_hbm, behind_hbm,
    o_result, o_tokens, o_qkv, o_out, o_fc1, o_fc2, o_sums,
    tok_all, cot_all, w_qkv, w_fc1, w_fc2, w_out, small_all,
    small_rows, vec_d, b_qkv, b_fc1, normed, q_s, k_s, v_s, attended, g_att, act, slope, gmixed,
    acc_q, acc_k, acc_v, acc_a, bias_s, g_hidden,
    give_qkv, give_fc1, give_fc2, give_out, got_qkv, got_fc1, got_fc2, got_out,
    own_qkv, own_fc1, own_fc2, own_out_g, far_qkv, far_fc1, far_fc2, far_out,
    pass_qkv, pass_fc1, pass_fc2, pass_out, log_s, seg_col, keep_ref, ahead_ref, behind_ref,
    part_got, part_own, norm_got, norm_own,
    swap_qkv, swap_fc1, swapped_qkv, swapped_fc1, out_planes, give_column, own_column, column_got,
    sums, sums_sib, sums_z, held,
    ctx_send, ctx_recv, z_send, z_recv, sib_send, sib_recv, loc,
    back_z_send, back_z_recv, back_sib_send, back_sib_recv, back_ctx_send, back_ctx_recv,
):
    f32, b16 = jnp.float32, jnp.bfloat16
    d, c = lax.axis_index("dp"), lax.axis_index("ctx")
    z, k = d // 2, lax.rem(d, 2)
    other = 2 * z + 1 - k
    wr, width = out_ref.shape
    dl = width // nc
    fr = fc2_ref.shape[0]
    nd = 2 * nz
    part = tok_ref.shape[0]
    length = part * nc
    head_dim = width // HEADS
    heads = HEADS // nc
    fl = nd * fr

    def ctx_to(j):
        return lax.rem(c + j, nc)

    def ctx_from(j):
        return lax.rem(c + nc - j, nc)

    def exists(delta):
        return (z + delta >= 0) & (z + delta < nz)

    def plane(delta):
        return 2 * jnp.clip(z + delta, 0, nz - 1) + k

    barrier = pltpu.get_barrier_semaphore()
    for j in range(1, nc):
        pl.semaphore_signal(barrier, inc=1, device_id=(d, ctx_to(j)), device_id_type=MESH)
    for delta in DELTAS:
        @pl.when(exists(delta))
        def _():
            pl.semaphore_signal(barrier, inc=1, device_id=(plane(delta), c), device_id_type=MESH)
    pl.semaphore_signal(barrier, inc=1, device_id=(other, c), device_id_type=MESH)
    planes = jnp.minimum(z, 2) + jnp.minimum(nz - 1 - z, 2)
    pl.semaphore_wait(barrier, nc + planes)

    def remote(src, dst, send, recv, device):
        return pltpu.make_async_remote_copy(
            src_ref=src, dst_ref=dst, send_sem=send, recv_sem=recv,
            device_id=device, device_id_type=MESH,
        )

    def rows(at):
        return pl.ds(pl.multiple_of(at * wr, wr), wr)

    def lanes(at, size):
        return pl.ds(pl.multiple_of(at * size, size), size)

    SMALL, QKV, FC1, TOK, COT, OUT, FC2 = range(7)

    def ctx_pieces(array, to):
        if array == SMALL:
            return [(small_ref, small_all.at[d, c])]
        if array == QKV:
            return [
                (qkv_ref.at[:, lanes(t * nc + to, dl)], w_qkv.at[d, rows(c), pl.ds(t * dl, dl)])
                for t in range(3)
            ]
        if array == FC1:
            return [
                (fc1_ref.at[:, lanes(g * nc + to, fr)], w_fc1.at[d, rows(c), pl.ds(g * fr, fr)])
                for g in range(nd)
            ]
        if array == TOK:
            return [(tok_ref, tok_all.at[c])]
        return [(cot_ref, cot_all.at[c])]

    def ctx_whole(array, sub):
        return {
            SMALL: lambda: small_all.at[d, sub],
            QKV: lambda: w_qkv.at[d, rows(sub), :],
            FC1: lambda: w_fc1.at[d, rows(sub), :],
            TOK: lambda: tok_all.at[sub],
            COT: lambda: cot_all.at[sub],
        }[array]()

    def ctx_start(array):
        for j in range(1, nc):
            for src, dst in ctx_pieces(array, ctx_to(j)):
                remote(src, dst, ctx_send.at[array, j], ctx_recv.at[array, j], (d, ctx_to(j))).start()
        for src, dst in ctx_pieces(array, c):
            pltpu.make_async_copy(src, dst, loc.at[array]).start()

    def ctx_arrive(array, j):
        got = ctx_whole(array, ctx_from(j))
        if j == 0:
            pltpu.make_async_copy(got, got, loc.at[array]).wait()
        else:
            remote(got, got, ctx_send.at[array, j], ctx_recv.at[array, j], (d, ctx_to(j))).wait_recv()

    def ctx_sent(array):
        for j in range(1, nc):
            got = ctx_whole(array, ctx_from(j))
            remote(got, got, ctx_send.at[array, j], ctx_recv.at[array, j], (d, ctx_to(j))).wait_send()

    def ctx_finish(array):
        for j in range(nc):
            ctx_arrive(array, j)

    side, across, corner = c + 1 - 2 * lax.rem(c, 2), lax.rem(c + 2, nc), nc - 1 - c
    first_half, second_half = pl.ds(0, part // 2), pl.ds(part // 2, part // 2)

    def pair_copy(array, n):
        store = tok_all if array == TOK else cot_all
        src = tok_ref if array == TOK else cot_ref
        if n == 1:
            dst, to = store.at[c], side
        elif n == 2:
            dst, to = store.at[c], across
        elif n == 3:
            src = store.at[side, first_half, :]
            dst, to = src, across
        else:
            src = store.at[across, second_half, :]
            dst, to = src, side
        return remote(src, dst, ctx_send.at[array, n], ctx_recv.at[array, n], (d, to))

    def pair_start(array):
        store, src = (tok_all, tok_ref) if array == TOK else (cot_all, cot_ref)
        pair_copy(array, 1).start()
        pair_copy(array, 2).start()
        pltpu.make_async_copy(src, store.at[c], loc.at[array]).start()

    def pair_got(array, n):
        store = tok_all if array == TOK else cot_all
        got = {
            0: lambda: store.at[corner, second_half, :],
            1: lambda: store.at[side],
            2: lambda: store.at[across],
            3: lambda: store.at[corner, first_half, :],
        }[n]()
        remote(got, got, ctx_send.at[array, n], ctx_recv.at[array, n], (d, side)).wait_recv()

    def pair_forward(array):
        pair_got(array, 1)
        pair_copy(array, 3).start()
        pair_got(array, 2)
        pair_copy(array, 0).start()

    def pair_own(array):
        store = tok_all if array == TOK else cot_all
        pltpu.make_async_copy(store.at[c], store.at[c], loc.at[array]).wait()

    def block_of(array, at):
        if array == OUT:
            return out_planes.at[lax.div(at, 2)]
        return {SMALL: small_all, QKV: w_qkv, FC1: w_fc1, FC2: w_fc2}[array].at[at]

    near_low, near_high = z == 1, z == nz - 2

    def z_copy(array, n, delta, owner):
        block = block_of(array, owner)
        src = block
        if array in (FC2, OUT) and n < PASSED:
            src = fc2_ref if array == FC2 else out_ref
        return remote(src, block, z_send.at[array, n], z_recv.at[array, n], (plane(delta), c))

    def z_got(array, n, owner):
        block = block_of(array, owner)
        return remote(block, block, z_send.at[array, n], z_recv.at[array, n], (d, c))

    def sib_copy(array, at):
        block = block_of(array, 2 * at + k)
        return remote(block, block, sib_send.at[array, at], sib_recv.at[array, at], (other, c))

    def z_own(array):
        for n, delta in enumerate(DELTAS):
            @pl.when(exists(delta))
            def _():
                z_copy(array, n, delta, d).start()
        if array not in (FC2, OUT):
            sib_copy(array, z).start()

    def z_forward(array):
        @pl.when(near_high)
        def _():
            z_got(array, DELTAS.index(2), k).wait_recv()
            z_copy(array, PASSED, 1, k).start()

        @pl.when(near_low)
        def _():
            z_got(array, DELTAS.index(-2), d + 4).wait_recv()
            z_copy(array, PASSED, -1, d + 4).start()

    def z_arrive(array):
        for n, delta in enumerate(DELTAS):
            done = near_high if delta == 2 else near_low if delta == -2 else None
            wanted = exists(-delta) if done is None else exists(-delta) & jnp.logical_not(done)

            @pl.when(wanted)
            def _():
                z_got(array, n, plane(-delta)).wait_recv()

        @pl.when(z == 0)
        def _():
            z_got(array, PASSED, 2 * (nz - 1) + k).wait_recv()

        @pl.when(z == nz - 1)
        def _():
            z_got(array, PASSED, k).wait_recv()

        if array == OUT:
            return
        for at in range(nz):
            if array == FC2:
                sib_copy(array, at).start()
            else:
                @pl.when(z != at)
                def _():
                    sib_copy(array, at).start()

    def z_finish(array):
        for at in range(nz):
            block = block_of(array, 2 * at + 1 - k)
            remote(block, block, sib_send.at[array, at], sib_recv.at[array, at], (other, c)).wait_recv()

    def z_sent(array):
        for n, delta in enumerate(DELTAS):
            @pl.when(exists(delta))
            def _():
                z_copy(array, n, delta, d).wait_send()

        @pl.when(near_high | near_low)
        def _():
            z_copy(array, PASSED, 1, k).wait_send()

        if array != OUT:
            for at in range(nz):
                sib_copy(array, at).wait_send()

    def out_copy(j, to, sub):
        piece = out_planes.at[to]
        return remote(piece, w_out.at[k, rows(sub), :], ctx_send.at[OUT, j], ctx_recv.at[OUT, j], (d, to))

    def own_out():
        return pltpu.make_async_copy(out_planes.at[c], w_out.at[k, rows(c), :], loc.at[OUT])

    def out_sib(which):
        piece = w_out.at[which]
        return remote(piece, piece, sib_send.at[OUT, 0], sib_recv.at[OUT, 0], (other, c))

    ctx_start(SMALL)
    ctx_start(QKV)
    z_own(OUT)
    tables = [(keep_hbm, keep_ref), (ahead_hbm, ahead_ref), (behind_hbm, behind_ref)]
    tables = [pltpu.make_async_copy(a, b, loc.at[8 + n]) for n, (a, b) in enumerate(tables)]
    for copy in tables:
        copy.start()
    copy_out = pltpu.make_async_copy(out_ref, out_planes.at[z], loc.at[7])
    copy_out.start()
    ctx_start(FC1)
    pair_start(TOK)
    copy_fc2 = pltpu.make_async_copy(fc2_ref, w_fc2.at[d], loc.at[FC2])
    copy_fc2.start()

    ctx_finish(SMALL)
    z_own(SMALL)
    ctx_finish(QKV)
    z_own(QKV)
    z_forward(OUT)
    z_forward(SMALL)
    ctx_finish(FC1)
    z_own(FC1)
    z_arrive(OUT)
    copy_out.wait()
    own_out().start()
    for j in range(1, nc):
        out_copy(j, ctx_to(j), c).start()
    pair_start(COT)
    z_arrive(SMALL)
    z_forward(QKV)
    z_own(FC2)
    z_finish(SMALL)

    def collect(p, carry):
        small_rows[pl.ds(p, 1), :] = small_all[p // nc, lax.rem(p, nc)]
        return carry

    lax.fori_loop(0, nd * nc, collect, 0)
    table = small_rows[...]
    pack = table.shape[1]

    def vector(mark, size, first, count):
        entry = lax.broadcasted_iota(jnp.int32, (1, count), 1).astype(f32) + first
        owner = jnp.floor((entry + 0.5) * (1.0 / size))
        lane = entry - owner * size + mark
        pick = lax.broadcasted_iota(jnp.int32, (pack, count), 0).astype(f32) == lane
        found = dot(table.astype(b16), jnp.where(pick, 1.0, 0.0).astype(b16), NORMAL)
        here = lax.broadcasted_iota(jnp.int32, (nd * nc, count), 0).astype(f32) == owner
        return jnp.sum(jnp.where(here, found, 0.0), axis=0, keepdims=True)

    for i in range(2):
        vec_d[pl.ds(i, 1), :] = vector(marks[2 + i], wr, 0.0, width)
    vec_d[2:3, :] = vector(marks[4], wr, 0.0, width) + vector(marks[5], wr, 0.0, width)
    for t in range(3):
        b_qkv[:, pl.ds(t * dl, dl)] = vector(marks[1], 3 * wr, (t * width + c * dl).astype(f32), dl)
    for g in range(nd):
        b_fc1[:, pl.ds(g * fr, fr)] = small_all[g, c][:, :fr]

    z_arrive(QKV)
    z_finish(QKV)

    seg_col[...] = jnp.broadcast_to(seg_ref[...].astype(f32), (128, length)).T

    chunk = 32

    def block_rows(b):
        return pl.ds(pl.multiple_of(b * part, part), part)

    def normalise_block(b):
        def step(i, carry):
            at = pl.multiple_of(i * chunk, chunk)
            x = tok_all[b, pl.ds(at, chunk), :].astype(f32)
            x = x - jnp.mean(x, axis=-1, keepdims=True)
            x = x * lax.rsqrt(jnp.mean(x * x, axis=-1, keepdims=True) + epsilon)
            normed[pl.ds(pl.multiple_of(b * part, part) + at, chunk), :] = (
                x * vec_d[0:1, :] + vec_d[1:2, :]
            ).astype(b16)
            return carry

        lax.fori_loop(0, part // chunk, step, 0)

    def qkv_block(b):
        at = block_rows(b)
        x = normed[at, :]
        keep = jnp.tile(keep_ref[at, :], (1, dl // keep_ref.shape[1]))
        ahead = jnp.tile(ahead_ref[at, :], (1, dl // keep_ref.shape[1]))
        behind = jnp.tile(behind_ref[at, :], (1, dl // keep_ref.shape[1]))
        for t, to in enumerate((q_s, k_s, v_s)):
            w = w_qkv[:, :, pl.ds(t * dl, dl)].reshape(width, dl)
            y = dot(x, w, NORMAL) + b_qkv[:, pl.ds(t * dl, dl)]
            if t < 2:
                y = turn(y, keep, ahead, behind)
            to[at, :] = y.astype(b16)

    for copy in tables:
        copy.wait()
    pair_own(TOK)
    normalise_block(c)
    qkv_block(c)
    pair_forward(TOK)
    normalise_block(side)
    qkv_block(side)
    normalise_block(across)
    qkv_block(across)
    pair_got(TOK, 3)
    pair_got(TOK, 0)
    normalise_block(corner)
    qkv_block(corner)

    z_forward(FC1)
    pair_forward(COT)

    tile = 256
    reach = 512 // tile
    scale = float(head_dim) ** (-0.5)

    def spans(i):
        first = max(0, i - reach) * tile
        count = (i + 1) * tile - first
        return pl.ds(i * tile, tile), pl.ds(first, count), count

    def mask(i):
        at, to, count = spans(i)
        same = seg_col[at, :1] == seg_ref[:1, to].astype(f32)
        row = lax.broadcasted_iota(jnp.int32, (tile, count), 0) + (tile * i - to.start)
        col = lax.broadcasted_iota(jnp.int32, (tile, count), 1)
        bias_s[:, :count] = jnp.where(same & (col <= row), 0.0, -1e30)

    def only_head(h):
        lane = lax.broadcasted_iota(jnp.int32, (1, dl), 1)
        return jnp.where((lane >= h * head_dim) & (lane < (h + 1) * head_dim), 1.0, 0.0)

    for i in range(length // tile):
        at, to, count = spans(i)
        mask(i)
        acc_a[...] = jnp.zeros_like(acc_a)

        def forward_step(h, carry):
            only = only_head(h)
            s = dot(q_s[at, :] * only.astype(b16), k_s[to, :], RIGHT_T) * scale + bias_s[:, :count]
            top = jnp.max(s, axis=-1, keepdims=True)
            e = jnp.exp(s - top)
            sum_e = jnp.sum(e, axis=-1, keepdims=True)
            log_s[h, at, :] = top + jnp.log(sum_e)
            p_low = (e * (1.0 / sum_e)).astype(b16)
            acc_a[...] += dot(p_low, v_s[to, :], NORMAL) * only
            return carry

        lax.fori_loop(0, heads, forward_step, 0, unroll=True)
        attended[at, :] = acc_a[...].astype(b16)

    z_arrive(FC1)
    z_finish(FC1)

    def hidden_block(b, carry):
        at = block_rows(b)
        x = normed[at, :]
        for g in range(0, fl, 256):
            w = w_fc1[:, :, pl.ds(g, 256)].reshape(width, 256)
            h = dot(x, w, NORMAL) + b_fc1[:, pl.ds(g, 256)]
            s = h * h
            t = jnp.tanh(h * (0.7978845608028654 + (0.7978845608028654 * 0.044715) * s))
            half_t = 0.5 + 0.5 * t
            act[at, pl.ds(g, 256)] = (h * half_t).astype(b16)
            slope[at, pl.ds(g, 256)] = half_t + 0.5 * h * (1.0 - t * t) * (
                0.7978845608028654 + (3 * 0.7978845608028654 * 0.044715) * s
            )
        return carry

    lax.fori_loop(0, nc, hidden_block, 0)

    z_forward(FC2)
    pair_own(COT)
    pair_got(COT, 3)
    pair_got(COT, 0)

    COLUMN = 7
    gives = {QKV: give_qkv, FC1: give_fc1, FC2: give_fc2, OUT: give_out, COLUMN: give_column}
    gots = {QKV: got_qkv, FC1: got_fc1, FC2: got_fc2, OUT: got_out}
    owns = {QKV: own_qkv, FC1: own_fc1, FC2: own_fc2, OUT: own_out_g, COLUMN: own_column}
    fars = {QKV: far_qkv, FC1: far_fc1, FC2: far_fc2, COLUMN: far_out}
    passes = {QKV: pass_qkv, FC1: pass_fc1, FC2: pass_fc2, COLUMN: pass_out}

    def cotangents():
        return cot_all[...].reshape(length, width)

    def weight_gradient(array, left, right):
        give, own = gives[array], owns[array]
        size = give.shape[1]

        def step(i, carry):
            both = dot(left[:, lanes(i, 2 * size)], right(), LEFT_T)
            low, high = both[:size], both[size:]
            own[i] = jnp.where(k == 0, low, high)
            give[i] = jnp.where(k == 0, high, low).astype(b16)
            return carry

        lax.fori_loop(0, give.shape[0], step, 0)
        to_sibling(array).start()

    def to_sibling(array):
        return remote(
            gives[array], gots[array], back_sib_send.at[array], back_sib_recv.at[array], (other, c)
        )

    def to_owner(array, n, delta):
        block = gives[array].at[jnp.clip(z + delta, 0, nz - 1)]
        return remote(
            block, fars[array].at[SLOTS[n]], back_z_send.at[array, n], back_z_recv.at[array, n], (plane(delta), c)
        )

    def to_pass(array, delta):
        block = gives[array].at[jnp.clip(z + 3 * delta, 0, nz - 1)]
        return remote(
            block, passes[array], back_z_send.at[array, PASSED], back_z_recv.at[array, PASSED], (plane(delta), c)
        )

    def both_cores(array, at):
        if array == COLUMN:
            return own_column[at]
        return owns[array][at] + gots[array][at].astype(f32)

    def send_back(array):
        for delta in (-1, 1):
            far = jnp.clip(z + 3 * delta, 0, nz - 1)

            @pl.when(z == (nz - 1 if delta < 0 else 0))
            def _():
                gives[array][far] = both_cores(array, far).astype(b16)
                to_pass(array, delta).start()
        for n, delta in enumerate(DELTAS):
            hold = {-2: near_high, 2: near_low}.get(delta)
            go = exists(delta) if hold is None else exists(delta) & jnp.logical_not(hold)
            at = jnp.clip(z + delta, 0, nz - 1)

            @pl.when(go)
            def _():
                gives[array][at] = both_cores(array, at).astype(b16)
                to_owner(array, n, delta).start()

    def add_sibling(array):
        to_sibling(array).wait()
        send_back(array)

    def pass_back(array):
        for near, delta in ((near_high, -2), (near_low, 2)):
            at = jnp.clip(z + delta, 0, nz - 1)

            @pl.when(near)
            def _():
                to_pass(array, delta).wait_recv()
                gives[array][at] = (both_cores(array, at) + passes[array][...].astype(f32)).astype(b16)
                to_owner(array, DELTAS.index(delta), delta).start()

    def gather_total(array):
        own = owns[array]
        own[z] = both_cores(array, z)
        for n, delta in enumerate(DELTAS):
            @pl.when(exists(-delta))
            def _():
                to_owner(array, n, delta).wait_recv()
                own[z] = own[z] + fars[array][SLOTS[n]].astype(f32)

    def owner_sent(array):
        for n, delta in enumerate(DELTAS):
            @pl.when(exists(delta))
            def _():
                to_owner(array, n, delta).wait_send()
        for delta in (-1, 1):
            @pl.when(z == (nz - 1 if delta < 0 else 0))
            def _():
                to_pass(array, delta).wait_send()

    def column_copy(j, to):
        return remote(
            give_out.at[0, rows(to), :], column_got.at[c], back_ctx_send.at[OUT, j], back_ctx_recv.at[OUT, j], (d, to)
        )

    def to_columns():
        to_sibling(OUT).wait()
        own_out_g[0] = own_out_g[0] + got_out[0].astype(f32)
        give_out[0] = own_out_g[0].astype(b16)
        for j in range(1, nc):
            column_copy(j, ctx_to(j)).start()
        own_column[c] = own_out_g[0, rows(c), :]

    def from_columns():
        for j in range(1, nc):
            source = ctx_from(j)
            got = column_got.at[source]
            remote(got, got, back_ctx_send.at[OUT, j], back_ctx_recv.at[OUT, j], (d, source)).wait_recv()
            own_column[source] = column_got[source].astype(f32)
        send_back(COLUMN)

    PART, NORM, SUMS = TOK, COT, SMALL

    def over_ctx(array, src, dst, j, to):
        return remote(src, dst, back_ctx_send.at[array, j], back_ctx_recv.at[array, j], (d, to))

    half_rows = part // 2
    terms = {PART: (tok_all, part_got, part_own), NORM: (cot_all, norm_got, norm_own)}

    def term_copy(array, n):
        store, got, _ = terms[array]
        whose, at, slot, to = (
            (corner, first_half, 2, side),
            (corner, second_half, 2, across),
            (side, first_half, 0, side),
            (side, second_half, 0, side),
            (across, second_half, 1, across),
            (across, first_half, 1, across),
        )[n]
        return remote(
            store.at[whose, at, :], got.at[slot, at, :], back_ctx_send.at[array, n], back_ctx_recv.at[array, n], (d, to)
        )

    def send_terms(array, term):
        store, _, own = terms[array]
        store[corner] = term(corner).astype(b16)
        term_copy(array, 0).start()
        term_copy(array, 1).start()
        x = term(side)
        store[side, first_half, :] = x[:half_rows].astype(b16)
        held[0] = x[half_rows:]
        term_copy(array, 2).start()
        x = term(across)
        store[across, second_half, :] = x[half_rows:].astype(b16)
        held[1] = x[:half_rows]
        term_copy(array, 4).start()
        own[...] = term(c)

    def pass_terms(array):
        store, got, _ = terms[array]
        term_copy(array, 1).wait_recv()
        store[side, second_half, :] = (held[0] + got[2, second_half, :].astype(f32)).astype(b16)
        term_copy(array, 3).start()
        term_copy(array, 0).wait_recv()
        store[across, first_half, :] = (held[1] + got[2, first_half, :].astype(f32)).astype(b16)
        term_copy(array, 5).start()

    def terms_arrive(array):
        for n in range(2, 6):
            term_copy(array, n).wait_recv()

    weight_gradient(FC2, act, cotangents)
    weight_gradient(OUT, attended, cotangents)

    own_out().wait()
    for j in range(1, nc):
        out_copy(j, ctx_to(j), ctx_from(j)).wait_recv()
    out_sib(k).start()
    out_sib(1 - k).wait_recv()

    w_o = w_out[...].reshape(dl, width)

    def g_att_block(b, carry):
        g_att[block_rows(b), :] = dot(cot_all[b], w_o, RIGHT_T).astype(b16)
        return carry

    lax.fori_loop(0, nc, g_att_block, 0)
    add_sibling(FC2)
    to_columns()

    acc_k[...] = jnp.zeros_like(acc_k)
    acc_v[...] = jnp.zeros_like(acc_v)
    wide = (1, dl // keep_ref.shape[1])
    def attend_back(i):
        at, to, count = spans(i)
        mask(i)
        acc_q[...] = jnp.zeros_like(acc_q)

        def backward_step(h, carry):
            only = only_head(h)
            only_low = only.astype(b16)
            qh = q_s[at, :] * only_low
            gh = g_att[at, :] * only_low
            keys, values = k_s[to, :], v_s[to, :]
            p = jnp.exp(dot(qh, keys, RIGHT_T) * scale + bias_s[:, :count] - log_s[h, at, :])
            gw = dot(gh, values, RIGHT_T)
            gs = (p * (gw - jnp.sum(gw * p, axis=-1, keepdims=True))).astype(b16)
            acc_q[...] += dot(gs, keys, NORMAL) * only
            acc_k[to, :] += dot(gs, qh, LEFT_T)
            acc_v[to, :] += dot(p.astype(b16), gh, LEFT_T)
            return carry

        lax.fori_loop(0, heads, backward_step, 0, unroll=True)
        gmixed[at, pl.ds(0, dl)] = turn(
            acc_q[...] * scale,
            jnp.tile(keep_ref[at, :], wide),
            -jnp.tile(ahead_ref[at, :], wide),
            -jnp.tile(behind_ref[at, :], wide),
        ).astype(b16)

    count_tiles = length // tile
    early = count_tiles // 2
    for i in range(early):
        attend_back(i)
    copy_fc2.wait()
    z_arrive(FC2)
    z_finish(FC2)

    def result_term(b):
        at = block_rows(b)
        return dot(attended[at, :], w_out[...].reshape(dl, width), NORMAL) + dot(
            act[at, :], w_fc2[...].reshape(fl, width), NORMAL
        )

    pair_copy(TOK, 3).wait_send()
    pair_copy(TOK, 0).wait_send()
    send_terms(PART, result_term)
    from_columns()
    for i in range(early, count_tiles):
        if i == count_tiles - 1:
            pass_back(FC2)
            pass_terms(PART)
        attend_back(i)

    def finish_block(b, carry):
        at = block_rows(b)
        gmixed[at, pl.ds(dl, dl)] = turn(
            acc_k[at, :] * scale,
            jnp.tile(keep_ref[at, :], wide),
            -jnp.tile(ahead_ref[at, :], wide),
            -jnp.tile(behind_ref[at, :], wide),
        ).astype(b16)
        gmixed[at, pl.ds(2 * dl, dl)] = acc_v[at, :].astype(b16)
        return carry

    lax.fori_loop(0, nc, finish_block, 0)

    weight_gradient(QKV, normed, lambda: gmixed[...])
    ones = jnp.ones((8, length), b16)
    sums[0, :, pl.ds(0, 3 * dl)] = dot(ones, gmixed[...], NORMAL)[:1]
    at_sum = 3 * dl + fl
    sums[0, :, pl.ds(at_sum, width)] = dot(ones[:, :part], cot_all[c], NORMAL)[:1]
    pass_back(COLUMN)
    add_sibling(QKV)

    def hidden_gradient(b, carry):
        at = block_rows(b)
        g = cot_all[b]
        for i in range(nd):
            to = pl.ds(i * fr, fr)
            g_hidden[at, to] = (dot(g, w_fc2[i], RIGHT_T) * slope[at, to]).astype(b16)
        return carry

    lax.fori_loop(0, nc, hidden_gradient, 0)

    def normed_term(b):
        at = block_rows(b)
        return dot(g_hidden[at, :], w_fc1[...].reshape(width, fl), RIGHT_T) + dot(
            gmixed[at, :], w_qkv[...].reshape(width, 3 * dl), RIGHT_T
        )

    pair_copy(COT, 3).wait_send()
    pair_copy(COT, 0).wait_send()
    send_terms(NORM, normed_term)
    pass_back(QKV)
    weight_gradient(FC1, normed, lambda: g_hidden[...])
    sums[0, :, pl.ds(3 * dl, fl)] = dot(ones, g_hidden[...], NORMAL)[:1]
    pass_terms(NORM)
    terms_arrive(PART)

    def result_step(i, carry):
        at = pl.ds(pl.multiple_of(i * chunk, chunk), chunk)
        y = tok_all[c, at, :].astype(f32) + part_own[at, :] + vec_d[2:3, :]
        for n in range(2):
            y = y + part_got[n, at, :].astype(f32)
        o_result[at, :] = y.astype(b16)
        return carry

    lax.fori_loop(0, part // chunk, result_step, 0)
    add_sibling(FC1)
    gather_total(FC2)
    o_fc2[...] = own_fc2[z]

    swaps = {QKV: (swap_qkv, swapped_qkv), FC1: (swap_fc1, swapped_fc1)}

    def place(array, source, x):
        if array == QKV:
            for t in range(3):
                o_qkv[:, lanes(t * nc + source, dl)] = x[:, t * dl : (t + 1) * dl]
        else:
            for g in range(nd):
                o_fc1[:, lanes(g * nc + source, fr)] = x[:, g * fr : (g + 1) * fr]

    def swap_start(array):
        gather_total(array)
        src, dst = swaps[array]
        own = owns[array]
        for j in range(1, nc):
            src[j - 1] = own[z, rows(ctx_to(j)), :].astype(b16)
            over_ctx(array, src.at[j - 1], dst.at[j - 1], j, ctx_to(j)).start()
        place(array, c, own[z, rows(c), :])

    def swap_finish(array):
        src, dst = swaps[array]
        for j in range(1, nc):
            over_ctx(array, src.at[j - 1], dst.at[j - 1], j, ctx_to(j)).wait_recv()
            place(array, ctx_from(j), dst[j - 1].astype(f32))

    gather_total(COLUMN)
    o_out[...] = own_column[z]
    pass_back(FC1)
    swap_start(QKV)
    terms_arrive(NORM)

    def norm_step(i, carry):
        gain_sum, shift_sum = carry
        at = pl.ds(pl.multiple_of(i * chunk, chunk), chunk)
        x = tok_all[c, at, :].astype(f32)
        x = x - jnp.mean(x, axis=-1, keepdims=True)
        inverse = lax.rsqrt(jnp.mean(x * x, axis=-1, keepdims=True) + epsilon)
        x = x * inverse
        g = norm_own[at, :]
        for n in range(2):
            g = g + norm_got[n, at, :].astype(f32)
        v = g * vec_d[0:1, :]
        y = inverse * (
            v - jnp.mean(v, axis=-1, keepdims=True) - x * jnp.mean(v * x, axis=-1, keepdims=True)
        )
        o_tokens[at, :] = (cot_all[c, at, :].astype(f32) + y).astype(b16)
        return (
            gain_sum + jnp.sum(g * x, axis=0, keepdims=True),
            shift_sum + jnp.sum(g, axis=0, keepdims=True),
        )

    zero = jnp.zeros((1, width), f32)
    gain_sum, shift_sum = lax.fori_loop(0, part // chunk, norm_step, (zero, zero))
    sums[0, :, pl.ds(at_sum + width, width)] = gain_sum
    sums[0, :, pl.ds(at_sum + 2 * width, width)] = shift_sum

    sum_sib = remote(sums.at[0], sums_sib.at[0], back_sib_send.at[SUMS], back_sib_recv.at[SUMS], (other, c))
    sum_sib.start()
    swap_finish(QKV)
    sum_sib.wait()
    sums[1] = sums[0] + sums_sib[0]
    trades = [
        remote(
            sums.at[n + 1], sums_z.at[n], back_z_send.at[SUMS, n], back_z_recv.at[SUMS, n], (2 * partner + k, c)
        )
        for n, partner in enumerate((z + 1 - 2 * lax.rem(z, 2), lax.rem(z + 2, nz)))
    ]
    trades[0].start()
    trades[0].wait()
    sums[2] = sums[1] + sums_z[0]
    trades[1].start()
    swap_start(FC1)
    trades[1].wait()
    sums[3] = sums[2] + sums_z[1]
    sums_mine = sums.at[3]
    for j in range(1, nc):
        over_ctx(SUMS, sums_mine, o_sums.at[c], j, ctx_to(j)).start()
    o_sums[c] = sums[3]
    swap_finish(FC1)
    for j in range(1, nc):
        over_ctx(SUMS, sums_mine, o_sums.at[ctx_from(j)], j, ctx_to(j)).wait_recv()

    for array in (SMALL, QKV, FC1, FC2, OUT):
        z_sent(array)
    for array in (SMALL, QKV, FC1):
        ctx_sent(array)
    for array in (TOK, COT):
        for n in (1, 2):
            pair_copy(array, n).wait_send()
    for n in range(6):
        term_copy(PART, n).wait_send()
        term_copy(NORM, n).wait_send()
    for j in range(1, nc):
        out_copy(j, ctx_to(j), c).wait_send()
        column_copy(j, ctx_to(j)).wait_send()
    out_sib(k).wait_send()
    for array in (QKV, COLUMN, FC1, FC2):
        owner_sent(array)
    for j in range(1, nc):
        over_ctx(SUMS, sums_mine, o_sums.at[c], j, ctx_to(j)).wait_send()
        for array in (QKV, FC1):
            over_ctx(array, swaps[array][0].at[j - 1], swaps[array][1].at[j - 1], j, c).wait_send()


def layer_all(nz, nc, marks, tokens, cotangent, segments, qkv_weight, fc1_weight, fc2_weight, out_weight, small):
    part, width = tokens.shape
    wr, fr = qkv_weight.shape[0], fc2_weight.shape[0]
    nd, dl = 2 * nz, width // nc
    length, fl = part * nc, 2 * nz * fr
    cw = nc * wr
    f32, b16 = jnp.float32, jnp.bfloat16
    tables = [jnp.asarray(t) for t in turn_tables(length, width // HEADS, 128)]
    pack = small.shape[1]
    total = 3 * dl + fl + 3 * width
    tile, window = 256, 768
    results = [
        ((part, width), b16),
        ((part, width), b16),
        ((wr, 3 * width), f32),
        ((wr, width), f32),
        ((wr, fl * nc), f32),
        ((fr, width), f32),
        ((nc, 1, total), f32),
    ]
    work = [
        ((nc, part, width), b16),
        ((nc, part, width), b16),
        ((nd, cw, 3 * dl), b16),
        ((nd, cw, fl), b16),
        ((nd, fr, width), b16),
        ((2, cw, width), b16),
        ((nd, nc, 1, pack), f32),
        ((nd * nc, pack), f32),
        ((8, width), f32),
        ((1, 3 * dl), f32),
        ((1, fl), f32),
        ((length, width), b16),
        ((length, dl), b16),
        ((length, dl), b16),
        ((length, dl), b16),
        ((length, dl), b16),
        ((length, dl), b16),
        ((length, fl), b16),
        ((length, fl), f32),
        ((length, 3 * dl), b16),
        ((tile, dl), f32),
        ((length, dl), f32),
        ((length, dl), f32),
        ((tile, dl), f32),
        ((tile, window), f32),
        ((length, fl), b16),
    ]
    grads = [(nz, cw, 3 * dl), (nz, cw, fl), (nz, fr, width), (1, cw, width)]
    passed = grads[:3] + [(nz, wr, width)]
    fars = [(3,) + g[1:] for g in passed]
    work += [(g, b16) for g in grads] + [(g, b16) for g in grads] + [(g, f32) for g in grads]
    work += [(g, b16) for g in fars] + [(g[1:], b16) for g in passed]
    work += [((HEADS // nc, length, 1), f32), ((length, 128), f32)] + [((length, 128), f32)] * 3
    work += [((nc - 1, part, width), b16), ((part, width), f32)] * 2
    work += [((nc - 1, wr, n), b16) for n in (3 * dl, fl)] * 2
    work += [((nz, wr, width), t) for t in (b16, b16, f32)] + [((nc, wr, width), b16)]
    work += [((n, 1, total), f32) for n in (4, 1, 2)]
    work += [((2, part // 2, width), f32)]
    dma = pltpu.SemaphoreType.DMA
    sems = [(7, nc), (7, nc), (7, 5), (7, 5), (7, nz), (7, nz), (11,)]
    sems += [(8, 5), (8, 5), (7,), (7,), (7, 6), (7, 6)]
    hbm, vmem = pl.BlockSpec(memory_space=pl.ANY), pl.BlockSpec(memory_space=pltpu.VMEM)
    return pl.pallas_call(
        functools.partial(layer_kernel, nz, nc, marks),
        out_shape=[jax.ShapeDtypeStruct(s, t) for s, t in results],
        in_specs=[hbm] * 7 + [vmem] + [hbm] * 3,
        out_specs=[vmem] * len(results),
        scratch_shapes=[pltpu.VMEM(s, t) for s, t in work] + [dma(s) for s in sems],
        compiler_params=pltpu.CompilerParams(
            collective_id=0, has_side_effects=True, vmem_limit_bytes=62 * 2**20
        ),
        name="layer",
    )(tokens, cotangent, qkv_weight, fc1_weight, fc2_weight, out_weight, small, segments.reshape(1, length), *tables)


def finish_kernel(
    dl, fr, wr,
    result, tokens, qkv, out, fc1, fc2, sums,
    o_result, o_tokens, o_qkv, o_out, o_fc1, o_fc2, o_qkv_b, o_out_b, o_fc1_b, o_fc2_b, o_gain, o_shift,
    row,
):
    moves = [(result, o_result), (tokens, o_tokens), (qkv, o_qkv), (out, o_out), (fc1, o_fc1), (fc2, o_fc2)]
    for source, to in moves:
        to[...] = source[...]
    nc, total = sums.shape[0], sums.shape[2]
    mine, group = lax.axis_index("ctx"), lax.axis_index("dp")
    place = group * nc + mine
    width = dl * nc
    fl = total - 3 * dl - 3 * width

    def piece(values, size):
        length = values.shape[1]
        return pltpu.roll(values, length - place * size, axis=1)[0, :size]

    for t in range(3):
        for rank in range(nc):
            row[:, pl.ds(t * width + rank * dl, dl)] = sums[rank][:, t * dl : (t + 1) * dl]
    o_qkv_b[...] = piece(row[...], 3 * wr)
    at = pl.ds(pl.multiple_of(3 * dl + group * fr, fr), fr)
    o_fc1_b[...] = sums[mine, :, at][0]
    for n, outs in enumerate(((o_out_b, o_fc2_b), (o_gain,), (o_shift,))):
        first = 3 * dl + fl + n * width
        whole = sums[0][:, first : first + width]
        for rank in range(1, nc):
            whole = whole + sums[rank][:, first : first + width]
        for to in outs:
            to[...] = piece(whole, wr)


def finish_all(dl, fr, wr, arrays):
    f32 = jnp.float32
    vmem = pl.BlockSpec(memory_space=pltpu.VMEM)
    vectors = [3 * wr, wr, fr, wr, wr, wr]
    nc = arrays[6].shape[0]
    return pl.pallas_call(
        functools.partial(finish_kernel, dl, fr, wr),
        out_shape=[jax.ShapeDtypeStruct(a.shape, a.dtype) for a in arrays[:6]]
        + [jax.ShapeDtypeStruct((n,), f32) for n in vectors],
        in_specs=[vmem] * 7,
        out_specs=[vmem] * 12,
        scratch_shapes=[pltpu.VMEM((1, 3 * dl * nc), f32)],
        name="finish",
    )(*arrays)


def local_direct(
    dp,
    ctx,
    tokens,
    segments,
    qkv_weight,
    qkv_bias,
    out_weight,
    out_bias,
    fc1_weight,
    fc1_bias,
    fc2_weight,
    fc2_bias,
    norm_gain,
    norm_shift,
    cotangent,
):
    width = tokens.shape[-1]
    dl, fl = width // ctx, fc1_weight.shape[1] // ctx
    wr, fr = qkv_weight.shape[0], fc2_weight.shape[0]
    pieces = [fc1_bias, qkv_bias, norm_gain, norm_shift, out_bias, fc2_bias]
    marks = [0]
    for piece in pieces:
        marks.append(marks[-1] + piece.shape[0])
    vector = jnp.concatenate(pieces).astype(jnp.float32)
    vector = jnp.pad(vector, (0, -marks[-1] % 128))[None]
    arrays = layer_all(
        dp // 2,
        ctx,
        tuple(marks),
        tokens[0],
        cotangent[0],
        segments[0],
        qkv_weight,
        fc1_weight,
        fc2_weight,
        out_weight,
        vector,
    )
    result, grad_tokens, *rest = finish_all(dl, fr, wr, arrays)
    grad_qkv, grad_out, grad_fc1, grad_fc2, g_qkv_b, g_out_b, g_fc1_b, g_fc2_b, g_gain, g_shift = rest
    return (
        result[None],
        grad_tokens[None],
        grad_qkv,
        g_qkv_b,
        grad_out,
        g_out_b,
        grad_fc1,
        g_fc1_b,
        grad_fc2,
        g_fc2_b,
        g_gain,
        g_shift,
    )


def solution(mesh):
    sizes = (mesh.shape["dp"], mesh.shape["ctx"])
    seq, mat, vec = P("dp", "ctx", None), P(BOTH, None), P(BOTH)

    def spread(*args):
        dp, ctx = sizes
        tokens, qkv_weight, fc2_weight = args[0], args[2], args[8]
        direct = (
            dp == 8
            and ctx == 4
            and tokens.shape[0] == 1
            and tokens.shape[1] % 256 == 0
            and qkv_weight.shape[0] % 32 == 0
            and fc2_weight.shape[0] % 128 == 0
        )
        return (local_direct if direct else local)(*sizes, *args)

    placed = (seq, P("dp", None), mat, vec, mat, vec, mat, vec, mat, vec, vec, vec, seq)
    return jax.shard_map(
        spread,
        mesh=mesh,
        in_specs=placed,
        out_specs=(seq, seq, mat, vec, mat, vec, mat, vec, mat, vec, vec, vec),
        check_vma=False,
    )
```

```python
import functools

import jax
import jax.numpy as jnp
import numpy as np
from jax import lax
from jax.experimental import pallas as pl
from jax.experimental.pallas import tpu as pltpu
from jax.sharding import PartitionSpec as P

HEADS = 16
ROT = 32
epsilon = 1e-05
BOTH = ("dp", "ctx")
MESH = pl.DeviceIdType.MESH


def angles(positions, rotary):
    freq_table = 1.0 / 10000.0 ** (jnp.arange(0, rotary, 2, dtype=jnp.float32) / rotary)
    theta = positions.astype(jnp.float32)[:, None] * freq_table[None, :]
    return (jnp.cos(theta)[:, None, :], jnp.sin(theta)[:, None, :])


def rotate(tensor, cosine, sine_table, rotary):
    half_len = rotary // 2
    first_half = tensor[..., :half_len]
    second_half = tensor[..., half_len:rotary]
    return jnp.concatenate(
        [
            first_half * cosine - second_half * sine_table,
            second_half * cosine + first_half * sine_table,
            tensor[..., rotary:],
        ],
        axis=-1,
    )


def contract_rows(left, right):
    return lax.dot_general(
        left, right, (((0,), (0,)), ((), ())), preferred_element_type=jnp.float32
    )


def times_transposed(left, right):
    return lax.dot_general(
        left, right, (((1,), (1,)), ((), ())), preferred_element_type=jnp.float32
    )


def times(left, right):
    return jnp.dot(left, right, preferred_element_type=jnp.float32)


def gelu_tanh(hidden_in):
    return jax.nn.gelu(hidden_in, approximate=True)


def normalise(inputs):
    center = inputs - jnp.mean(inputs, axis=-1, keepdims=True)
    inverse = lax.rsqrt(jnp.mean(center * center, axis=-1, keepdims=True) + epsilon)
    return center * inverse, inverse


def attention(q, k, v, segments, back, cosine, sine):
    length, head_dim = q.shape[1], q.shape[3]
    scale = float(head_dim) ** (-0.5)
    index = jnp.arange(length, dtype=jnp.int32)
    allowed = (segments[:, :, None] == segments[:, None, :]) & (index[None, :] <= index[:, None])[
        None
    ]
    scores = jnp.einsum("sqhd,skhd->shqk", q, k, preferred_element_type=jnp.float32) * scale
    scores = jnp.where(allowed[:, None], scores, -1e30)
    row_max = jnp.max(scores, axis=-1, keepdims=True)
    log_total = row_max + jnp.log(jnp.sum(jnp.exp(scores - row_max), axis=-1, keepdims=True))
    probs = jnp.exp(scores - log_total)
    probs_low = probs.astype(jnp.bfloat16)
    attended = jnp.einsum("shqk,skhd->sqhd", probs_low, v, preferred_element_type=jnp.float32)

    def backward(grad_attended):
        grad_weights = jnp.einsum(
            "sqhd,skhd->shqk", grad_attended, v, preferred_element_type=jnp.float32
        )
        row_dot = jnp.sum(grad_weights * probs, axis=-1, keepdims=True)
        grad_scores = (probs * (grad_weights - row_dot)).astype(jnp.bfloat16)
        grad_q = (
            jnp.einsum("shqk,skhd->sqhd", grad_scores, k, preferred_element_type=jnp.float32)
            * scale
        )
        grad_k = (
            jnp.einsum("shqk,sqhd->skhd", grad_scores, q, preferred_element_type=jnp.float32)
            * scale
        )
        grad_v = jnp.einsum(
            "shqk,sqhd->skhd", probs_low, grad_attended, preferred_element_type=jnp.float32
        )
        return grad_q, grad_k, grad_v

    return attended, backward


def local(
    dp,
    ctx,
    tokens,
    segments,
    qkv_weight,
    qkv_bias,
    out_weight,
    out_bias,
    fc1_weight,
    fc1_bias,
    fc2_weight,
    fc2_bias,
    norm_gain,
    norm_shift,
    cotangent,
):
    f32, b16 = jnp.float32, jnp.bfloat16
    seqs, part, width = tokens.shape
    length = part * ctx
    rows = seqs * length
    ff = fc1_weight.shape[1]
    fl, dl = ff // ctx, width // ctx
    heads = HEADS // ctx
    head_dim = width // HEADS
    wr, fr = qkv_weight.shape[0], fc2_weight.shape[0]
    mine = lax.axis_index("ctx")
    devices = dp * ctx

    pieces = [qkv_bias, fc1_bias, out_bias, fc2_bias, norm_gain, norm_shift]
    marks = [0]
    for piece in pieces:
        marks.append(marks[-1] + piece.shape[0])
    small = lax.all_gather(jnp.concatenate(pieces), BOTH, axis=0)
    parts = [small[:, a:b] for a, b in zip(marks, marks[1:])]
    b_qkv = lax.dynamic_index_in_dim(
        parts[0].reshape(3, ctx, dl), mine, 1, keepdims=False
    ).reshape(3 * dl)
    b_fc1 = lax.dynamic_index_in_dim(
        parts[1].reshape(dp, ctx, fr), mine, 1, keepdims=False
    ).reshape(fl)
    b_out, b_fc2, gain, shift = [p.reshape(width).astype(f32) for p in parts[2:]]

    send_qkv = jnp.moveaxis(qkv_weight.reshape(wr, 3, ctx, dl), 2, 0).reshape(ctx, wr, 3 * dl)
    send_fc1 = jnp.moveaxis(fc1_weight.reshape(wr, dp, ctx, fr), 2, 0).reshape(ctx, wr, fl)
    sent = lax.all_to_all(
        jnp.concatenate([send_qkv, send_fc1], axis=2), "ctx", split_axis=0, concat_axis=0
    )
    out_perm = [(b, (b % dp) * ctx + b // dp) for b in range(devices)]
    out_back = [(j, i) for i, j in out_perm]
    out_piece = lax.ppermute(out_weight, BOTH, out_perm)
    w_qkv = lax.all_gather(sent[:, :, : 3 * dl], "dp", axis=0).reshape(width, 3 * dl)
    w_fc1 = lax.all_gather(sent[:, :, 3 * dl :], "dp", axis=0).reshape(width, fl)
    w_fc2 = lax.all_gather(fc2_weight, "dp", axis=0).reshape(fl, width)
    w_out = lax.all_gather(out_piece, "dp", axis=0).reshape(dl, width)

    tokens_all = lax.all_gather(tokens, "ctx", axis=1, tiled=True)
    cot_all = lax.all_gather(cotangent, "ctx", axis=1, tiled=True)

    positions = jnp.arange(length, dtype=jnp.int32)
    cosine, sine = angles(positions, ROT)

    scaled_all, _ = normalise(tokens_all.astype(f32).reshape(rows, width))
    normed = (scaled_all * gain + shift).astype(b16)
    grad_out = cot_all.reshape(rows, width)

    mixed = times(normed, w_qkv) + b_qkv.astype(f32)
    shape4 = (seqs, length, heads, head_dim)
    q = rotate(mixed[:, :dl].reshape(shape4), cosine, sine, ROT).astype(b16)
    k = rotate(mixed[:, dl : 2 * dl].reshape(shape4), cosine, sine, ROT).astype(b16)
    v = mixed[:, 2 * dl :].astype(b16).reshape(shape4)
    attended, attention_back = attention(q, k, v, segments, None, cosine, sine)
    attended = attended.reshape(rows, dl).astype(b16)

    hidden = times(normed, w_fc1) + b_fc1.astype(f32)
    act, gelu_back = jax.vjp(gelu_tanh, hidden)
    act = act.astype(b16)
    partial = times(attended, w_out) + times(act, w_fc2)
    summed = lax.psum_scatter(
        partial.astype(b16).reshape(seqs, length, width), "ctx", scatter_dimension=1, tiled=True
    )
    result = (tokens.astype(f32) + summed.astype(f32) + (b_out + b_fc2)).astype(b16)

    grad_act = times_transposed(grad_out, w_fc2)
    grad_hidden = gelu_back(grad_act)[0].astype(b16)
    grad_fc2 = contract_rows(act, grad_out)
    grad_fc2 = lax.psum_scatter(grad_fc2.astype(b16), "dp", scatter_dimension=0, tiled=True)
    grad_fc1 = contract_rows(normed, grad_hidden)
    grad_fc1_b = jnp.sum(grad_hidden, axis=0, dtype=f32)
    grad_fc1 = lax.psum_scatter(grad_fc1.astype(b16), "dp", scatter_dimension=0, tiled=True)
    grad_out_w = contract_rows(attended, grad_out)
    grad_out_w = lax.psum_scatter(grad_out_w.astype(b16), "dp", scatter_dimension=0, tiled=True)
    grad_attended = times_transposed(grad_out, w_out).astype(b16).reshape(shape4)
    grad_q, grad_k, grad_v = attention_back(grad_attended)
    grad_mixed = jnp.concatenate(
        [
            rotate(grad_q, cosine, -sine, ROT).reshape(rows, dl),
            rotate(grad_k, cosine, -sine, ROT).reshape(rows, dl),
            grad_v.reshape(rows, dl),
        ],
        axis=1,
    ).astype(b16)
    grad_normed = times_transposed(grad_hidden, w_fc1) + times_transposed(grad_mixed, w_qkv)
    grad_normed = lax.psum_scatter(
        grad_normed.astype(b16).reshape(seqs, length, width), "ctx", scatter_dimension=1, tiled=True
    ).astype(f32)
    grad_qkv = contract_rows(normed, grad_mixed)
    grad_qkv_b = jnp.sum(grad_mixed, axis=0, dtype=f32)
    grad_qkv = lax.psum_scatter(grad_qkv.astype(b16), "dp", scatter_dimension=0, tiled=True)

    back = lax.all_to_all(
        jnp.concatenate([grad_qkv, grad_fc1], axis=1).reshape(ctx, wr, 3 * dl + fl),
        "ctx",
        split_axis=0,
        concat_axis=0,
    ).astype(f32)
    grad_qkv = jnp.moveaxis(back[:, :, : 3 * dl].reshape(ctx, wr, 3, dl), 0, 2).reshape(
        wr, 3 * width
    )
    grad_fc1 = jnp.moveaxis(back[:, :, 3 * dl :].reshape(ctx, wr, dp, fr), 0, 2).reshape(wr, ff)
    grad_out_w = lax.ppermute(grad_out_w, BOTH, out_back).astype(f32)
    grad_fc2 = grad_fc2.astype(f32)

    grad_normed = grad_normed.reshape(seqs, part, width)
    own = tokens.astype(f32)
    cot = cotangent.astype(f32)
    scaled, inverse = normalise(own)
    grad_gain = jnp.sum(grad_normed * scaled, axis=(0, 1))
    grad_shift = jnp.sum(grad_normed, axis=(0, 1))
    grad_scaled = grad_normed * gain
    grad_input = inverse * (
        grad_scaled
        - jnp.mean(grad_scaled, axis=-1, keepdims=True)
        - scaled * jnp.mean(grad_scaled * scaled, axis=-1, keepdims=True)
    )
    grad_tokens = (cot + grad_input).astype(b16)

    wide_qkv_b = lax.dynamic_update_index_in_dim(
        jnp.zeros((3, ctx, dl), f32), grad_qkv_b.reshape(3, dl), mine, 1
    )
    wide_fc1_b = lax.dynamic_update_index_in_dim(
        jnp.zeros((dp, ctx, fr), f32), grad_fc1_b.reshape(dp, fr), mine, 1
    )
    bias_out = jnp.sum(cot, axis=(0, 1))
    sums = jnp.concatenate(
        [
            x.reshape(devices, -1)
            for x in (wide_qkv_b, wide_fc1_b, bias_out, grad_gain, grad_shift)
        ],
        axis=1,
    )
    sums = lax.psum_scatter(sums, BOTH, scatter_dimension=0, tiled=True)[0]
    at = [0, marks[1], marks[2], marks[3], marks[3] + wr, marks[3] + 2 * wr]
    g_qkv_b, g_fc1_b, g_bias, g_gain, g_shift = [sums[a:b] for a, b in zip(at, at[1:])]
    return (
        result,
        grad_tokens,
        grad_qkv,
        g_qkv_b,
        grad_out_w,
        g_bias,
        grad_fc1,
        g_fc1_b,
        grad_fc2,
        g_bias,
        g_gain,
        g_shift,
    )


def dot(left, right, contract):
    return lax.dot_general(
        left, right, ((contract[:1], contract[1:]), ((), ())), preferred_element_type=jnp.float32
    )


NORMAL, RIGHT_T, LEFT_T = (1, 0), (1, 1), (0, 0)


def turn_tables(length, head_dim, lanes):
    half = ROT // 2
    freq = np.float32(1.0) / np.power(
        np.float32(10000.0), np.arange(0, ROT, 2, dtype=np.float32) / np.float32(ROT)
    )
    theta = np.arange(length, dtype=np.float32)[:, None] * freq[None, :]
    cosine, sine = np.cos(theta), np.sin(theta)
    keep = np.ones((length, head_dim), np.float32)
    keep[:, :half] = cosine
    keep[:, half:ROT] = cosine
    ahead = np.zeros((length, head_dim), np.float32)
    ahead[:, :half] = -sine
    behind = np.zeros((length, head_dim), np.float32)
    behind[:, half:ROT] = sine
    return [np.tile(t, (1, lanes // head_dim)) for t in (keep, ahead, behind)]


def turn(x, keep, ahead, behind):
    half, lanes = ROT // 2, x.shape[1]
    return (
        x * keep
        + pltpu.roll(x, lanes - half, axis=1) * ahead
        + pltpu.roll(x, half, axis=1) * behind
    )


DELTAS = (-2, 2, -1, 1)
SLOTS = (0, 0, 1, 2)
PASSED = 4


def layer_kernel(
    nz, nc, marks,
    tok_ref, cot_ref, qkv_ref, fc1_ref, fc2_ref, out_ref, small_ref,
    seg_ref, keep_hbm, ahead_hbm, behind_hbm,
    o_result, o_tokens, o_qkv, o_out, o_fc1, o_fc2, o_sums,
    tok_all, cot_all, w_qkv, w_fc1, w_fc2, w_out, small_all,
    small_rows, vec_d, b_qkv, b_fc1, normed, q_s, k_s, v_s, attended, g_att, act, slope, gmixed,
    acc_q, acc_k, acc_v, acc_a, bias_s, g_hidden,
    give_qkv, give_fc1, give_fc2, give_out, got_qkv, got_fc1, got_fc2, got_out,
    own_qkv, own_fc1, own_fc2, own_out_g, far_qkv, far_fc1, far_fc2, far_out,
    pass_qkv, pass_fc1, pass_fc2, pass_out, log_s, seg_col, keep_ref, ahead_ref, behind_ref,
    part_got, part_own, norm_got, norm_own,
    swap_qkv, swap_fc1, swapped_qkv, swapped_fc1, out_planes, give_column, own_column, column_got,
    sums, sums_sib, sums_z, held,
    ctx_send, ctx_recv, z_send, z_recv, sib_send, sib_recv, loc,
    back_z_send, back_z_recv, back_sib_send, back_sib_recv, back_ctx_send, back_ctx_recv,
):
    f32, b16 = jnp.float32, jnp.bfloat16
    d, c = lax.axis_index("dp"), lax.axis_index("ctx")
    z, k = d // 2, lax.rem(d, 2)
    other = 2 * z + 1 - k
    wr, width = out_ref.shape
    dl = width // nc
    fr = fc2_ref.shape[0]
    nd = 2 * nz
    part = tok_ref.shape[0]
    length = part * nc
    head_dim = width // HEADS
    heads = HEADS // nc
    fl = nd * fr

    def ctx_to(j):
        return lax.rem(c + j, nc)

    def ctx_from(j):
        return lax.rem(c + nc - j, nc)

    def exists(delta):
        return (z + delta >= 0) & (z + delta < nz)

    def plane(delta):
        return 2 * jnp.clip(z + delta, 0, nz - 1) + k

    barrier = pltpu.get_barrier_semaphore()
    for j in range(1, nc):
        pl.semaphore_signal(barrier, inc=1, device_id=(d, ctx_to(j)), device_id_type=MESH)
    for delta in DELTAS:
        @pl.when(exists(delta))
        def _():
            pl.semaphore_signal(barrier, inc=1, device_id=(plane(delta), c), device_id_type=MESH)
    pl.semaphore_signal(barrier, inc=1, device_id=(other, c), device_id_type=MESH)
    planes = jnp.minimum(z, 2) + jnp.minimum(nz - 1 - z, 2)
    pl.semaphore_wait(barrier, nc + planes)

    def remote(src, dst, send, recv, device):
        return pltpu.make_async_remote_copy(
            src_ref=src, dst_ref=dst, send_sem=send, recv_sem=recv,
            device_id=device, device_id_type=MESH,
        )

    def rows(at):
        return pl.ds(pl.multiple_of(at * wr, wr), wr)

    def lanes(at, size):
        return pl.ds(pl.multiple_of(at * size, size), size)

    SMALL, QKV, FC1, TOK, COT, OUT, FC2 = range(7)

    def ctx_pieces(array, to):
        if array == SMALL:
            return [(small_ref, small_all.at[d, c])]
        if array == QKV:
            return [
                (qkv_ref.at[:, lanes(t * nc + to, dl)], w_qkv.at[d, rows(c), pl.ds(t * dl, dl)])
                for t in range(3)
            ]
        if array == FC1:
            return [
                (fc1_ref.at[:, lanes(g * nc + to, fr)], w_fc1.at[d, rows(c), pl.ds(g * fr, fr)])
                for g in range(nd)
            ]
        if array == TOK:
            return [(tok_ref, tok_all.at[c])]
        return [(cot_ref, cot_all.at[c])]

    def ctx_whole(array, sub):
        return {
            SMALL: lambda: small_all.at[d, sub],
            QKV: lambda: w_qkv.at[d, rows(sub), :],
            FC1: lambda: w_fc1.at[d, rows(sub), :],
            TOK: lambda: tok_all.at[sub],
            COT: lambda: cot_all.at[sub],
        }[array]()

    def ctx_start(array):
        for j in range(1, nc):
            for src, dst in ctx_pieces(array, ctx_to(j)):
                remote(src, dst, ctx_send.at[array, j], ctx_recv.at[array, j], (d, ctx_to(j))).start()
        for src, dst in ctx_pieces(array, c):
            pltpu.make_async_copy(src, dst, loc.at[array]).start()

    def ctx_arrive(array, j):
        got = ctx_whole(array, ctx_from(j))
        if j == 0:
            pltpu.make_async_copy(got, got, loc.at[array]).wait()
        else:
            remote(got, got, ctx_send.at[array, j], ctx_recv.at[array, j], (d, ctx_to(j))).wait_recv()

    def ctx_sent(array):
        for j in range(1, nc):
            got = ctx_whole(array, ctx_from(j))
            remote(got, got, ctx_send.at[array, j], ctx_recv.at[array, j], (d, ctx_to(j))).wait_send()

    def ctx_finish(array):
        for j in range(nc):
            ctx_arrive(array, j)

    side, across, corner = c + 1 - 2 * lax.rem(c, 2), lax.rem(c + 2, nc), nc - 1 - c
    first_half, second_half = pl.ds(0, part // 2), pl.ds(part // 2, part // 2)

    def pair_copy(array, n):
        store = tok_all if array == TOK else cot_all
        src = tok_ref if array == TOK else cot_ref
        if n == 1:
            dst, to = store.at[c], side
        elif n == 2:
            dst, to = store.at[c], across
        elif n == 3:
            src = store.at[side, first_half, :]
            dst, to = src, across
        else:
            src = store.at[across, second_half, :]
            dst, to = src, side
        return remote(src, dst, ctx_send.at[array, n], ctx_recv.at[array, n], (d, to))

    def pair_start(array):
        store, src = (tok_all, tok_ref) if array == TOK else (cot_all, cot_ref)
        pair_copy(array, 1).start()
        pair_copy(array, 2).start()
        pltpu.make_async_copy(src, store.at[c], loc.at[array]).start()

    def pair_got(array, n):
        store = tok_all if array == TOK else cot_all
        got = {
            0: lambda: store.at[corner, second_half, :],
            1: lambda: store.at[side],
            2: lambda: store.at[across],
            3: lambda: store.at[corner, first_half, :],
        }[n]()
        remote(got, got, ctx_send.at[array, n], ctx_recv.at[array, n], (d, side)).wait_recv()

    def pair_forward(array):
        pair_got(array, 1)
        pair_copy(array, 3).start()
        pair_got(array, 2)
        pair_copy(array, 0).start()

    def pair_own(array):
        store = tok_all if array == TOK else cot_all
        pltpu.make_async_copy(store.at[c], store.at[c], loc.at[array]).wait()

    def block_of(array, at):
        if array == OUT:
            return out_planes.at[lax.div(at, 2)]
        return {SMALL: small_all, QKV: w_qkv, FC1: w_fc1, FC2: w_fc2}[array].at[at]

    near_low, near_high = z == 1, z == nz - 2

    def z_copy(array, n, delta, owner):
        block = block_of(array, owner)
        src = block
        if array in (FC2, OUT) and n < PASSED:
            src = fc2_ref if array == FC2 else out_ref
        return remote(src, block, z_send.at[array, n], z_recv.at[array, n], (plane(delta), c))

    def z_got(array, n, owner):
        block = block_of(array, owner)
        return remote(block, block, z_send.at[array, n], z_recv.at[array, n], (d, c))

    def sib_copy(array, at):
        block = block_of(array, 2 * at + k)
        return remote(block, block, sib_send.at[array, at], sib_recv.at[array, at], (other, c))

    def z_own(array):
        for n, delta in enumerate(DELTAS):
            @pl.when(exists(delta))
            def _():
                z_copy(array, n, delta, d).start()
        if array not in (FC2, OUT):
            sib_copy(array, z).start()

    def z_forward(array):
        @pl.when(near_high)
        def _():
            z_got(array, DELTAS.index(2), k).wait_recv()
            z_copy(array, PASSED, 1, k).start()

        @pl.when(near_low)
        def _():
            z_got(array, DELTAS.index(-2), d + 4).wait_recv()
            z_copy(array, PASSED, -1, d + 4).start()

    def z_arrive(array):
        for n, delta in enumerate(DELTAS):
            done = near_high if delta == 2 else near_low if delta == -2 else None
            wanted = exists(-delta) if done is None else exists(-delta) & jnp.logical_not(done)

            @pl.when(wanted)
            def _():
                z_got(array, n, plane(-delta)).wait_recv()

        @pl.when(z == 0)
        def _():
            z_got(array, PASSED, 2 * (nz - 1) + k).wait_recv()

        @pl.when(z == nz - 1)
        def _():
            z_got(array, PASSED, k).wait_recv()

        if array == OUT:
            return
        for at in range(nz):
            if array == FC2:
                sib_copy(array, at).start()
            else:
                @pl.when(z != at)
                def _():
                    sib_copy(array, at).start()

    def z_finish(array):
        for at in range(nz):
            block = block_of(array, 2 * at + 1 - k)
            remote(block, block, sib_send.at[array, at], sib_recv.at[array, at], (other, c)).wait_recv()

    def z_sent(array):
        for n, delta in enumerate(DELTAS):
            @pl.when(exists(delta))
            def _():
                z_copy(array, n, delta, d).wait_send()

        @pl.when(near_high | near_low)
        def _():
            z_copy(array, PASSED, 1, k).wait_send()

        if array != OUT:
            for at in range(nz):
                sib_copy(array, at).wait_send()

    def out_copy(j, to, sub):
        piece = out_planes.at[to]
        return remote(piece, w_out.at[k, rows(sub), :], ctx_send.at[OUT, j], ctx_recv.at[OUT, j], (d, to))

    def own_out():
        return pltpu.make_async_copy(out_planes.at[c], w_out.at[k, rows(c), :], loc.at[OUT])

    def out_sib(which):
        piece = w_out.at[which]
        return remote(piece, piece, sib_send.at[OUT, 0], sib_recv.at[OUT, 0], (other, c))

    ctx_start(SMALL)
    ctx_start(QKV)
    z_own(OUT)
    tables = [(keep_hbm, keep_ref), (ahead_hbm, ahead_ref), (behind_hbm, behind_ref)]
    tables = [pltpu.make_async_copy(a, b, loc.at[8 + n]) for n, (a, b) in enumerate(tables)]
    for copy in tables:
        copy.start()
    copy_out = pltpu.make_async_copy(out_ref, out_planes.at[z], loc.at[7])
    copy_out.start()
    ctx_start(FC1)
    pair_start(TOK)
    copy_fc2 = pltpu.make_async_copy(fc2_ref, w_fc2.at[d], loc.at[FC2])
    copy_fc2.start()

    ctx_finish(SMALL)
    z_own(SMALL)
    ctx_finish(QKV)
    z_own(QKV)
    z_forward(OUT)
    z_forward(SMALL)
    ctx_finish(FC1)
    z_own(FC1)
    z_arrive(OUT)
    copy_out.wait()
    own_out().start()
    for j in range(1, nc):
        out_copy(j, ctx_to(j), c).start()
    pair_start(COT)
    z_arrive(SMALL)
    z_forward(QKV)
    z_own(FC2)
    z_finish(SMALL)

    def collect(p, carry):
        small_rows[pl.ds(p, 1), :] = small_all[p // nc, lax.rem(p, nc)]
        return carry

    lax.fori_loop(0, nd * nc, collect, 0)
    table = small_rows[...]
    pack = table.shape[1]

    def vector(mark, size, first, count):
        entry = lax.broadcasted_iota(jnp.int32, (1, count), 1).astype(f32) + first
        owner = jnp.floor((entry + 0.5) * (1.0 / size))
        lane = entry - owner * size + mark
        pick = lax.broadcasted_iota(jnp.int32, (pack, count), 0).astype(f32) == lane
        found = dot(table.astype(b16), jnp.where(pick, 1.0, 0.0).astype(b16), NORMAL)
        here = lax.broadcasted_iota(jnp.int32, (nd * nc, count), 0).astype(f32) == owner
        return jnp.sum(jnp.where(here, found, 0.0), axis=0, keepdims=True)

    for i in range(2):
        vec_d[pl.ds(i, 1), :] = vector(marks[2 + i], wr, 0.0, width)
    vec_d[2:3, :] = vector(marks[4], wr, 0.0, width) + vector(marks[5], wr, 0.0, width)
    for t in range(3):
        b_qkv[:, pl.ds(t * dl, dl)] = vector(marks[1], 3 * wr, (t * width + c * dl).astype(f32), dl)
    for g in range(nd):
        b_fc1[:, pl.ds(g * fr, fr)] = small_all[g, c][:, :fr]

    z_arrive(QKV)
    z_finish(QKV)

    seg_col[...] = jnp.broadcast_to(seg_ref[...].astype(f32), (128, length)).T

    chunk = 32

    def block_rows(b):
        return pl.ds(pl.multiple_of(b * part, part), part)

    def normalise_block(b):
        def step(i, carry):
            at = pl.multiple_of(i * chunk, chunk)
            x = tok_all[b, pl.ds(at, chunk), :].astype(f32)
            x = x - jnp.mean(x, axis=-1, keepdims=True)
            x = x * lax.rsqrt(jnp.mean(x * x, axis=-1, keepdims=True) + epsilon)
            normed[pl.ds(pl.multiple_of(b * part, part) + at, chunk), :] = (
                x * vec_d[0:1, :] + vec_d[1:2, :]
            ).astype(b16)
            return carry

        lax.fori_loop(0, part // chunk, step, 0)

    def qkv_block(b):
        at = block_rows(b)
        x = normed[at, :]
        keep = jnp.tile(keep_ref[at, :], (1, dl // keep_ref.shape[1]))
        ahead = jnp.tile(ahead_ref[at, :], (1, dl // keep_ref.shape[1]))
        behind = jnp.tile(behind_ref[at, :], (1, dl // keep_ref.shape[1]))
        for t, to in enumerate((q_s, k_s, v_s)):
            w = w_qkv[:, :, pl.ds(t * dl, dl)].reshape(width, dl)
            y = dot(x, w, NORMAL) + b_qkv[:, pl.ds(t * dl, dl)]
            if t < 2:
                y = turn(y, keep, ahead, behind)
            to[at, :] = y.astype(b16)

    for copy in tables:
        copy.wait()
    pair_own(TOK)
    normalise_block(c)
    qkv_block(c)
    pair_forward(TOK)
    normalise_block(side)
    qkv_block(side)
    normalise_block(across)
    qkv_block(across)
    pair_got(TOK, 3)
    pair_got(TOK, 0)
    normalise_block(corner)
    qkv_block(corner)

    z_forward(FC1)
    pair_forward(COT)

    tile = 256
    reach = 512 // tile
    scale = float(head_dim) ** (-0.5)

    def spans(i):
        first = max(0, i - reach) * tile
        count = (i + 1) * tile - first
        return pl.ds(i * tile, tile), pl.ds(first, count), count

    def mask(i):
        at, to, count = spans(i)
        same = seg_col[at, :1] == seg_ref[:1, to].astype(f32)
        row = lax.broadcasted_iota(jnp.int32, (tile, count), 0) + (tile * i - to.start)
        col = lax.broadcasted_iota(jnp.int32, (tile, count), 1)
        bias_s[:, :count] = jnp.where(same & (col <= row), 0.0, -1e30)

    def only_head(h):
        lane = lax.broadcasted_iota(jnp.int32, (1, dl), 1)
        return jnp.where((lane >= h * head_dim) & (lane < (h + 1) * head_dim), 1.0, 0.0)

    for i in range(length // tile):
        at, to, count = spans(i)
        mask(i)
        acc_a[...] = jnp.zeros_like(acc_a)

        def forward_step(h, carry):
            only = only_head(h)
            s = dot(q_s[at, :] * only.astype(b16), k_s[to, :], RIGHT_T) * scale + bias_s[:, :count]
            top = jnp.max(s, axis=-1, keepdims=True)
            e = jnp.exp(s - top)
            sum_e = jnp.sum(e, axis=-1, keepdims=True)
            log_s[h, at, :] = top + jnp.log(sum_e)
            p_low = (e * (1.0 / sum_e)).astype(b16)
            acc_a[...] += dot(p_low, v_s[to, :], NORMAL) * only
            return carry

        lax.fori_loop(0, heads, forward_step, 0, unroll=True)
        attended[at, :] = acc_a[...].astype(b16)

    z_arrive(FC1)
    z_finish(FC1)

    def hidden_block(b, carry):
        at = block_rows(b)
        x = normed[at, :]
        for g in range(0, fl, 256):
            w = w_fc1[:, :, pl.ds(g, 256)].reshape(width, 256)
            h = dot(x, w, NORMAL) + b_fc1[:, pl.ds(g, 256)]
            s = h * h
            t = jnp.tanh(h * (0.7978845608028654 + (0.7978845608028654 * 0.044715) * s))
            half_t = 0.5 + 0.5 * t
            act[at, pl.ds(g, 256)] = (h * half_t).astype(b16)
            slope[at, pl.ds(g, 256)] = half_t + 0.5 * h * (1.0 - t * t) * (
                0.7978845608028654 + (3 * 0.7978845608028654 * 0.044715) * s
            )
        return carry

    lax.fori_loop(0, nc, hidden_block, 0)

    z_forward(FC2)
    pair_own(COT)
    pair_got(COT, 3)
    pair_got(COT, 0)

    COLUMN = 7
    gives = {QKV: give_qkv, FC1: give_fc1, FC2: give_fc2, OUT: give_out, COLUMN: give_column}
    gots = {QKV: got_qkv, FC1: got_fc1, FC2: got_fc2, OUT: got_out}
    owns = {QKV: own_qkv, FC1: own_fc1, FC2: own_fc2, OUT: own_out_g, COLUMN: own_column}
    fars = {QKV: far_qkv, FC1: far_fc1, FC2: far_fc2, COLUMN: far_out}
    passes = {QKV: pass_qkv, FC1: pass_fc1, FC2: pass_fc2, COLUMN: pass_out}

    def cotangents():
        return cot_all[...].reshape(length, width)

    def weight_gradient(array, left, right):
        give, own = gives[array], owns[array]
        size = give.shape[1]

        def step(i, carry):
            both = dot(left[:, lanes(i, 2 * size)], right(), LEFT_T)
            low, high = both[:size], both[size:]
            own[i] = jnp.where(k == 0, low, high)
            give[i] = jnp.where(k == 0, high, low).astype(b16)
            return carry

        lax.fori_loop(0, give.shape[0], step, 0)
        to_sibling(array).start()

    def to_sibling(array):
        return remote(
            gives[array], gots[array], back_sib_send.at[array], back_sib_recv.at[array], (other, c)
        )

    def to_owner(array, n, delta):
        block = gives[array].at[jnp.clip(z + delta, 0, nz - 1)]
        return remote(
            block, fars[array].at[SLOTS[n]], back_z_send.at[array, n], back_z_recv.at[array, n], (plane(delta), c)
        )

    def to_pass(array, delta):
        block = gives[array].at[jnp.clip(z + 3 * delta, 0, nz - 1)]
        return remote(
            block, passes[array], back_z_send.at[array, PASSED], back_z_recv.at[array, PASSED], (plane(delta), c)
        )

    def both_cores(array, at):
        if array == COLUMN:
            return own_column[at]
        return owns[array][at] + gots[array][at].astype(f32)

    def send_back(array):
        for delta in (-1, 1):
            far = jnp.clip(z + 3 * delta, 0, nz - 1)

            @pl.when(z == (nz - 1 if delta < 0 else 0))
            def _():
                gives[array][far] = both_cores(array, far).astype(b16)
                to_pass(array, delta).start()
        for n, delta in enumerate(DELTAS):
            hold = {-2: near_high, 2: near_low}.get(delta)
            go = exists(delta) if hold is None else exists(delta) & jnp.logical_not(hold)
            at = jnp.clip(z + delta, 0, nz - 1)

            @pl.when(go)
            def _():
                gives[array][at] = both_cores(array, at).astype(b16)
                to_owner(array, n, delta).start()

    def add_sibling(array):
        to_sibling(array).wait()
        send_back(array)

    def pass_back(array):
        for near, delta in ((near_high, -2), (near_low, 2)):
            at = jnp.clip(z + delta, 0, nz - 1)

            @pl.when(near)
            def _():
                to_pass(array, delta).wait_recv()
                gives[array][at] = (both_cores(array, at) + passes[array][...].astype(f32)).astype(b16)
                to_owner(array, DELTAS.index(delta), delta).start()

    def gather_total(array):
        own = owns[array]
        own[z] = both_cores(array, z)
        for n, delta in enumerate(DELTAS):
            @pl.when(exists(-delta))
            def _():
                to_owner(array, n, delta).wait_recv()
                own[z] = own[z] + fars[array][SLOTS[n]].astype(f32)

    def owner_sent(array):
        for n, delta in enumerate(DELTAS):
            @pl.when(exists(delta))
            def _():
                to_owner(array, n, delta).wait_send()
        for delta in (-1, 1):
            @pl.when(z == (nz - 1 if delta < 0 else 0))
            def _():
                to_pass(array, delta).wait_send()

    def column_copy(j, to):
        return remote(
            give_out.at[0, rows(to), :], column_got.at[c], back_ctx_send.at[OUT, j], back_ctx_recv.at[OUT, j], (d, to)
        )

    def to_columns():
        to_sibling(OUT).wait()
        own_out_g[0] = own_out_g[0] + got_out[0].astype(f32)
        give_out[0] = own_out_g[0].astype(b16)
        for j in range(1, nc):
            column_copy(j, ctx_to(j)).start()
        own_column[c] = own_out_g[0, rows(c), :]

    def from_columns():
        for j in range(1, nc):
            source = ctx_from(j)
            got = column_got.at[source]
            remote(got, got, back_ctx_send.at[OUT, j], back_ctx_recv.at[OUT, j], (d, source)).wait_recv()
            own_column[source] = column_got[source].astype(f32)
        send_back(COLUMN)

    PART, NORM, SUMS = TOK, COT, SMALL

    def over_ctx(array, src, dst, j, to):
        return remote(src, dst, back_ctx_send.at[array, j], back_ctx_recv.at[array, j], (d, to))

    half_rows = part // 2
    terms = {PART: (tok_all, part_got, part_own), NORM: (cot_all, norm_got, norm_own)}

    def term_copy(array, n):
        store, got, _ = terms[array]
        whose, at, slot, to = (
            (corner, first_half, 2, side),
            (corner, second_half, 2, across),
            (side, first_half, 0, side),
            (side, second_half, 0, side),
            (across, second_half, 1, across),
            (across, first_half, 1, across),
        )[n]
        return remote(
            store.at[whose, at, :], got.at[slot, at, :], back_ctx_send.at[array, n], back_ctx_recv.at[array, n], (d, to)
        )

    def send_terms(array, term):
        store, _, own = terms[array]
        store[corner] = term(corner).astype(b16)
        term_copy(array, 0).start()
        term_copy(array, 1).start()
        x = term(side)
        store[side, first_half, :] = x[:half_rows].astype(b16)
        held[0] = x[half_rows:]
        term_copy(array, 2).start()
        x = term(across)
        store[across, second_half, :] = x[half_rows:].astype(b16)
        held[1] = x[:half_rows]
        term_copy(array, 4).start()
        own[...] = term(c)

    def pass_terms(array):
        store, got, _ = terms[array]
        term_copy(array, 1).wait_recv()
        store[side, second_half, :] = (held[0] + got[2, second_half, :].astype(f32)).astype(b16)
        term_copy(array, 3).start()
        term_copy(array, 0).wait_recv()
        store[across, first_half, :] = (held[1] + got[2, first_half, :].astype(f32)).astype(b16)
        term_copy(array, 5).start()

    def terms_arrive(array):
        for n in range(2, 6):
            term_copy(array, n).wait_recv()

    weight_gradient(FC2, act, cotangents)
    weight_gradient(OUT, attended, cotangents)

    own_out().wait()
    for j in range(1, nc):
        out_copy(j, ctx_to(j), ctx_from(j)).wait_recv()
    out_sib(k).start()
    out_sib(1 - k).wait_recv()

    w_o = w_out[...].reshape(dl, width)

    def g_att_block(b, carry):
        g_att[block_rows(b), :] = dot(cot_all[b], w_o, RIGHT_T).astype(b16)
        return carry

    lax.fori_loop(0, nc, g_att_block, 0)
    add_sibling(FC2)
    to_columns()

    acc_k[...] = jnp.zeros_like(acc_k)
    acc_v[...] = jnp.zeros_like(acc_v)
    wide = (1, dl // keep_ref.shape[1])
    def attend_back(i):
        at, to, count = spans(i)
        mask(i)
        acc_q[...] = jnp.zeros_like(acc_q)

        def backward_step(h, carry):
            only = only_head(h)
            only_low = only.astype(b16)
            qh = q_s[at, :] * only_low
            gh = g_att[at, :] * only_low
            keys, values = k_s[to, :], v_s[to, :]
            p = jnp.exp(dot(qh, keys, RIGHT_T) * scale + bias_s[:, :count] - log_s[h, at, :])
            gw = dot(gh, values, RIGHT_T)
            gs = (p * (gw - jnp.sum(gw * p, axis=-1, keepdims=True))).astype(b16)
            acc_q[...] += dot(gs, keys, NORMAL) * only
            acc_k[to, :] += dot(gs, qh, LEFT_T)
            acc_v[to, :] += dot(p.astype(b16), gh, LEFT_T)
            return carry

        lax.fori_loop(0, heads, backward_step, 0, unroll=True)
        gmixed[at, pl.ds(0, dl)] = turn(
            acc_q[...] * scale,
            jnp.tile(keep_ref[at, :], wide),
            -jnp.tile(ahead_ref[at, :], wide),
            -jnp.tile(behind_ref[at, :], wide),
        ).astype(b16)

    count_tiles = length // tile
    for i in range(count_tiles):
        attend_back(i)

    def finish_block(b, carry):
        at = block_rows(b)
        gmixed[at, pl.ds(dl, dl)] = turn(
            acc_k[at, :] * scale,
            jnp.tile(keep_ref[at, :], wide),
            -jnp.tile(ahead_ref[at, :], wide),
            -jnp.tile(behind_ref[at, :], wide),
        ).astype(b16)
        gmixed[at, pl.ds(2 * dl, dl)] = acc_v[at, :].astype(b16)
        return carry

    lax.fori_loop(0, nc, finish_block, 0)

    weight_gradient(QKV, normed, lambda: gmixed[...])
    ones = jnp.ones((8, length), b16)
    sums[0, :, pl.ds(0, 3 * dl)] = dot(ones, gmixed[...], NORMAL)[:1]
    at_sum = 3 * dl + fl
    sums[0, :, pl.ds(at_sum, width)] = dot(ones[:, :part], cot_all[c], NORMAL)[:1]
    copy_fc2.wait()
    z_arrive(FC2)
    z_finish(FC2)
    add_sibling(QKV)

    def result_term(b):
        at = block_rows(b)
        return dot(attended[at, :], w_out[...].reshape(dl, width), NORMAL) + dot(
            act[at, :], w_fc2[...].reshape(fl, width), NORMAL
        )

    pair_copy(TOK, 3).wait_send()
    pair_copy(TOK, 0).wait_send()
    send_terms(PART, result_term)
    from_columns()
    pass_back(FC2)

    def hidden_gradient(b, carry):
        at = block_rows(b)
        g = cot_all[b]
        for i in range(nd):
            to = pl.ds(i * fr, fr)
            g_hidden[at, to] = (dot(g, w_fc2[i], RIGHT_T) * slope[at, to]).astype(b16)
        return carry

    lax.fori_loop(0, nc, hidden_gradient, 0)
    pass_terms(PART)
    pass_back(QKV)
    pass_back(COLUMN)

    def normed_term(b):
        at = block_rows(b)
        return dot(g_hidden[at, :], w_fc1[...].reshape(width, fl), RIGHT_T) + dot(
            gmixed[at, :], w_qkv[...].reshape(width, 3 * dl), RIGHT_T
        )

    pair_copy(COT, 3).wait_send()
    pair_copy(COT, 0).wait_send()
    send_terms(NORM, normed_term)
    weight_gradient(FC1, normed, lambda: g_hidden[...])
    sums[0, :, pl.ds(3 * dl, fl)] = dot(ones, g_hidden[...], NORMAL)[:1]
    pass_terms(NORM)
    terms_arrive(PART)

    def result_step(i, carry):
        at = pl.ds(pl.multiple_of(i * chunk, chunk), chunk)
        y = tok_all[c, at, :].astype(f32) + part_own[at, :] + vec_d[2:3, :]
        for n in range(2):
            y = y + part_got[n, at, :].astype(f32)
        o_result[at, :] = y.astype(b16)
        return carry

    lax.fori_loop(0, part // chunk, result_step, 0)
    add_sibling(FC1)
    gather_total(FC2)
    o_fc2[...] = own_fc2[z]

    swaps = {QKV: (swap_qkv, swapped_qkv), FC1: (swap_fc1, swapped_fc1)}

    def place(array, source, x):
        if array == QKV:
            for t in range(3):
                o_qkv[:, lanes(t * nc + source, dl)] = x[:, t * dl : (t + 1) * dl]
        else:
            for g in range(nd):
                o_fc1[:, lanes(g * nc + source, fr)] = x[:, g * fr : (g + 1) * fr]

    def swap_start(array):
        gather_total(array)
        src, dst = swaps[array]
        own = owns[array]
        for j in range(1, nc):
            src[j - 1] = own[z, rows(ctx_to(j)), :].astype(b16)
            over_ctx(array, src.at[j - 1], dst.at[j - 1], j, ctx_to(j)).start()
        place(array, c, own[z, rows(c), :])

    def swap_finish(array):
        src, dst = swaps[array]
        for j in range(1, nc):
            over_ctx(array, src.at[j - 1], dst.at[j - 1], j, ctx_to(j)).wait_recv()
            place(array, ctx_from(j), dst[j - 1].astype(f32))

    gather_total(COLUMN)
    o_out[...] = own_column[z]
    pass_back(FC1)
    swap_start(QKV)
    terms_arrive(NORM)

    def norm_step(i, carry):
        gain_sum, shift_sum = carry
        at = pl.ds(pl.multiple_of(i * chunk, chunk), chunk)
        x = tok_all[c, at, :].astype(f32)
        x = x - jnp.mean(x, axis=-1, keepdims=True)
        inverse = lax.rsqrt(jnp.mean(x * x, axis=-1, keepdims=True) + epsilon)
        x = x * inverse
        g = norm_own[at, :]
        for n in range(2):
            g = g + norm_got[n, at, :].astype(f32)
        v = g * vec_d[0:1, :]
        y = inverse * (
            v - jnp.mean(v, axis=-1, keepdims=True) - x * jnp.mean(v * x, axis=-1, keepdims=True)
        )
        o_tokens[at, :] = (cot_all[c, at, :].astype(f32) + y).astype(b16)
        return (
            gain_sum + jnp.sum(g * x, axis=0, keepdims=True),
            shift_sum + jnp.sum(g, axis=0, keepdims=True),
        )

    zero = jnp.zeros((1, width), f32)
    gain_sum, shift_sum = lax.fori_loop(0, part // chunk, norm_step, (zero, zero))
    sums[0, :, pl.ds(at_sum + width, width)] = gain_sum
    sums[0, :, pl.ds(at_sum + 2 * width, width)] = shift_sum

    sum_sib = remote(sums.at[0], sums_sib.at[0], back_sib_send.at[SUMS], back_sib_recv.at[SUMS], (other, c))
    sum_sib.start()
    swap_finish(QKV)
    sum_sib.wait()
    sums[1] = sums[0] + sums_sib[0]
    trades = [
        remote(
            sums.at[n + 1], sums_z.at[n], back_z_send.at[SUMS, n], back_z_recv.at[SUMS, n], (2 * partner + k, c)
        )
        for n, partner in enumerate((z + 1 - 2 * lax.rem(z, 2), lax.rem(z + 2, nz)))
    ]
    trades[0].start()
    trades[0].wait()
    sums[2] = sums[1] + sums_z[0]
    trades[1].start()
    swap_start(FC1)
    trades[1].wait()
    sums[3] = sums[2] + sums_z[1]
    sums_mine = sums.at[3]
    for j in range(1, nc):
        over_ctx(SUMS, sums_mine, o_sums.at[c], j, ctx_to(j)).start()
    o_sums[c] = sums[3]
    swap_finish(FC1)
    for j in range(1, nc):
        over_ctx(SUMS, sums_mine, o_sums.at[ctx_from(j)], j, ctx_to(j)).wait_recv()

    for array in (SMALL, QKV, FC1, FC2, OUT):
        z_sent(array)
    for array in (SMALL, QKV, FC1):
        ctx_sent(array)
    for array in (TOK, COT):
        for n in (1, 2):
            pair_copy(array, n).wait_send()
    for n in range(6):
        term_copy(PART, n).wait_send()
        term_copy(NORM, n).wait_send()
    for j in range(1, nc):
        out_copy(j, ctx_to(j), c).wait_send()
        column_copy(j, ctx_to(j)).wait_send()
    out_sib(k).wait_send()
    for array in (QKV, COLUMN, FC1, FC2):
        owner_sent(array)
    for j in range(1, nc):
        over_ctx(SUMS, sums_mine, o_sums.at[c], j, ctx_to(j)).wait_send()
        for array in (QKV, FC1):
            over_ctx(array, swaps[array][0].at[j - 1], swaps[array][1].at[j - 1], j, c).wait_send()


def layer_all(nz, nc, marks, tokens, cotangent, segments, qkv_weight, fc1_weight, fc2_weight, out_weight, small):
    part, width = tokens.shape
    wr, fr = qkv_weight.shape[0], fc2_weight.shape[0]
    nd, dl = 2 * nz, width // nc
    length, fl = part * nc, 2 * nz * fr
    cw = nc * wr
    f32, b16 = jnp.float32, jnp.bfloat16
    tables = [jnp.asarray(t) for t in turn_tables(length, width // HEADS, 128)]
    pack = small.shape[1]
    total = 3 * dl + fl + 3 * width
    tile, window = 256, 768
    results = [
        ((part, width), b16),
        ((part, width), b16),
        ((wr, 3 * width), f32),
        ((wr, width), f32),
        ((wr, fl * nc), f32),
        ((fr, width), f32),
        ((nc, 1, total), f32),
    ]
    work = [
        ((nc, part, width), b16),
        ((nc, part, width), b16),
        ((nd, cw, 3 * dl), b16),
        ((nd, cw, fl), b16),
        ((nd, fr, width), b16),
        ((2, cw, width), b16),
        ((nd, nc, 1, pack), f32),
        ((nd * nc, pack), f32),
        ((8, width), f32),
        ((1, 3 * dl), f32),
        ((1, fl), f32),
        ((length, width), b16),
        ((length, dl), b16),
        ((length, dl), b16),
        ((length, dl), b16),
        ((length, dl), b16),
        ((length, dl), b16),
        ((length, fl), b16),
        ((length, fl), f32),
        ((length, 3 * dl), b16),
        ((tile, dl), f32),
        ((length, dl), f32),
        ((length, dl), f32),
        ((tile, dl), f32),
        ((tile, window), f32),
        ((length, fl), b16),
    ]
    grads = [(nz, cw, 3 * dl), (nz, cw, fl), (nz, fr, width), (1, cw, width)]
    passed = grads[:3] + [(nz, wr, width)]
    fars = [(3,) + g[1:] for g in passed]
    work += [(g, b16) for g in grads] + [(g, b16) for g in grads] + [(g, f32) for g in grads]
    work += [(g, b16) for g in fars] + [(g[1:], b16) for g in passed]
    work += [((HEADS // nc, length, 1), f32), ((length, 128), f32)] + [((length, 128), f32)] * 3
    work += [((nc - 1, part, width), b16), ((part, width), f32)] * 2
    work += [((nc - 1, wr, n), b16) for n in (3 * dl, fl)] * 2
    work += [((nz, wr, width), t) for t in (b16, b16, f32)] + [((nc, wr, width), b16)]
    work += [((n, 1, total), f32) for n in (4, 1, 2)]
    work += [((2, part // 2, width), f32)]
    dma = pltpu.SemaphoreType.DMA
    sems = [(7, nc), (7, nc), (7, 5), (7, 5), (7, nz), (7, nz), (11,)]
    sems += [(8, 5), (8, 5), (7,), (7,), (7, 6), (7, 6)]
    hbm, vmem = pl.BlockSpec(memory_space=pl.ANY), pl.BlockSpec(memory_space=pltpu.VMEM)
    return pl.pallas_call(
        functools.partial(layer_kernel, nz, nc, marks),
        out_shape=[jax.ShapeDtypeStruct(s, t) for s, t in results],
        in_specs=[hbm] * 7 + [vmem] + [hbm] * 3,
        out_specs=[vmem] * len(results),
        scratch_shapes=[pltpu.VMEM(s, t) for s, t in work] + [dma(s) for s in sems],
        compiler_params=pltpu.CompilerParams(
            collective_id=0, has_side_effects=True, vmem_limit_bytes=62 * 2**20
        ),
        name="layer",
    )(tokens, cotangent, qkv_weight, fc1_weight, fc2_weight, out_weight, small, segments.reshape(1, length), *tables)


def finish_kernel(
    dl, fr, wr,
    result, tokens, qkv, out, fc1, fc2, sums,
    o_result, o_tokens, o_qkv, o_out, o_fc1, o_fc2, o_qkv_b, o_out_b, o_fc1_b, o_fc2_b, o_gain, o_shift,
    row,
):
    moves = [(result, o_result), (tokens, o_tokens), (qkv, o_qkv), (out, o_out), (fc1, o_fc1), (fc2, o_fc2)]
    for source, to in moves:
        to[...] = source[...]
    nc, total = sums.shape[0], sums.shape[2]
    mine, group = lax.axis_index("ctx"), lax.axis_index("dp")
    place = group * nc + mine
    width = dl * nc
    fl = total - 3 * dl - 3 * width

    def piece(values, size):
        length = values.shape[1]
        return pltpu.roll(values, length - place * size, axis=1)[0, :size]

    for t in range(3):
        for rank in range(nc):
            row[:, pl.ds(t * width + rank * dl, dl)] = sums[rank][:, t * dl : (t + 1) * dl]
    o_qkv_b[...] = piece(row[...], 3 * wr)
    at = pl.ds(pl.multiple_of(3 * dl + group * fr, fr), fr)
    o_fc1_b[...] = sums[mine, :, at][0]
    for n, outs in enumerate(((o_out_b, o_fc2_b), (o_gain,), (o_shift,))):
        first = 3 * dl + fl + n * width
        whole = sums[0][:, first : first + width]
        for rank in range(1, nc):
            whole = whole + sums[rank][:, first : first + width]
        for to in outs:
            to[...] = piece(whole, wr)


def finish_all(dl, fr, wr, arrays):
    f32 = jnp.float32
    vmem = pl.BlockSpec(memory_space=pltpu.VMEM)
    vectors = [3 * wr, wr, fr, wr, wr, wr]
    nc = arrays[6].shape[0]
    return pl.pallas_call(
        functools.partial(finish_kernel, dl, fr, wr),
        out_shape=[jax.ShapeDtypeStruct(a.shape, a.dtype) for a in arrays[:6]]
        + [jax.ShapeDtypeStruct((n,), f32) for n in vectors],
        in_specs=[vmem] * 7,
        out_specs=[vmem] * 12,
        scratch_shapes=[pltpu.VMEM((1, 3 * dl * nc), f32)],
        name="finish",
    )(*arrays)


def local_direct(
    dp,
    ctx,
    tokens,
    segments,
    qkv_weight,
    qkv_bias,
    out_weight,
    out_bias,
    fc1_weight,
    fc1_bias,
    fc2_weight,
    fc2_bias,
    norm_gain,
    norm_shift,
    cotangent,
):
    width = tokens.shape[-1]
    dl, fl = width // ctx, fc1_weight.shape[1] // ctx
    wr, fr = qkv_weight.shape[0], fc2_weight.shape[0]
    pieces = [fc1_bias, qkv_bias, norm_gain, norm_shift, out_bias, fc2_bias]
    marks = [0]
    for piece in pieces:
        marks.append(marks[-1] + piece.shape[0])
    vector = jnp.concatenate(pieces).astype(jnp.float32)
    vector = jnp.pad(vector, (0, -marks[-1] % 128))[None]
    arrays = layer_all(
        dp // 2,
        ctx,
        tuple(marks),
        tokens[0],
        cotangent[0],
        segments[0],
        qkv_weight,
        fc1_weight,
        fc2_weight,
        out_weight,
        vector,
    )
    result, grad_tokens, *rest = finish_all(dl, fr, wr, arrays)
    grad_qkv, grad_out, grad_fc1, grad_fc2, g_qkv_b, g_out_b, g_fc1_b, g_fc2_b, g_gain, g_shift = rest
    return (
        result[None],
        grad_tokens[None],
        grad_qkv,
        g_qkv_b,
        grad_out,
        g_out_b,
        grad_fc1,
        g_fc1_b,
        grad_fc2,
        g_fc2_b,
        g_gain,
        g_shift,
    )


def solution(mesh):
    sizes = (mesh.shape["dp"], mesh.shape["ctx"])
    seq, mat, vec = P("dp", "ctx", None), P(BOTH, None), P(BOTH)

    def spread(*args):
        dp, ctx = sizes
        tokens, qkv_weight, fc2_weight = args[0], args[2], args[8]
        direct = (
            dp == 8
            and ctx == 4
            and tokens.shape[0] == 1
            and tokens.shape[1] % 256 == 0
            and qkv_weight.shape[0] % 32 == 0
            and fc2_weight.shape[0] % 128 == 0
        )
        return (local_direct if direct else local)(*sizes, *args)

    placed = (seq, P("dp", None), mat, vec, mat, vec, mat, vec, mat, vec, vec, vec, seq)
    return jax.shard_map(
        spread,
        mesh=mesh,
        in_specs=placed,
        out_specs=(seq, seq, mat, vec, mat, vec, mat, vec, mat, vec, vec, vec),
        check_vma=False,
    )
```
